32 devices in a mesh: light: 4 (over x, core), strip: 8 (over z, y).
Axes of the slice: x: 2, y: 2, z: 4, core: 2. Of those that a mesh axis runs over, the one named last changes fastest.
Arguments:
- depth_start: float32 [128, 4096], P(None, 'strip'), may hold values from -0.3 to 0.3
- albedo_start: float32 [128, 4096], P(None, 'strip'), may hold values from 0.5 to 2
- observations: bfloat16 [32, 128, 4096], P('light', None, 'strip'), may hold values from 0 to 26
- light_table: int32 [32, 4], P('light'), may hold values from 0 to 999
- valid_mask: int32 [128, 4096], P(None, 'strip'), may hold values 0 or 1
Outputs:
- depth_final: float32 [128, 4096], P(None, 'strip')
- albedo_final: float32 [128, 4096], P(None, 'strip')
The draws below stay inside these ranges and needn't reach their ends.
All inputs are finite; a program needn't handle non-finite values. No bound on the sum of `valid_mask` on one device may be relied on, other than what follows from the above.
Results may differ from the reference program's by a relative error of at most 0.0003.
Values may be sent and summed in bfloat16 or wider, within the bound.
No kernel may reach another device: no remote copies, remote signals or barrier semaphores. Data moves between devices by JAX's collectives and lax.ppermute only.
A program may use at most 64 MiB of HBM per device.

```python
import math
import jax
import jax.numpy as jnp
from jax import lax

NL = 32
ROWS = 128
ITERS = 2
COLS = 4096


def draw_observations(key, part):
    subkeys = jax.random.split(key, 3)
    row_scale = jnp.exp(jax.random.uniform(subkeys[0], (1, ROWS, 1), jnp.float32, 0.0, math.log(1.6)))
    col_scale = jnp.exp(jax.random.uniform(subkeys[1], (1, 1, COLS), jnp.float32, 0.0, math.log(1.6)))
    position = jnp.arange(COLS, dtype=jnp.float32) / max(COLS - 1, 1)
    incline = (1.0 + 8.0 * position)[None, None, :]
    texture = jax.random.uniform(subkeys[2], (NL, ROWS, COLS), jnp.float32, 0.2, 1.1)
    values = row_scale * col_scale * incline * texture
    return values.astype(jnp.bfloat16)


def plant(result, own_key, least, high):
    longest = result.shape.index(max(result.shape))
    spots = []
    for shift in (0, 1):
        where = [jax.random.randint(jax.random.fold_in(own_key, axis), (), 0, length) for axis, length in enumerate(result.shape)]
        where[longest] = (where[longest] + shift) % result.shape[longest]
        spots.append(tuple(where))
    return result.at[spots[0]].set(least).at[spots[1]].set(high)


def block_levels(stream_key, dims, pieces, low, high):
    level, own = 1.0, jax.random.fold_in(stream_key, 6)
    for dim, shards_of in pieces:
        draws = jnp.exp(jax.random.uniform(jax.random.fold_in(own, dim), (shards_of,), jnp.float32, low / len(pieces), high / len(pieces)))
        level = level * jnp.repeat(draws, dims[dim] // shards_of).reshape([-1 if axis == dim else 1 for axis in range(len(dims))])
    return level


def setup_inputs(seed: int = 0) -> dict:
    seeds = jax.random.split(jax.random.key(seed), 6)
    return {
        "depth_start": jnp.clip(jax.random.uniform(seeds[0], (ROWS, COLS), jnp.float32, -0.3, 0.3) * block_levels(seeds[0], (ROWS, COLS), ((1, 8),), -0.4, 0.0), -0.3, 0.3),
        "albedo_start": jnp.clip(jnp.exp(math.log(2.0) - 1.3862944 * jax.random.uniform(seeds[1], (ROWS, COLS), jnp.float32) ** block_levels(seeds[1], (ROWS, COLS), ((1, 8),), -0.2, 0.2)), 0.5, 2.0),
        "observations": draw_observations(jax.random.fold_in(seeds[5], 71), 0),
        "light_table": plant(jax.random.randint(seeds[3], (NL, 4), 0, 1000), jax.random.fold_in(seeds[3], 1), 0, 999).astype(jnp.int32),
        "valid_mask": plant((jax.random.randint(seeds[4], (ROWS, COLS), 0, 8) < 7).astype(jnp.int32), jax.random.fold_in(seeds[4], 1), 0, 1),
    }


temper = 0.5
step_depth = 0.1
step_albedo = 0.2
epsilon = 1e-06

def decode_lights(table):
    values = table.astype(jnp.float32)
    light_x = (values[:, 0] / 500.0 - 1.0)[:, None, None]
    light_y = (values[:, 1] / 500.0 - 1.0)[:, None, None]
    light_z = (1.0 + values[:, 2] / 1000.0)[:, None, None]
    intensity = (0.5 + values[:, 3] / 1000.0)[:, None, None]
    return (light_x, light_y, light_z, intensity)

def shade_terms(surface, col_pad, row_pad, albedo, observed, table, valid, coord_x, coord_y):
    slope_x = 0.5 * (col_pad[:, 2:] - col_pad[:, :-2])
    slope_y = 0.5 * (row_pad[2:] - row_pad[:-2])
    light_x, light_y, light_z, intensity = decode_lights(table)
    delta_x = light_x - coord_x
    delta_y = light_y - coord_y
    delta_z = light_z - surface
    distance_sq = delta_x * delta_x + delta_y * delta_y + delta_z * delta_z
    norm_sq = 1.0 + slope_x * slope_x + slope_y * slope_y
    facing = -slope_x * delta_x - slope_y * delta_y + delta_z
    falloff = intensity / (distance_sq * jnp.sqrt(distance_sq) * jnp.sqrt(norm_sq))
    radiance = albedo * falloff * facing
    residual = valid * (radiance - observed.astype(jnp.float32))
    scores = -temper * residual * residual
    return (scores, residual, falloff, facing, delta_x, delta_y, delta_z, distance_sq, norm_sq, slope_x, slope_y)

def light_gradients(weights, terms, albedo):
    scores, residual, falloff, facing, delta_x, delta_y, delta_z, distance_sq, norm_sq, slope_x, slope_y = terms
    lit = weights * residual * falloff
    grad_albedo = lax.optimization_barrier(jnp.sum(lit * facing, axis=0))
    scaled = lit * albedo
    grad_direct = lax.optimization_barrier(jnp.sum(scaled * (-1.0 + 3.0 * facing * delta_z / distance_sq), axis=0))
    grad_x = lax.optimization_barrier(jnp.sum(scaled * (-delta_x - facing * slope_x / norm_sq), axis=0))
    grad_y = lax.optimization_barrier(jnp.sum(scaled * (-delta_y - facing * slope_y / norm_sq), axis=0))
    return (grad_x, grad_y, grad_direct, grad_albedo)

def depth_stencil(grad_x_pad, grad_y_pad, grad_direct):
    return grad_direct + 0.5 * (grad_x_pad[:, :-2] - grad_x_pad[:, 2:]) + 0.5 * (grad_y_pad[:-2] - grad_y_pad[2:])

def reference(depth_start, albedo_start, observations, light_table, valid_mask):
    surface = depth_start
    albedo = albedo_start
    valid = valid_mask.astype(jnp.float32)
    nrows, ncols = surface.shape
    coord_x = ((jnp.arange(ncols).astype(jnp.float32) + 0.5) / ncols - 0.5)[None, :]
    coord_y = ((jnp.arange(nrows).astype(jnp.float32) + 0.5 - nrows / 2.0) / ncols)[:, None]
    for iteration in range(ITERS):
        col_pad = jnp.pad(surface, ((0, 0), (1, 1)))
        row_pad = jnp.pad(surface, ((1, 1), (0, 0)))

        def first_pass(running, inputs):
            observed, table_row = inputs
            terms = shade_terms(surface, col_pad, row_pad, albedo, observed[None], table_row[None], valid, coord_x, coord_y)
            scores = terms[0][0]
            highest = jnp.maximum(running[0], scores)
            summed = running[1] * jnp.exp(running[0] - highest) + jnp.exp(scores - highest)
            return ((highest, summed), None)
        start_pair = (jnp.full(surface.shape, -jnp.inf, jnp.float32), jnp.zeros(surface.shape, jnp.float32))
        (highest, summed), unused = lax.scan(first_pass, start_pair, (observations, light_table))

        def second_pass(running, inputs):
            observed, table_row = inputs
            terms = shade_terms(surface, col_pad, row_pad, albedo, observed[None], table_row[None], valid, coord_x, coord_y)
            weights = jnp.exp(terms[0] - highest) / summed
            fields = light_gradients(weights, terms, albedo)
            return (tuple((running[index] + fields[index] for index in range(4))), None)
        zeros_four = tuple((jnp.zeros(surface.shape, jnp.float32) for index in range(4)))
        (grad_x, grad_y, grad_direct, grad_albedo), unused = lax.scan(second_pass, zeros_four, (observations, light_table))
        full_depth = depth_stencil(jnp.pad(grad_x, ((0, 0), (1, 1))), jnp.pad(grad_y, ((1, 1), (0, 0))), grad_direct)
        mean_depth = jnp.sum(full_depth * full_depth) / full_depth.size
        mean_albedo = jnp.sum(grad_albedo * grad_albedo) / grad_albedo.size
        surface = surface - step_depth * jnp.tanh(full_depth / jnp.sqrt(mean_depth + epsilon))
        albedo = albedo - step_albedo * jnp.tanh(grad_albedo / jnp.sqrt(mean_albedo + epsilon))
    return (surface, albedo)
```

```python
import functools
import math

import jax
import jax.numpy as jnp
from jax import lax
from jax.experimental import pallas as pl
from jax.experimental.pallas import tpu as pltpu
from jax.sharding import PartitionSpec as P

AXES = ("light", "strip")
STEP_DEPTH = 0.1
STEP_ALBEDO = 0.2
EPS = 1e-06
HALF_LOG2E = 0.5 * math.log2(math.e)
F32 = jnp.float32
VM = pl.BlockSpec(memory_space=pltpu.VMEM)
TR = 16


def iota(shape, dim):
    return lax.broadcasted_iota(jnp.int32, shape, dim)


def position():
    nl, ns = lax.axis_size("light"), lax.axis_size("strip")
    li, si = lax.axis_index("light"), lax.axis_index("strip")
    return li, si, si * nl + li, nl * ns


def exchange_index(place):
    nl, ns = lax.axis_size("light"), lax.axis_size("strip")
    return lax.rem(place, nl) * ns + lax.div(place, nl)


def call(body, out, scratch=(), name=None, aliases=None, cost=None):
    return pl.pallas_call(
        body,
        out_shape=out,
        scratch_shapes=list(scratch),
        name=name,
        input_output_aliases=aliases or {},
        compiler_params=pltpu.CompilerParams(vmem_limit_bytes=40 << 20),
        cost_estimate=cost,
    )


def edges_body(nl, obs_ref, depth_ref, albedo_ref, valid_ref, fwd_ref, bwd_ref, eh_ref, sr_ref):
    lights, rows, cols = obs_ref.shape
    w = cols // nl

    def picks(columns):
        pad = -len(columns) % 8
        row = iota((len(columns) + pad, cols), 0)
        col = iota((len(columns) + pad, cols), 1)
        hit = jnp.zeros(row.shape, jnp.bool_)
        for index, column in enumerate(columns):
            hit = hit | ((row == index) & (col == column))
        return hit.astype(F32)

    ends = []
    for q in range(nl):
        ends += [q * w, q * w + w - 1]
    pairs = []
    for q in range(nl):
        pairs += [q * w, q * w + 1, q * w + w - 2, q * w + w - 1]
    contract = (((1,), (1,)), ((), ()))
    pick_ends = picks(ends)
    pick_pairs = picks(pairs)
    exact = lax.Precision.HIGHEST
    depth = lax.dot_general(pick_pairs, depth_ref[...], contract, precision=exact, preferred_element_type=F32)
    albedo = lax.dot_general(pick_ends, albedo_ref[...], contract, precision=exact, preferred_element_type=F32)
    valid = lax.dot_general(
        pick_ends, valid_ref[...].astype(F32), contract, precision=exact, preferred_element_type=F32
    )
    zero = jnp.zeros((1, rows), F32)
    fwd_ref[...] = jnp.zeros_like(fwd_ref)
    bwd_ref[...] = jnp.zeros_like(bwd_ref)
    eh_ref[...] = jnp.zeros_like(eh_ref)
    sr_ref[...] = jnp.zeros_like(sr_ref)
    pick16 = pick_ends.astype(jnp.bfloat16)
    for l in range(lights):
        e = lax.dot_general(pick16, obs_ref[l], contract, preferred_element_type=F32)
        bwd_ref[l : l + 1, :] = e[0:1]
        fwd_ref[l : l + 1, :] = e[2 * nl - 1 : 2 * nl]
        for q in range(nl):
            if q > 0:
                eh_ref[q, l : l + 1, :] = e[2 * q - 1 : 2 * q]
            if q < nl - 1:
                eh_ref[q, lights + l : lights + l + 1, :] = e[2 * q + 2 : 2 * q + 3]
    n = lights
    last = 4 * (nl - 1)
    fwd_ref[n : n + 2, :] = depth[last + 2 : last + 4]
    fwd_ref[n + 2 : n + 3, :] = albedo[2 * nl - 1 : 2 * nl]
    fwd_ref[n + 3 : n + 4, :] = valid[2 * nl - 1 : 2 * nl]
    bwd_ref[n : n + 2, :] = depth[0:2]
    bwd_ref[n + 2 : n + 3, :] = albedo[0:1]
    bwd_ref[n + 3 : n + 4, :] = valid[0:1]
    for q in range(nl):
        sr_ref[q, 2:3, :] = depth[4 * q : 4 * q + 1]
        sr_ref[q, 3:4, :] = depth[4 * q + 3 : 4 * q + 4]
        if q > 0:
            sr_ref[q, 0:2, :] = depth[4 * q - 2 : 4 * q]
            sr_ref[q, 6:7, :] = albedo[2 * q - 1 : 2 * q]
            sr_ref[q, 8:9, :] = valid[2 * q - 1 : 2 * q]
        if q < nl - 1:
            sr_ref[q, 4:6, :] = depth[4 * q + 4 : 4 * q + 6]
            sr_ref[q, 7:8, :] = albedo[2 * q + 2 : 2 * q + 3]
            sr_ref[q, 9:10, :] = valid[2 * q + 2 : 2 * q + 3]


def halos_body(nl, eh_ref, sr_ref, low_ref, high_ref, table_ref, *outs):
    small_refs, own_ref = outs[:nl], outs[nl]
    li = lax.axis_index("light")
    n = table_ref.shape[0]
    table = table_ref[...].astype(F32)
    for k in range(nl):
        q = li ^ k
        ref = small_refs[k]
        ref[0 : 2 * n, :] = eh_ref[q]
        ref[2 * n :, :] = jnp.zeros((ref.shape[0] - 2 * n, ref.shape[1]), F32)
        ref[2 * n : 3 * n, 0:4] = table

        @pl.when(q == 0)
        def _():
            ref[0:n, :] = low_ref[0:n, :]

        @pl.when(q == nl - 1)
        def _():
            ref[n : 2 * n, :] = high_ref[0:n, :]

    own_ref[...] = sr_ref[li]

    @pl.when(li == 0)
    def _():
        own_ref[0:2, :] = low_ref[n : n + 2, :]
        own_ref[6:7, :] = low_ref[n + 2 : n + 3, :]
        own_ref[8:9, :] = low_ref[n + 3 : n + 4, :]

    @pl.when(li == nl - 1)
    def _():
        own_ref[4:6, :] = high_ref[n : n + 2, :]
        own_ref[7:8, :] = high_ref[n + 2 : n + 3, :]
        own_ref[9:10, :] = high_ref[n + 3 : n + 4, :]


def decode(table):
    return (
        table[:, 0:1] / 500.0 - 1.0,
        table[:, 1:2] / 500.0 - 1.0,
        1.0 + table[:, 2:3] / 1000.0,
        0.5 + table[:, 3:4] / 1000.0,
    )


def columns_from(left, right, shape):
    rows, w = shape
    at = iota((w, rows), 0)
    return jnp.transpose(jnp.where(at == 0, left, jnp.where(at == w - 1, right, 0.0)))


def shifts_rows(x):
    r = iota(x.shape, 0)
    n = x.shape[0]
    above = jnp.where(r == 0, 0.0, pltpu.roll(x, 1, 0))
    below = jnp.where(r == n - 1, 0.0, pltpu.roll(x, n - 1, 0))
    return above, below


def shifts_cols(x, ends):
    c = iota(x.shape, 1)
    n = x.shape[1]
    before = jnp.where(c == 0, ends, pltpu.roll(x, 1, 1))
    after = jnp.where(c == n - 1, ends, pltpu.roll(x, n - 1, 1))
    return before, after


def fill_context(ctx_ref, surface, albedo, left, right):
    ends = columns_from(left, right, surface.shape)
    before, after = shifts_cols(surface, ends)
    above, below = shifts_rows(surface)
    sx = 0.5 * (after - before)
    sy = 0.5 * (below - above)
    ctx_ref[0] = surface
    ctx_ref[1] = sx
    ctx_ref[2] = sy
    ctx_ref[3] = albedo * lax.rsqrt(1.0 + sx * sx + sy * sy)


def fill_params(pb_ref, base, small_ref, w, place, total):
    n = small_ref.shape[0] // 3
    lx, ly, lz, le = decode(small_ref[2 * n : 3 * n, :])
    col = iota((8, w), 1) + place * w
    px = (col.astype(F32) + 0.5) / total - 0.5
    for j in range(n):
        dx = jnp.broadcast_to(lx[j : j + 1], (8, w)) - px
        pb_ref[base + j, 0] = dx
        pb_ref[base + j, 1] = dx * dx
        pb_ref[base + j, 2] = jnp.broadcast_to(ly[j : j + 1], (8, w))
        pb_ref[base + j, 3] = jnp.broadcast_to(lz[j : j + 1], (8, w))
        pb_ref[base + j, 4] = jnp.broadcast_to(le[j : j + 1], (8, w))


def accumulate(state, tile, py, obs, pb_ref, base):
    surface, sx, sy, scaled = tile
    kept = []
    least = None
    for j in range(len(obs)):
        dx, dx2 = pb_ref[base + j, 0], pb_ref[base + j, 1]
        dy = pb_ref[base + j, 2] - py
        dz = pb_ref[base + j, 3] - surface
        dist = (dx2 + dy * dy) + dz * dz
        facing = dz - (sx * dx + sy * dy)
        r = lax.rsqrt(dist)
        r2 = r * r
        g = (r2 * r) * pb_ref[base + j, 4]
        residual = scaled * (g * facing) - obs[j]
        square = residual * residual
        least = square if least is None else jnp.minimum(least, square)
        kept.append((square, residual * g, facing, dz * r2, dx, dy))
    if state is not None:
        before = state[0]
        least = jnp.minimum(least, before)
    sums = None
    for square, q, facing, drop, dx, dy in kept:
        w = jnp.exp2((least - square) * HALF_LOG2E)
        p = w * q
        pf = p * facing
        terms = (w, p, p * dx, p * dy, pf, pf * drop)
        sums = terms if sums is None else tuple(a + b for a, b in zip(sums, terms))
    if state is not None:
        fade = jnp.exp2((least - before) * HALF_LOG2E)
        sums = tuple(a * fade + b for a, b in zip(state[1:], sums))
    return (least,) + sums


def sweep(ctx_ref, pb_ref, obs_refs, bases, total, load, store):
    rows, w = ctx_ref.shape[1:]
    split = (TR // 8, 8, w)

    def step(i, carry):
        at = pl.ds(pl.multiple_of(i * TR, TR), TR)
        tile = tuple(ctx_ref[f, at, :].reshape(split) for f in range(4))
        row = iota(split, 0) * 8 + iota(split, 1) + i * TR
        py = (row.astype(F32) + (0.5 - rows / 2.0)) / total
        state = load(at)
        for obs_ref, base in zip(obs_refs, bases):
            obs = [obs_ref[j, at, :].astype(F32).reshape(split) for j in range(obs_ref.shape[0])]
            state = accumulate(state, tile, py, obs, pb_ref, base)
        store(at, state)
        return carry

    lax.fori_loop(0, rows // TR, step, 0)


def state_load(state_ref, w):
    return lambda at: tuple(state_ref[f, at, :].reshape(TR // 8, 8, w) for f in range(7))


def state_store(state_ref, w):
    def store(at, state):
        for f in range(7):
            state_ref[f, at, :] = state[f].reshape(TR, w)

    return store


def halo_slope(column, side, small_refs, srow_ref, rows, total):
    n = small_refs[0].shape[0] // 3
    obs = jnp.concatenate([ref[side * n : (side + 1) * n, :] for ref in small_refs], axis=0)
    table = jnp.concatenate([ref[2 * n : 3 * n, :] for ref in small_refs], axis=0)
    lx, ly, lz, le = decode(table)
    outer, inner = (0, 2) if side == 0 else (5, 3)
    here = 1 if side == 0 else 4
    surface = srow_ref[here : here + 1, :]
    toward = srow_ref[inner : inner + 1, :] - srow_ref[outer : outer + 1, :]
    sx = 0.5 * toward if side == 0 else -0.5 * toward
    lane = iota((8, rows), 1)
    wide = jnp.broadcast_to(surface, (8, rows))
    above = jnp.where(lane == 0, 0.0, pltpu.roll(wide, 1, 1))
    below = jnp.where(lane == rows - 1, 0.0, pltpu.roll(wide, rows - 1, 1))
    sy = (0.5 * (below - above))[0:1]
    albedo = srow_ref[6 + side : 7 + side, :]
    valid = srow_ref[8 + side : 9 + side, :]
    px = (column.astype(F32) + 0.5) / total - 0.5
    py = (iota((1, rows), 1).astype(F32) + (0.5 - rows / 2.0)) / total
    rn = lax.rsqrt(1.0 + sx * sx + sy * sy)
    dx = jnp.broadcast_to(lx - px, obs.shape)
    dy = ly - py
    dz = lz - surface
    dist = dx * dx + dy * dy + dz * dz
    facing = dz - (sx * dx + sy * dy)
    r = lax.rsqrt(dist)
    g = (r * r) * r * le
    residual = (albedo * rn) * (g * facing) - obs
    square = residual * residual
    least = jnp.min(square, axis=0, keepdims=True)
    w = jnp.exp2((least - square) * HALF_LOG2E)
    p = w * residual * g
    total_w = jnp.sum(w, axis=0, keepdims=True)
    px_sum = jnp.sum(p * dx, axis=0, keepdims=True)
    pf_sum = jnp.sum(p * facing, axis=0, keepdims=True)
    return -(valid * albedo * rn / total_w) * (px_sum + (sx * rn * rn) * pf_sum)


def gradients(state_ref, ctx_ref, albedo, valid, slope_low, slope_high):
    sx, sy = ctx_ref[1], ctx_ref[2]
    rn = lax.rsqrt(1.0 + sx * sx + sy * sy)
    inverse = valid * rn / state_ref[1]
    factor = inverse * albedo
    pf = state_ref[5]
    rn2pf = rn * rn * pf
    grad_albedo = inverse * pf
    direct = factor * (3.0 * state_ref[6] - state_ref[2])
    grad_x = -factor * (state_ref[3] + sx * rn2pf)
    grad_y = -factor * (state_ref[4] + sy * rn2pf)
    before, after = shifts_cols(grad_x, columns_from(slope_low, slope_high, grad_x.shape))
    above, below = shifts_rows(grad_y)
    return direct + 0.5 * (before - after) + 0.5 * (above - below), grad_albedo


def partial_sums(depth, albedo):
    n = depth.shape[1]
    d = jnp.sum(depth * depth, axis=0, keepdims=True)
    a = jnp.sum(albedo * albedo, axis=0, keepdims=True)
    d = jnp.broadcast_to(d, (8, n))
    a = jnp.broadcast_to(a, (8, n))
    d = d + pltpu.roll(d, n // 2, 1)
    a = a + pltpu.roll(a, n // 2, 1)
    return jnp.where(iota((8, n), 1) < n // 2, d, a)[0:1]


def inverse_scales(recv_ref, row, count):
    rows = recv_ref[:, row, :]
    n = rows.shape[1]
    lane = iota(rows.shape, 1)
    d = jnp.sum(jnp.where(lane < n // 2, rows, 0.0), keepdims=True)
    a = jnp.sum(jnp.where(lane < n // 2, 0.0, rows), keepdims=True)
    return lax.rsqrt(d / count + EPS), lax.rsqrt(a / count + EPS)


def first_body(nl, depth_ref, albedo_ref, valid_ref, srow_ref, small0, small1, obs0, obs1, ctx_ref, mask_ref, state_ref, pb_ref):
    li, si, place, count = position()
    rows, w = ctx_ref.shape[1:]
    at = pl.ds(pl.multiple_of(li * w, w), w)
    albedo = albedo_ref[:, at]
    mask_ref[0] = albedo
    mask_ref[1] = valid_ref[:, at].astype(F32)
    fill_context(ctx_ref, depth_ref[:, at], albedo, srow_ref[1:2, :], srow_ref[4:5, :])
    total = w * count
    n = obs0.shape[0]
    fill_params(pb_ref, 0, small0, w, place, total)
    fill_params(pb_ref, n, small1, w, place, total)
    sweep(ctx_ref, pb_ref, (obs0, obs1), (0, n), total, lambda at: None, state_store(state_ref, w))


def more_body(ctx_ref, in_ref, small, obs, state_ref, pb_ref):
    li, si, place, count = position()
    rows, w = ctx_ref.shape[1:]
    total = w * count
    fill_params(pb_ref, 0, small, w, place, total)
    sweep(ctx_ref, pb_ref, (obs,), (0,), total, state_load(in_ref, w), state_store(state_ref, w))


def finish(state_ref, ctx_ref, albedo, valid, small_refs, srow_ref, grad_ref, edge_ref, pay_ref):
    li, si, place, count = position()
    rows, w = ctx_ref.shape[1:]
    total = w * count
    low = halo_slope(place * w - 1, 0, small_refs, srow_ref, rows, total)
    high = halo_slope(place * w + w, 1, small_refs, srow_ref, rows, total)
    depth, grad_albedo = gradients(state_ref, ctx_ref, albedo, valid, low, high)
    sums = partial_sums(depth, grad_albedo)
    if edge_ref is None:
        pay_ref[...] = jnp.broadcast_to(sums[None], pay_ref.shape)
        return depth, grad_albedo
    grad_ref[0] = depth
    grad_ref[1] = grad_albedo
    dt = jnp.transpose(depth)
    at = jnp.transpose(grad_albedo)
    edge_ref[0:1, :] = dt[0:1]
    edge_ref[1:2, :] = dt[w - 1 : w]
    pay_ref[:, 0:2, :] = jnp.broadcast_to(dt[0:2][None], (count, 2, rows))
    pay_ref[:, 2:3, :] = jnp.broadcast_to(at[0:1][None], (count, 1, rows))
    pay_ref[:, 3:4, :] = jnp.broadcast_to(sums[None], (count, 1, w))

    @pl.when(place < count - 1)
    def _():
        to = exchange_index(place + 1)
        pay_ref[to, 0:2, :] = dt[w - 2 : w]
        pay_ref[to, 2:3, :] = at[w - 1 : w]

    return depth, grad_albedo


def last_body(nl, ctx_ref, mask_ref, in_ref, srow_ref, *rest):
    small_refs, (obs, grad_ref, edge_ref, pay_ref, pb_ref, state_ref) = rest[:nl], rest[nl:]
    li, si, place, count = position()
    rows, w = ctx_ref.shape[1:]
    total = w * count
    fill_params(pb_ref, 0, small_refs[nl - 1], w, place, total)
    sweep(ctx_ref, pb_ref, (obs,), (0,), total, state_load(in_ref, w), state_store(state_ref, w))
    edge_ref[...] = jnp.zeros_like(edge_ref)
    finish(state_ref, ctx_ref, mask_ref[0], mask_ref[1], small_refs, srow_ref, grad_ref, edge_ref, pay_ref)


def second_body(nl, recv_ref, grad_ref, edge_ref, ctx0_ref, mask_ref, srow0_ref, *rest):
    small_refs, obs_refs = rest[:nl], rest[nl : 2 * nl]
    out_ref, pay_ref, ctx_ref, state_ref, pb_ref, srow_ref = rest[2 * nl :]
    li, si, place, count = position()
    rows, w = ctx_ref.shape[1:]
    total = w * count
    inv_depth, inv_albedo = inverse_scales(recv_ref, 3, float(rows * total))
    surface = ctx0_ref[0] - STEP_DEPTH * jnp.tanh(grad_ref[0] * inv_depth)
    albedo = mask_ref[0] - STEP_ALBEDO * jnp.tanh(grad_ref[1] * inv_albedo)
    out_ref[0] = surface
    out_ref[1] = albedo
    srow_ref[...] = jnp.zeros_like(srow_ref)
    srow_ref[2:4, :] = edge_ref[0:2, :]

    @pl.when(place > 0)
    def _():
        frm = exchange_index(jnp.maximum(place - 1, 0))
        srow_ref[0:2, :] = recv_ref[frm, 0:2, :]
        srow_ref[6:7, :] = recv_ref[frm, 2:3, :]

    @pl.when(place < count - 1)
    def _():
        frm = exchange_index(jnp.minimum(place + 1, count - 1))
        srow_ref[4:6, :] = recv_ref[frm, 0:2, :]
        srow_ref[7:8, :] = recv_ref[frm, 2:3, :]

    changes = srow_ref[0:8, :]
    kind = iota(changes.shape, 0) < 6
    changes = jnp.where(
        kind, STEP_DEPTH * jnp.tanh(changes * inv_depth), STEP_ALBEDO * jnp.tanh(changes * inv_albedo)
    )
    srow_ref[0:8, :] = srow0_ref[0:8, :] - changes
    srow_ref[8:16, :] = srow0_ref[8:16, :]
    fill_context(ctx_ref, surface, albedo, srow_ref[1:2, :], srow_ref[4:5, :])
    n = obs_refs[0].shape[0]
    bases = tuple(k * n for k in range(nl))
    for k in range(nl):
        fill_params(pb_ref, bases[k], small_refs[k], w, place, total)
    sweep(ctx_ref, pb_ref, obs_refs, bases, total, lambda at: None, state_store(state_ref, w))
    depth, grad_albedo = finish(
        state_ref, ctx_ref, albedo, mask_ref[1], small_refs, srow_ref, None, None, pay_ref
    )
    out_ref[2] = depth
    out_ref[3] = grad_albedo


def final_body(nl, recv_ref, *rest):
    parts, (depth_ref, albedo_ref) = rest[:nl], rest[nl:]
    li, si, place, count = position()
    rows, w = parts[0].shape[1:]
    inv_depth, inv_albedo = inverse_scales(recv_ref, 0, float(rows * w * count))
    for k in range(nl):
        at = pl.ds(pl.multiple_of((li ^ k) * w, w), w)
        depth_ref[:, at] = parts[k][0] - STEP_DEPTH * jnp.tanh(parts[k][2] * inv_depth)
        albedo_ref[:, at] = parts[k][1] - STEP_ALBEDO * jnp.tanh(parts[k][3] * inv_albedo)


def shape(*dims, dtype=F32):
    return jax.ShapeDtypeStruct(dims, dtype)


def shards(depth_start, albedo_start, observations, light_table, valid_mask):
    nl, ns = lax.axis_size("light"), lax.axis_size("strip")
    nd = nl * ns
    lights, rows, cols = observations.shape
    w = cols // nl
    li = lax.axis_index("light")

    def over(k):
        return [(i, i ^ k) for i in range(nl)]

    def block(x, k):
        return lax.dynamic_slice_in_dim(x, (li ^ k) * w, w, axis=2)

    obs2 = lax.ppermute(block(observations, 2), "light", over(2))
    obs1 = lax.ppermute(block(observations, 1), "light", over(1))
    obs0 = block(observations, 0)
    up = 2 * lights
    fwd, bwd, eh, sr = call(
        functools.partial(edges_body, nl),
        (shape(up, rows), shape(up, rows), shape(nl, up, rows), shape(nl, 16, rows)),
        name="edges",
    )(observations, depth_start, albedo_start, valid_mask)
    low = lax.ppermute(fwd, "strip", [(i, i + 1) for i in range(ns - 1)])
    high = lax.ppermute(bwd, "strip", [(i + 1, i) for i in range(ns - 1)])
    *small, srow = call(
        functools.partial(halos_body, nl),
        tuple(shape(3 * lights, rows) for _ in range(nl)) + (shape(16, rows),),
        name="halos",
    )(eh, sr, low, high, light_table)
    send3, small[3] = lax.optimization_barrier((block(observations, 3), small[3]))
    small = [small[0]] + [lax.ppermute(small[k], "light", over(k)) for k in range(1, nl)]
    obs3 = lax.ppermute(send3, "light", over(3))

    pb = pltpu.VMEM((2 * lights, 5, 8, w), F32)
    field = (rows, w)
    ctx, mask, state = call(
        functools.partial(first_body, nl),
        (shape(4, *field), shape(2, *field), shape(7, *field)),
        [pb],
        name="first",
    )(depth_start, albedo_start, valid_mask, srow, small[0], small[1], obs0, obs1)
    state = call(more_body, shape(7, *field), [pb], name="more")(ctx, state, small[2], obs2)
    grad, edge, pay = call(
        functools.partial(last_body, nl),
        (shape(2, *field), shape(8, rows), shape(nd, 4, rows)),
        [pb, pltpu.VMEM((7, *field), F32)],
        name="last",
    )(ctx, mask, state, srow, *small, obs3)
    recv = lax.all_to_all(pay, AXES, 0, 0, tiled=True)
    own, pay = call(
        functools.partial(second_body, nl),
        (shape(4, *field), shape(nd, 1, rows)),
        [
            pltpu.VMEM((4, *field), F32),
            pltpu.VMEM((7, *field), F32),
            pltpu.VMEM((nl * lights, 5, 8, w), F32),
            pltpu.VMEM((16, rows), F32),
        ],
        name="second",
    )(recv, grad, edge, ctx, mask, srow, *small, obs0, obs1, obs2, obs3)
    part2 = lax.ppermute(own, "light", over(2))
    part1 = lax.ppermute(own, "light", over(1))
    recv = lax.all_to_all(pay, AXES, 0, 0, tiled=True)
    part3 = lax.ppermute(part2, "light", over(1))
    return tuple(
        call(functools.partial(final_body, nl), (shape(rows, cols), shape(rows, cols)), name="final")(
            recv, own, part1, part2, part3
        )
    )


def solution(mesh):
    in_specs = (
        P(None, "strip"),
        P(None, "strip"),
        P("light", None, "strip"),
        P("light", None),
        P(None, "strip"),
    )
    out_specs = (P(None, "strip"), P(None, "strip"))
    return jax.shard_map(shards, mesh=mesh, in_specs=in_specs, out_specs=out_specs, check_vma=False)
```

```python
import functools
import math

import jax
import jax.numpy as jnp
from jax import lax
from jax.experimental import pallas as pl
from jax.experimental.pallas import tpu as pltpu
from jax.sharding import PartitionSpec as P


AXES = ("light", "strip")
STEP_DEPTH = 0.1
STEP_ALBEDO = 0.2
EPS = 1e-06
HALF_LOG2E = 0.5 * math.log2(math.e)
F32 = jnp.float32
VM = pl.BlockSpec(memory_space=pltpu.VMEM)
TR = 16


def iota(shape, dim):
    return lax.broadcasted_iota(jnp.int32, shape, dim)


def position():
    nl, ns = lax.axis_size("light"), lax.axis_size("strip")
    li, si = lax.axis_index("light"), lax.axis_index("strip")
    return li, si, si * nl + li, nl * ns


def exchange_index(place):
    nl, ns = lax.axis_size("light"), lax.axis_size("strip")
    return lax.rem(place, nl) * ns + lax.div(place, nl)


def call(body, out, scratch=(), vmem=40 << 20, **more):
    return pl.pallas_call(
        body,
        out_shape=out,
        scratch_shapes=list(scratch),
        compiler_params=pltpu.CompilerParams(vmem_limit_bytes=vmem),
        **more,
    )


def cut_body(nl, obs_ref, table_ref, *rest):
    outs, (table, sems) = rest[:nl], rest[nl:]
    lights, rows, cols = obs_ref.shape
    w = cols // nl
    li = lax.axis_index("light")
    copies = []
    for k in (2, 3, 1, 0):
        at = pl.ds(pl.multiple_of((li ^ k) * w, w), w)
        for l in range(lights):
            copy = pltpu.make_async_copy(
                obs_ref.at[l, :, at], outs[k].at[pl.ds(l * rows, rows)], sems.at[k * lights + l]
            )
            copy.start()
            copies.append(copy)
    fetch = pltpu.make_async_copy(table_ref, table, sems.at[nl * lights])
    fetch.start()
    fetch.wait()
    entries = table[...]
    high = lax.shift_right_logical(entries, 5)
    both = jnp.concatenate([high, entries - high * 32], axis=0).astype(F32)
    wide = jnp.concatenate([both, jnp.zeros((8, w - lights), F32)], axis=1)
    under = jnp.concatenate([wide, jnp.zeros((8, w), F32)], axis=0).astype(jnp.bfloat16)
    for k in range(nl):
        outs[k][pl.ds(lights * rows, 16), :] = under
    for copy in copies:
        copy.wait()


def edges_body(nl, depth_ref, albedo_ref, valid_ref, *rest):
    block_refs, (fwd_ref, bwd_ref, eh_ref, sr_ref) = rest[:nl], rest[nl:]
    rows, cols = depth_ref.shape
    w = cols // nl
    lights = block_refs[0].shape[0] // rows
    li = lax.axis_index("light")

    def picks(columns, size):
        pad = -len(columns) % 8
        row = iota((len(columns) + pad, size), 0)
        col = iota((len(columns) + pad, size), 1)
        hit = jnp.zeros(row.shape, jnp.bool_)
        for index, column in enumerate(columns):
            hit = hit | ((row == index) & (col == column))
        return hit.astype(F32)

    ends, pairs = [], []
    for q in range(nl):
        ends += [q * w, q * w + w - 1]
        pairs += [q * w, q * w + 1, q * w + w - 2, q * w + w - 1]
    contract = (((1,), (1,)), ((), ()))
    pick_ends = picks(ends, cols)
    exact = dict(precision=lax.Precision.HIGHEST, preferred_element_type=F32)
    depth = lax.dot_general(picks(pairs, cols), depth_ref[...], contract, **exact)
    albedo = lax.dot_general(pick_ends, albedo_ref[...], contract, **exact)
    valid = lax.dot_general(pick_ends, valid_ref[...].astype(F32), contract, **exact)
    fwd_ref[...] = jnp.zeros_like(fwd_ref)
    bwd_ref[...] = jnp.zeros_like(bwd_ref)
    sr_ref[...] = jnp.zeros_like(sr_ref)
    pick16 = picks([0, w - 1], w).astype(jnp.bfloat16)
    for k in range(nl):
        q = li ^ k
        for l in range(lights):
            e = lax.dot_general(
                pick16, block_refs[k][pl.ds(l * rows, rows), :], contract, preferred_element_type=F32
            )
            eh_ref[q, lights + l : lights + l + 1, :] = e[0:1]
            eh_ref[q + 2, l : l + 1, :] = e[1:2]
    n = lights
    last = 4 * (nl - 1)
    bwd_ref[0:n, :] = eh_ref[0, n : 2 * n, :]
    fwd_ref[0:n, :] = eh_ref[nl + 1, 0:n, :]
    fwd_ref[n : n + 2, :] = depth[last + 2 : last + 4]
    fwd_ref[n + 2 : n + 3, :] = albedo[2 * nl - 1 : 2 * nl]
    fwd_ref[n + 3 : n + 4, :] = valid[2 * nl - 1 : 2 * nl]
    bwd_ref[n : n + 2, :] = depth[0:2]
    bwd_ref[n + 2 : n + 3, :] = albedo[0:1]
    bwd_ref[n + 3 : n + 4, :] = valid[0:1]
    for q in range(nl):
        sr_ref[q, 2:3, :] = depth[4 * q : 4 * q + 1]
        sr_ref[q, 3:4, :] = depth[4 * q + 3 : 4 * q + 4]
        if q > 0:
            sr_ref[q, 0:2, :] = depth[4 * q - 2 : 4 * q]
            sr_ref[q, 6:7, :] = albedo[2 * q - 1 : 2 * q]
            sr_ref[q, 8:9, :] = valid[2 * q - 1 : 2 * q]
        if q < nl - 1:
            sr_ref[q, 4:6, :] = depth[4 * q + 4 : 4 * q + 6]
            sr_ref[q, 7:8, :] = albedo[2 * q + 2 : 2 * q + 3]
            sr_ref[q, 9:10, :] = valid[2 * q + 2 : 2 * q + 3]


def halos_body(nl, eh_ref, sr_ref, low_ref, high_ref, table_ref, *outs):
    small_refs, own_ref = outs[:nl], outs[nl]
    li = lax.axis_index("light")
    n = table_ref.shape[0]
    table = table_ref[...].astype(F32)
    for k in range(nl):
        q = li ^ k
        ref = small_refs[k]
        ref[0 : 2 * n, :] = eh_ref[q + 1]
        ref[2 * n :, :] = jnp.zeros((ref.shape[0] - 2 * n, ref.shape[1]), F32)
        ref[2 * n : 3 * n, 0:4] = table

        @pl.when(q == 0)
        def _():
            ref[0:n, :] = low_ref[0:n, :]

        @pl.when(q == nl - 1)
        def _():
            ref[n : 2 * n, :] = high_ref[0:n, :]

    own_ref[...] = sr_ref[li]

    @pl.when(li == 0)
    def _():
        own_ref[0:2, :] = low_ref[n : n + 2, :]
        own_ref[6:7, :] = low_ref[n + 2 : n + 3, :]
        own_ref[8:9, :] = low_ref[n + 3 : n + 4, :]

    @pl.when(li == nl - 1)
    def _():
        own_ref[4:6, :] = high_ref[n : n + 2, :]
        own_ref[7:8, :] = high_ref[n + 2 : n + 3, :]
        own_ref[9:10, :] = high_ref[n + 3 : n + 4, :]


def decode(table):
    return (
        table[:, 0:1] / 500.0 - 1.0,
        table[:, 1:2] / 500.0 - 1.0,
        1.0 + table[:, 2:3] / 1000.0,
        0.5 + table[:, 3:4] / 1000.0,
    )


def decode_rows(table):
    return (
        table[0:1] / 500.0 - 1.0,
        table[1:2] / 500.0 - 1.0,
        1.0 + table[2:3] / 1000.0,
        0.5 + table[3:4] / 1000.0,
    )


def columns_from(left, right, shape):
    rows, w = shape
    at = iota((w, rows), 0)
    return jnp.transpose(jnp.where(at == 0, left, jnp.where(at == w - 1, right, 0.0)))


def shifts_rows(x):
    r = iota(x.shape, 0)
    n = x.shape[0]
    above = jnp.where(r == 0, 0.0, pltpu.roll(x, 1, 0))
    below = jnp.where(r == n - 1, 0.0, pltpu.roll(x, n - 1, 0))
    return above, below


def shifts_cols(x, ends):
    c = iota(x.shape, 1)
    n = x.shape[1]
    before = jnp.where(c == 0, ends, pltpu.roll(x, 1, 1))
    after = jnp.where(c == n - 1, ends, pltpu.roll(x, n - 1, 1))
    return before, after


def fill_context(ctx_ref, surface, albedo, left, right):
    ends = columns_from(left, right, surface.shape)
    before, after = shifts_cols(surface, ends)
    above, below = shifts_rows(surface)
    sx = 0.5 * (after - before)
    sy = 0.5 * (below - above)
    ctx_ref[0] = surface
    ctx_ref[1] = sx
    ctx_ref[2] = sy
    ctx_ref[3] = albedo * lax.rsqrt(1.0 + sx * sx + sy * sy)


def fill_params(pb_ref, base, block_ref, n, w, place, total):
    under = block_ref[pl.ds(block_ref.shape[0] - 16, 16), :].astype(F32)
    lx, ly, lz, le = decode_rows(under[0:4] * 32.0 + under[4:8])
    col = iota((8, w), 1) + place * w
    px = (col.astype(F32) + 0.5) / total - 0.5
    for j in range(n):
        dx = jnp.broadcast_to(lx[:, j : j + 1], (8, w)) - px
        pb_ref[base + j, 0] = dx
        pb_ref[base + j, 1] = dx * dx
        pb_ref[base + j, 2] = jnp.broadcast_to(ly[:, j : j + 1], (8, w))
        pb_ref[base + j, 3] = jnp.broadcast_to(lz[:, j : j + 1], (8, w))
        pb_ref[base + j, 4] = jnp.broadcast_to(le[:, j : j + 1], (8, w))


def accumulate(state, tile, py, obs, pb_ref, base):
    surface, sx, sy, scaled = tile
    kept = []
    least = None
    for j in range(len(obs)):
        dx, dx2 = pb_ref[base + j, 0], pb_ref[base + j, 1]
        dy = pb_ref[base + j, 2] - py
        dz = pb_ref[base + j, 3] - surface
        dist = (dx2 + dy * dy) + dz * dz
        facing = dz - (sx * dx + sy * dy)
        r = lax.rsqrt(dist)
        r2 = r * r
        g = (r2 * r) * pb_ref[base + j, 4]
        residual = scaled * (g * facing) - obs[j]
        square = residual * residual
        least = square if least is None else jnp.minimum(least, square)
        kept.append((square, residual * g, facing, dz * r2, dx, dy))
    if state is not None:
        before = state[0]
        least = jnp.minimum(least, before)
    sums = None
    for square, q, facing, drop, dx, dy in kept:
        w = jnp.exp2((least - square) * HALF_LOG2E)
        p = w * q
        pf = p * facing
        terms = (w, p, p * dx, p * dy, pf, pf * drop)
        sums = terms if sums is None else tuple(a + b for a, b in zip(sums, terms))
    if state is not None:
        fade = jnp.exp2((least - before) * HALF_LOG2E)
        sums = tuple(a * fade + b for a, b in zip(state[1:], sums))
    return (least,) + sums


def sweep(ctx_ref, pb_ref, obs_refs, bases, total, load, store):
    rows, w = ctx_ref.shape[1:]
    lights = obs_refs[0].shape[0] // rows
    split = (TR // 8, 8, w)

    def step(i, carry):
        at = pl.ds(pl.multiple_of(i * TR, TR), TR)
        tile = tuple(ctx_ref[f, at, :].reshape(split) for f in range(4))
        row = iota(split, 0) * 8 + iota(split, 1) + i * TR
        py = (row.astype(F32) + (0.5 - rows / 2.0)) / total
        state = load(at)
        for obs_ref, base in zip(obs_refs, bases):
            obs = [
                obs_ref[pl.ds(pl.multiple_of(j * rows + i * TR, TR), TR), :].astype(F32).reshape(split)
                for j in range(lights)
            ]
            state = accumulate(state, tile, py, obs, pb_ref, base)
        store(at, state)
        return carry

    lax.fori_loop(0, rows // TR, step, 0)


def state_load(state_ref, w):
    return lambda at: tuple(state_ref[f, at, :].reshape(TR // 8, 8, w) for f in range(7))


def state_store(state_ref, w):
    def store(at, state):
        for f in range(7):
            state_ref[f, at, :] = state[f].reshape(TR, w)

    return store


def halo_slope(column, side, small_refs, srow_ref, rows, total):
    n = small_refs[0].shape[0] // 3
    obs = jnp.concatenate([ref[side * n : (side + 1) * n, :] for ref in small_refs], axis=0)
    table = jnp.concatenate([ref[2 * n : 3 * n, :] for ref in small_refs], axis=0)
    lx, ly, lz, le = decode(table)
    outer, inner = (0, 2) if side == 0 else (5, 3)
    here = 1 if side == 0 else 4
    surface = srow_ref[here : here + 1, :]
    toward = srow_ref[inner : inner + 1, :] - srow_ref[outer : outer + 1, :]
    sx = 0.5 * toward if side == 0 else -0.5 * toward
    lane = iota((8, rows), 1)
    wide = jnp.broadcast_to(surface, (8, rows))
    above = jnp.where(lane == 0, 0.0, pltpu.roll(wide, 1, 1))
    below = jnp.where(lane == rows - 1, 0.0, pltpu.roll(wide, rows - 1, 1))
    sy = (0.5 * (below - above))[0:1]
    albedo = srow_ref[6 + side : 7 + side, :]
    valid = srow_ref[8 + side : 9 + side, :]
    px = (column.astype(F32) + 0.5) / total - 0.5
    py = (iota((1, rows), 1).astype(F32) + (0.5 - rows / 2.0)) / total
    rn = lax.rsqrt(1.0 + sx * sx + sy * sy)
    dx = jnp.broadcast_to(lx - px, obs.shape)
    dy = ly - py
    dz = lz - surface
    dist = dx * dx + dy * dy + dz * dz
    facing = dz - (sx * dx + sy * dy)
    r = lax.rsqrt(dist)
    g = (r * r) * r * le
    residual = (albedo * rn) * (g * facing) - obs
    square = residual * residual
    least = jnp.min(square, axis=0, keepdims=True)
    w = jnp.exp2((least - square) * HALF_LOG2E)
    p = w * residual * g
    total_w = jnp.sum(w, axis=0, keepdims=True)
    px_sum = jnp.sum(p * dx, axis=0, keepdims=True)
    pf_sum = jnp.sum(p * facing, axis=0, keepdims=True)
    return -(valid * albedo * rn / total_w) * (px_sum + (sx * rn * rn) * pf_sum)


def gradients(state_ref, ctx_ref, albedo, valid, slope_low, slope_high):
    sx, sy = ctx_ref[1], ctx_ref[2]
    rn = lax.rsqrt(1.0 + sx * sx + sy * sy)
    inverse = valid * rn / state_ref[1]
    factor = inverse * albedo
    pf = state_ref[5]
    rn2pf = rn * rn * pf
    grad_albedo = inverse * pf
    direct = factor * (3.0 * state_ref[6] - state_ref[2])
    grad_x = -factor * (state_ref[3] + sx * rn2pf)
    grad_y = -factor * (state_ref[4] + sy * rn2pf)
    before, after = shifts_cols(grad_x, columns_from(slope_low, slope_high, grad_x.shape))
    above, below = shifts_rows(grad_y)
    return direct + 0.5 * (before - after) + 0.5 * (above - below), grad_albedo


def partial_sums(depth, albedo):
    n = depth.shape[1]
    d = jnp.sum(depth * depth, axis=0, keepdims=True)
    a = jnp.sum(albedo * albedo, axis=0, keepdims=True)
    d = jnp.broadcast_to(d, (8, n))
    a = jnp.broadcast_to(a, (8, n))
    d = d + pltpu.roll(d, n // 2, 1)
    a = a + pltpu.roll(a, n // 2, 1)
    return jnp.where(iota((8, n), 1) < n // 2, d, a)[0:1]


def inverse_scales(recv_ref, row, count):
    rows = recv_ref[:, row, :]
    n = rows.shape[1]
    lane = iota(rows.shape, 1)
    d = jnp.sum(jnp.where(lane < n // 2, rows, 0.0), keepdims=True)
    a = jnp.sum(jnp.where(lane < n // 2, 0.0, rows), keepdims=True)
    return lax.rsqrt(d / count + EPS), lax.rsqrt(a / count + EPS)


def first_body(depth_ref, albedo_ref, valid_ref, srow_ref, obs0, obs1, ctx_ref, mask_ref, state_ref, pb_ref):
    li, _, place, count = position()
    rows, w = ctx_ref.shape[1:]
    at = pl.ds(pl.multiple_of(li * w, w), w)
    albedo = albedo_ref[:, at]
    mask_ref[0] = albedo
    mask_ref[1] = valid_ref[:, at].astype(F32)
    fill_context(ctx_ref, depth_ref[:, at], albedo, srow_ref[1:2, :], srow_ref[4:5, :])
    total = w * count
    n = obs0.shape[0] // rows
    fill_params(pb_ref, 0, obs0, n, w, place, total)
    fill_params(pb_ref, n, obs1, n, w, place, total)
    sweep(ctx_ref, pb_ref, (obs0, obs1), (0, n), total, lambda at: None, state_store(state_ref, w))


def more_body(ctx_ref, in_ref, obs, state_ref, pb_ref):
    _, _, place, count = position()
    rows, w = ctx_ref.shape[1:]
    total = w * count
    fill_params(pb_ref, 0, obs, obs.shape[0] // rows, w, place, total)
    sweep(ctx_ref, pb_ref, (obs,), (0,), total, state_load(in_ref, w), state_store(state_ref, w))


def finish(state_ref, ctx_ref, albedo, valid, small_refs, srow_ref, grad_ref, edge_ref, pay_ref):
    _, _, place, count = position()
    rows, w = ctx_ref.shape[1:]
    total = w * count
    low = halo_slope(place * w - 1, 0, small_refs, srow_ref, rows, total)
    high = halo_slope(place * w + w, 1, small_refs, srow_ref, rows, total)
    depth, grad_albedo = gradients(state_ref, ctx_ref, albedo, valid, low, high)
    sums = partial_sums(depth, grad_albedo)
    if edge_ref is None:
        pay_ref[...] = jnp.broadcast_to(sums[None], pay_ref.shape)
        return depth, grad_albedo
    grad_ref[0] = depth
    grad_ref[1] = grad_albedo
    dt = jnp.transpose(depth)
    at = jnp.transpose(grad_albedo)
    edge_ref[0:1, :] = dt[0:1]
    edge_ref[1:2, :] = dt[w - 1 : w]
    pay_ref[:, 0:2, :] = jnp.broadcast_to(dt[0:2][None], (count, 2, rows))
    pay_ref[:, 2:3, :] = jnp.broadcast_to(at[0:1][None], (count, 1, rows))
    pay_ref[:, 3:4, :] = jnp.broadcast_to(sums[None], (count, 1, w))

    @pl.when(place < count - 1)
    def _():
        to = exchange_index(place + 1)
        pay_ref[to, 0:2, :] = dt[w - 2 : w]
        pay_ref[to, 2:3, :] = at[w - 1 : w]

    return depth, grad_albedo


def last_body(nl, ctx_ref, mask_ref, state_ref, srow_ref, *rest):
    small_refs, (grad_ref, edge_ref, pay_ref) = rest[:nl], rest[nl:]
    edge_ref[...] = jnp.zeros_like(edge_ref)
    finish(state_ref, ctx_ref, mask_ref[0], mask_ref[1], small_refs, srow_ref, grad_ref, edge_ref, pay_ref)


def second_body(nl, recv_ref, grad_ref, edge_ref, ctx0_ref, mask_ref, srow0_ref, *rest):
    small_refs, obs_refs = rest[:nl], rest[nl : 2 * nl]
    out_ref, pay_ref, ctx_ref, state_ref, pb_ref, srow_ref = rest[2 * nl :]
    _, _, place, count = position()
    rows, w = ctx_ref.shape[1:]
    total = w * count
    inv_depth, inv_albedo = inverse_scales(recv_ref, 3, float(rows * total))
    surface = ctx0_ref[0] - STEP_DEPTH * jnp.tanh(grad_ref[0] * inv_depth)
    albedo = mask_ref[0] - STEP_ALBEDO * jnp.tanh(grad_ref[1] * inv_albedo)
    out_ref[0] = surface
    out_ref[1] = albedo
    srow_ref[...] = jnp.zeros_like(srow_ref)
    srow_ref[2:4, :] = edge_ref[0:2, :]

    @pl.when(place > 0)
    def _():
        frm = exchange_index(jnp.maximum(place - 1, 0))
        srow_ref[0:2, :] = recv_ref[frm, 0:2, :]
        srow_ref[6:7, :] = recv_ref[frm, 2:3, :]

    @pl.when(place < count - 1)
    def _():
        frm = exchange_index(jnp.minimum(place + 1, count - 1))
        srow_ref[4:6, :] = recv_ref[frm, 0:2, :]
        srow_ref[7:8, :] = recv_ref[frm, 2:3, :]

    changes = srow_ref[0:8, :]
    kind = iota(changes.shape, 0) < 6
    changes = jnp.where(
        kind, STEP_DEPTH * jnp.tanh(changes * inv_depth), STEP_ALBEDO * jnp.tanh(changes * inv_albedo)
    )
    srow_ref[0:8, :] = srow0_ref[0:8, :] - changes
    srow_ref[8:16, :] = srow0_ref[8:16, :]
    fill_context(ctx_ref, surface, albedo, srow_ref[1:2, :], srow_ref[4:5, :])
    n = obs_refs[0].shape[0] // rows
    bases = tuple(k * n for k in range(nl))
    for k in range(nl):
        fill_params(pb_ref, bases[k], obs_refs[k], n, w, place, total)
    sweep(ctx_ref, pb_ref, obs_refs, bases, total, lambda at: None, state_store(state_ref, w))
    depth, grad_albedo = finish(
        state_ref, ctx_ref, albedo, mask_ref[1], small_refs, srow_ref, None, None, pay_ref
    )
    out_ref[2] = depth
    out_ref[3] = grad_albedo


def final_body(nl, recv_ref, *rest):
    parts, (depth_ref, albedo_ref) = rest[:nl], rest[nl:]
    li, _, _, count = position()
    rows, w = parts[0].shape[1:]
    inv_depth, inv_albedo = inverse_scales(recv_ref, 0, float(rows * w * count))
    for k in range(nl):
        at = pl.ds(pl.multiple_of((li ^ k) * w, w), w)
        depth_ref[:, at] = parts[k][0] - STEP_DEPTH * jnp.tanh(parts[k][2] * inv_depth)
        albedo_ref[:, at] = parts[k][1] - STEP_ALBEDO * jnp.tanh(parts[k][3] * inv_albedo)


def shape(*dims, dtype=F32):
    return jax.ShapeDtypeStruct(dims, dtype)


def program(depth_start, albedo_start, observations, light_table, valid_mask):
    nl, ns = lax.axis_size("light"), lax.axis_size("strip")
    nd = nl * ns
    lights, rows, cols = observations.shape
    w = cols // nl

    def swap(x, k):
        return lax.ppermute(x, "light", [(i, i ^ k) for i in range(nl)])

    hbm = pl.BlockSpec(memory_space=pltpu.HBM)
    blocks = call(
        functools.partial(cut_body, nl),
        tuple(shape(lights * rows + 16, w, dtype=jnp.bfloat16) for _ in range(nl)),
        [pltpu.VMEM((4, lights), jnp.int32), pltpu.SemaphoreType.DMA((nl * lights + 1,))],
        vmem=54_750_000,
        in_specs=[hbm, hbm],
    )(observations, light_table.T)
    obs2 = swap(blocks[2], 2)
    obs3 = swap(blocks[3], 3)
    obs1 = swap(blocks[1], 1)
    obs0 = blocks[0]
    up = 2 * lights
    fwd, bwd, eh, sr = call(
        functools.partial(edges_body, nl),
        (shape(up, rows), shape(up, rows), shape(nl + 2, up, rows), shape(nl, 16, rows)),
    )(depth_start, albedo_start, valid_mask, *blocks)
    low = lax.ppermute(fwd, "strip", [(i, i + 1) for i in range(ns - 1)])
    high = lax.ppermute(bwd, "strip", [(i + 1, i) for i in range(ns - 1)])
    *small, srow = call(
        functools.partial(halos_body, nl), tuple(shape(3 * lights, rows) for _ in range(nl)) + (shape(16, rows),)
    )(eh, sr, low, high, light_table)
    small = [small[0]] + [swap(small[k], k) for k in range(1, nl)]

    pb = pltpu.VMEM((2 * lights, 5, 8, w), F32)
    field = (rows, w)
    ctx, mask, state = call(
        first_body, (shape(4, *field), shape(2, *field), shape(7, *field)), [pb]
    )(depth_start, albedo_start, valid_mask, srow, obs0, obs1)
    state = call(more_body, shape(7, *field), [pb])(ctx, state, obs2)
    state = call(more_body, shape(7, *field), [pb])(ctx, state, obs3)
    grad, edge, pay = call(
        functools.partial(last_body, nl), (shape(2, *field), shape(8, rows), shape(nd, 4, rows))
    )(ctx, mask, state, srow, *small)
    recv = lax.all_to_all(pay, AXES, 0, 0, tiled=True)
    own, pay = call(
        functools.partial(second_body, nl),
        (shape(4, *field), shape(nd, 1, rows)),
        [
            pltpu.VMEM((4, *field), F32),
            pltpu.VMEM((7, *field), F32),
            pltpu.VMEM((nl * lights, 5, 8, w), F32),
            pltpu.VMEM((16, rows), F32),
        ],
    )(recv, grad, edge, ctx, mask, srow, *small, obs0, obs1, obs2, obs3)
    part2 = swap(own, 2)
    part1 = swap(own, 1)
    recv = lax.all_to_all(pay, AXES, 0, 0, tiled=True)
    recv, part2 = lax.optimization_barrier((recv, part2))
    part3 = swap(part2, 1)
    return tuple(
        call(functools.partial(final_body, nl), (shape(rows, cols), shape(rows, cols)))(recv, own, part1, part2, part3)
    )


def solution(mesh):
    in_specs = (
        P(None, "strip"),
        P(None, "strip"),
        P("light", None, "strip"),
        P("light", None),
        P(None, "strip"),
    )
    out_specs = (P(None, "strip"), P(None, "strip"))
    return jax.shard_map(program, mesh=mesh, in_specs=in_specs, out_specs=out_specs, check_vma=False)
```

```python
import functools
import math

import jax
import jax.numpy as jnp
from jax import lax
from jax.experimental import pallas as pl
from jax.experimental.pallas import tpu as pltpu
from jax.sharding import PartitionSpec as P


AXES = ("light", "strip")
STEP_DEPTH = 0.1
STEP_ALBEDO = 0.2
EPS = 1e-06
HALF_LOG2E = 0.5 * math.log2(math.e)
F32 = jnp.float32
VM = pl.BlockSpec(memory_space=pltpu.VMEM)
TR = 16
CUT_VMEM = 40 << 20


def iota(shape, dim):
    return lax.broadcasted_iota(jnp.int32, shape, dim)


def position():
    nl, ns = lax.axis_size("light"), lax.axis_size("strip")
    li, si = lax.axis_index("light"), lax.axis_index("strip")
    return li, si, si * nl + li, nl * ns


def exchange_index(place):
    nl, ns = lax.axis_size("light"), lax.axis_size("strip")
    return lax.rem(place, nl) * ns + lax.div(place, nl)


def call(body, out, scratch=(), vmem=40 << 20, **more):
    return pl.pallas_call(
        body,
        out_shape=out,
        scratch_shapes=list(scratch),
        compiler_params=pltpu.CompilerParams(vmem_limit_bytes=vmem),
        **more,
    )


def cut_body(nl, obs_ref, table_ref, depth_ref, albedo_ref, valid_ref, *rest):
    blocks, (tile_ref, surf_ref, sr_ref), (table, near, mask, sems, extra) = rest[:nl], rest[nl : nl + 3], rest[nl + 3 :]
    lights, rows, cols = obs_ref.shape
    w = cols // nl
    li = lax.axis_index("light")

    def columns(q):
        return pl.ds(pl.multiple_of(q * w, w), w)

    fetch = pltpu.make_async_copy(table_ref, table, extra.at[0])
    fetch.start()
    sides = (jnp.maximum(li - 1, 0), li, jnp.minimum(li + 1, nl - 1))
    edges = []
    for f, (source, target) in enumerate(((depth_ref, near), (albedo_ref, near), (valid_ref, mask))):
        for side, q in enumerate(sides):
            slot = target.at[side] if f == 2 else target.at[f, side]
            edges.append(pltpu.make_async_copy(source.at[:, columns(q)], slot, extra.at[1 + 3 * f + side]))
            edges[-1].start()
    copies = []
    for k in (2, 3, 1, 0):
        for l in range(lights):
            copy = pltpu.make_async_copy(
                obs_ref.at[l, :, columns(li ^ k)], blocks[k].at[pl.ds(l * rows, rows)], sems.at[k * lights + l]
            )
            copy.start()
            copies.append(copy)
    fetch.wait()
    entries = table[...]
    high = lax.shift_right_logical(entries, 5)
    both = jnp.concatenate([high, entries - high * 32], axis=0).astype(F32)
    wide = jnp.concatenate([both, jnp.zeros((8, w - lights), F32)], axis=1)
    under = jnp.concatenate([wide, jnp.zeros((8, w), F32)], axis=0).astype(jnp.bfloat16)
    for k in range(nl):
        blocks[k][pl.ds(lights * rows, 16), :] = under
    for copy in edges:
        copy.wait()
    lane = iota((rows, w), 1)
    is_last = li == nl - 1
    surf_ref[...] = jnp.zeros_like(surf_ref)
    sr_ref[...] = jnp.zeros_like(sr_ref)
    for f in range(3):
        before, own, after = (mask[s].astype(F32) if f == 2 else near[f, s] for s in range(3))
        tile_ref[f] = own
        inner = jnp.transpose(own)
        outer = jnp.transpose(jnp.where(lane < w // 2, after, before))
        low = jnp.where(li == 0, 0.0, outer[w - 2 : w])
        high = jnp.where(is_last, 0.0, outer[0:2])
        if f == 0:
            sr_ref[0:2, :] = low
            sr_ref[2:3, :] = inner[0:1]
            sr_ref[3:4, :] = inner[w - 1 : w]
            sr_ref[4:6, :] = high
            surf_ref[0:2, :] = jnp.where(is_last, inner[w - 2 : w], inner[0:2])
        else:
            at = 4 + 2 * f
            sr_ref[at : at + 1, :] = low[1:2]
            sr_ref[at + 1 : at + 2, :] = high[0:1]
            surf_ref[1 + f : 2 + f, :] = jnp.where(is_last, inner[w - 1 : w], inner[0:1])
    for copy in copies:
        copy.wait()


def edges_body(nl, *rest):
    block_refs, (fwd_ref, bwd_ref, eh_ref) = rest[:nl], rest[nl:]
    w = block_refs[0].shape[1]
    rows, n = eh_ref.shape[2], eh_ref.shape[1] // 2
    li = lax.axis_index("light")
    at, col = iota((8, w), 0), iota((8, w), 1)
    pick = (((at == 0) & (col == 0)) | ((at == 1) & (col == w - 1))).astype(jnp.bfloat16)
    for k in range(nl):
        q = li ^ k
        for l in range(n):
            e = lax.dot_general(
                pick,
                block_refs[k][pl.ds(l * rows, rows), :],
                (((1,), (1,)), ((), ())),
                preferred_element_type=F32,
            )
            eh_ref[q, n + l : n + l + 1, :] = e[0:1]
            eh_ref[q + 2, l : l + 1, :] = e[1:2]
    bwd_ref[...] = eh_ref[0, n : 2 * n, :]
    fwd_ref[...] = eh_ref[nl + 1, 0:n, :]


def halos_body(nl, eh_ref, low_ref, high_ref, table_ref, *small_refs):
    li = lax.axis_index("light")
    n = table_ref.shape[0]
    table = table_ref[...].astype(F32)
    for k in range(nl):
        q = li ^ k
        ref = small_refs[k]
        ref[0 : 2 * n, :] = eh_ref[q + 1]
        ref[2 * n :, :] = jnp.zeros((ref.shape[0] - 2 * n, ref.shape[1]), F32)
        ref[2 * n : 3 * n, 0:4] = table

        @pl.when(q == 0)
        def _():
            ref[0:n, :] = low_ref[...]

        @pl.when(q == nl - 1)
        def _():
            ref[n : 2 * n, :] = high_ref[...]


def decode(table):
    return (
        table[:, 0:1] / 500.0 - 1.0,
        table[:, 1:2] / 500.0 - 1.0,
        1.0 + table[:, 2:3] / 1000.0,
        0.5 + table[:, 3:4] / 1000.0,
    )


def decode_rows(table):
    return (
        table[0:1] / 500.0 - 1.0,
        table[1:2] / 500.0 - 1.0,
        1.0 + table[2:3] / 1000.0,
        0.5 + table[3:4] / 1000.0,
    )


def columns_from(left, right, shape):
    rows, w = shape
    at = iota((w, rows), 0)
    return jnp.transpose(jnp.where(at == 0, left, jnp.where(at == w - 1, right, 0.0)))


def shifts_rows(x):
    r = iota(x.shape, 0)
    n = x.shape[0]
    above = jnp.where(r == 0, 0.0, pltpu.roll(x, 1, 0))
    below = jnp.where(r == n - 1, 0.0, pltpu.roll(x, n - 1, 0))
    return above, below


def shifts_cols(x, ends):
    c = iota(x.shape, 1)
    n = x.shape[1]
    before = jnp.where(c == 0, ends, pltpu.roll(x, 1, 1))
    after = jnp.where(c == n - 1, ends, pltpu.roll(x, n - 1, 1))
    return before, after


def fill_context(ctx_ref, surface, albedo, left, right):
    ends = columns_from(left, right, surface.shape)
    before, after = shifts_cols(surface, ends)
    above, below = shifts_rows(surface)
    sx = 0.5 * (after - before)
    sy = 0.5 * (below - above)
    ctx_ref[0] = surface
    ctx_ref[1] = sx
    ctx_ref[2] = sy
    ctx_ref[3] = albedo * lax.rsqrt(1.0 + sx * sx + sy * sy)


def fill_params(pb_ref, base, block_ref, n, w, place, total):
    under = block_ref[pl.ds(block_ref.shape[0] - 16, 16), :].astype(F32)
    lx, ly, lz, le = decode_rows(under[0:4] * 32.0 + under[4:8])
    col = iota((8, w), 1) + place * w
    px = (col.astype(F32) + 0.5) / total - 0.5
    for j in range(n):
        dx = jnp.broadcast_to(lx[:, j : j + 1], (8, w)) - px
        pb_ref[base + j, 0] = dx
        pb_ref[base + j, 1] = dx * dx
        pb_ref[base + j, 2] = jnp.broadcast_to(ly[:, j : j + 1], (8, w))
        pb_ref[base + j, 3] = jnp.broadcast_to(lz[:, j : j + 1], (8, w))
        pb_ref[base + j, 4] = jnp.broadcast_to(le[:, j : j + 1], (8, w))


def accumulate(state, tile, py, obs, pb_ref, base):
    surface, sx, sy, scaled = tile
    kept = []
    least = None
    for j in range(len(obs)):
        dx, dx2 = pb_ref[base + j, 0], pb_ref[base + j, 1]
        dy = pb_ref[base + j, 2] - py
        dz = pb_ref[base + j, 3] - surface
        dist = (dx2 + dy * dy) + dz * dz
        facing = dz - (sx * dx + sy * dy)
        r = lax.rsqrt(dist)
        r2 = r * r
        g = (r2 * r) * pb_ref[base + j, 4]
        residual = scaled * (g * facing) - obs[j]
        square = residual * residual
        least = square if least is None else jnp.minimum(least, square)
        kept.append((square, residual * g, facing, dz * r2, dx, dy))
    if state is not None:
        before = state[0]
        least = jnp.minimum(least, before)
    sums = None
    for square, q, facing, drop, dx, dy in kept:
        w = jnp.exp2((least - square) * HALF_LOG2E)
        p = w * q
        pf = p * facing
        terms = (w, p, p * dx, p * dy, pf, pf * drop)
        sums = terms if sums is None else tuple(a + b for a, b in zip(sums, terms))
    if state is not None:
        fade = jnp.exp2((least - before) * HALF_LOG2E)
        sums = tuple(a * fade + b for a, b in zip(state[1:], sums))
    return (least,) + sums


def sweep(ctx_ref, pb_ref, obs_refs, bases, total, load, store):
    rows, w = ctx_ref.shape[1:]
    lights = obs_refs[0].shape[0] // rows
    split = (TR // 8, 8, w)

    def step(i, carry):
        at = pl.ds(pl.multiple_of(i * TR, TR), TR)
        tile = tuple(ctx_ref[f, at, :].reshape(split) for f in range(4))
        row = iota(split, 0) * 8 + iota(split, 1) + i * TR
        py = (row.astype(F32) + (0.5 - rows / 2.0)) / total
        state = load(at)
        for obs_ref, base in zip(obs_refs, bases):
            obs = [
                obs_ref[pl.ds(pl.multiple_of(j * rows + i * TR, TR), TR), :].astype(F32).reshape(split)
                for j in range(lights)
            ]
            state = accumulate(state, tile, py, obs, pb_ref, base)
        store(at, state)
        return carry

    lax.fori_loop(0, rows // TR, step, 0)


def state_load(state_ref, w):
    return lambda at: tuple(state_ref[f, at, :].reshape(TR // 8, 8, w) for f in range(7))


def state_store(state_ref, w):
    def store(at, state):
        for f in range(7):
            state_ref[f, at, :] = state[f].reshape(TR, w)

    return store


def halo_slope(column, side, small_refs, srow_ref, rows, total):
    n = small_refs[0].shape[0] // 3
    obs = jnp.concatenate([ref[side * n : (side + 1) * n, :] for ref in small_refs], axis=0)
    table = jnp.concatenate([ref[2 * n : 3 * n, :] for ref in small_refs], axis=0)
    lx, ly, lz, le = decode(table)
    outer, inner = (0, 2) if side == 0 else (5, 3)
    here = 1 if side == 0 else 4
    surface = srow_ref[here : here + 1, :]
    toward = srow_ref[inner : inner + 1, :] - srow_ref[outer : outer + 1, :]
    sx = 0.5 * toward if side == 0 else -0.5 * toward
    lane = iota((8, rows), 1)
    wide = jnp.broadcast_to(surface, (8, rows))
    above = jnp.where(lane == 0, 0.0, pltpu.roll(wide, 1, 1))
    below = jnp.where(lane == rows - 1, 0.0, pltpu.roll(wide, rows - 1, 1))
    sy = (0.5 * (below - above))[0:1]
    albedo = srow_ref[6 + side : 7 + side, :]
    valid = srow_ref[8 + side : 9 + side, :]
    px = (column.astype(F32) + 0.5) / total - 0.5
    py = (iota((1, rows), 1).astype(F32) + (0.5 - rows / 2.0)) / total
    rn = lax.rsqrt(1.0 + sx * sx + sy * sy)
    dx = jnp.broadcast_to(lx - px, obs.shape)
    dy = ly - py
    dz = lz - surface
    dist = dx * dx + dy * dy + dz * dz
    facing = dz - (sx * dx + sy * dy)
    r = lax.rsqrt(dist)
    g = (r * r) * r * le
    residual = (albedo * rn) * (g * facing) - obs
    square = residual * residual
    least = jnp.min(square, axis=0, keepdims=True)
    w = jnp.exp2((least - square) * HALF_LOG2E)
    p = w * residual * g
    total_w = jnp.sum(w, axis=0, keepdims=True)
    px_sum = jnp.sum(p * dx, axis=0, keepdims=True)
    pf_sum = jnp.sum(p * facing, axis=0, keepdims=True)
    return -(valid * albedo * rn / total_w) * (px_sum + (sx * rn * rn) * pf_sum)


def gradients(state_ref, ctx_ref, albedo, valid, slope_low, slope_high):
    sx, sy = ctx_ref[1], ctx_ref[2]
    rn = lax.rsqrt(1.0 + sx * sx + sy * sy)
    inverse = valid * rn / state_ref[1]
    factor = inverse * albedo
    pf = state_ref[5]
    rn2pf = rn * rn * pf
    grad_albedo = inverse * pf
    direct = factor * (3.0 * state_ref[6] - state_ref[2])
    grad_x = -factor * (state_ref[3] + sx * rn2pf)
    grad_y = -factor * (state_ref[4] + sy * rn2pf)
    before, after = shifts_cols(grad_x, columns_from(slope_low, slope_high, grad_x.shape))
    above, below = shifts_rows(grad_y)
    return direct + 0.5 * (before - after) + 0.5 * (above - below), grad_albedo


def partial_sums(depth, albedo):
    n = depth.shape[1]
    d = jnp.sum(depth * depth, axis=0, keepdims=True)
    a = jnp.sum(albedo * albedo, axis=0, keepdims=True)
    d = jnp.broadcast_to(d, (8, n))
    a = jnp.broadcast_to(a, (8, n))
    d = d + pltpu.roll(d, n // 2, 1)
    a = a + pltpu.roll(a, n // 2, 1)
    return jnp.where(iota((8, n), 1) < n // 2, d, a)[0:1]


def inverse_scales(recv_ref, row, count):
    rows = recv_ref[:, row, :]
    n = rows.shape[1]
    lane = iota(rows.shape, 1)
    d = jnp.sum(jnp.where(lane < n // 2, rows, 0.0), keepdims=True)
    a = jnp.sum(jnp.where(lane < n // 2, 0.0, rows), keepdims=True)
    return lax.rsqrt(d / count + EPS), lax.rsqrt(a / count + EPS)


def first_body(nl, tile_ref, sr_ref, surf_ref, obs0, obs1, ctx_ref, srow_ref, state_ref, pb_ref):
    li, _, place, count = position()
    rows, w = ctx_ref.shape[1:]
    srow_ref[...] = sr_ref[...]

    @pl.when(li == 0)
    def _():
        srow_ref[0:2, :] = surf_ref[0:2, :]
        srow_ref[6:7, :] = surf_ref[2:3, :]
        srow_ref[8:9, :] = surf_ref[3:4, :]

    @pl.when(li == nl - 1)
    def _():
        srow_ref[4:6, :] = surf_ref[0:2, :]
        srow_ref[7:8, :] = surf_ref[2:3, :]
        srow_ref[9:10, :] = surf_ref[3:4, :]

    fill_context(ctx_ref, tile_ref[0], tile_ref[1], srow_ref[1:2, :], srow_ref[4:5, :])
    total = w * count
    n = obs0.shape[0] // rows
    fill_params(pb_ref, 0, obs0, n, w, place, total)
    fill_params(pb_ref, n, obs1, n, w, place, total)
    sweep(ctx_ref, pb_ref, (obs0, obs1), (0, n), total, lambda at: None, state_store(state_ref, w))


def more_body(ctx_ref, in_ref, obs, state_ref, pb_ref):
    _, _, place, count = position()
    rows, w = ctx_ref.shape[1:]
    total = w * count
    fill_params(pb_ref, 0, obs, obs.shape[0] // rows, w, place, total)
    sweep(ctx_ref, pb_ref, (obs,), (0,), total, state_load(in_ref, w), state_store(state_ref, w))


def finish(state_ref, ctx_ref, albedo, valid, small_refs, srow_ref, grad_ref, edge_ref, pay_ref):
    _, _, place, count = position()
    rows, w = ctx_ref.shape[1:]
    total = w * count
    low = halo_slope(place * w - 1, 0, small_refs, srow_ref, rows, total)
    high = halo_slope(place * w + w, 1, small_refs, srow_ref, rows, total)
    depth, grad_albedo = gradients(state_ref, ctx_ref, albedo, valid, low, high)
    sums = partial_sums(depth, grad_albedo)
    if edge_ref is None:
        pay_ref[...] = jnp.broadcast_to(sums[None], pay_ref.shape)
        return depth, grad_albedo
    grad_ref[0] = depth
    grad_ref[1] = grad_albedo
    dt = jnp.transpose(depth)
    at = jnp.transpose(grad_albedo)
    edge_ref[0:1, :] = dt[0:1]
    edge_ref[1:2, :] = dt[w - 1 : w]
    pay_ref[:, 0:2, :] = jnp.broadcast_to(dt[0:2][None], (count, 2, rows))
    pay_ref[:, 2:3, :] = jnp.broadcast_to(at[0:1][None], (count, 1, rows))
    pay_ref[:, 3:4, :] = jnp.broadcast_to(sums[None], (count, 1, w))

    @pl.when(place < count - 1)
    def _():
        to = exchange_index(place + 1)
        pay_ref[to, 0:2, :] = dt[w - 2 : w]
        pay_ref[to, 2:3, :] = at[w - 1 : w]

    return depth, grad_albedo


def last_body(nl, ctx_ref, tile_ref, state_ref, srow_ref, *rest):
    small_refs, (grad_ref, edge_ref, pay_ref) = rest[:nl], rest[nl:]
    edge_ref[...] = jnp.zeros_like(edge_ref)
    finish(state_ref, ctx_ref, tile_ref[1], tile_ref[2], small_refs, srow_ref, grad_ref, edge_ref, pay_ref)


def second_body(nl, recv_ref, grad_ref, edge_ref, tile_ref, srow0_ref, *rest):
    small_refs, obs_refs = rest[:nl], rest[nl : 2 * nl]
    out_ref, pay_ref, ctx_ref, state_ref, pb_ref, srow_ref = rest[2 * nl :]
    _, _, place, count = position()
    rows, w = ctx_ref.shape[1:]
    total = w * count
    inv_depth, inv_albedo = inverse_scales(recv_ref, 3, float(rows * total))
    surface = tile_ref[0] - STEP_DEPTH * jnp.tanh(grad_ref[0] * inv_depth)
    albedo = tile_ref[1] - STEP_ALBEDO * jnp.tanh(grad_ref[1] * inv_albedo)
    out_ref[0] = surface
    out_ref[1] = albedo
    srow_ref[...] = jnp.zeros_like(srow_ref)
    srow_ref[2:4, :] = edge_ref[0:2, :]

    @pl.when(place > 0)
    def _():
        frm = exchange_index(jnp.maximum(place - 1, 0))
        srow_ref[0:2, :] = recv_ref[frm, 0:2, :]
        srow_ref[6:7, :] = recv_ref[frm, 2:3, :]

    @pl.when(place < count - 1)
    def _():
        frm = exchange_index(jnp.minimum(place + 1, count - 1))
        srow_ref[4:6, :] = recv_ref[frm, 0:2, :]
        srow_ref[7:8, :] = recv_ref[frm, 2:3, :]

    changes = srow_ref[0:8, :]
    kind = iota(changes.shape, 0) < 6
    changes = jnp.where(
        kind, STEP_DEPTH * jnp.tanh(changes * inv_depth), STEP_ALBEDO * jnp.tanh(changes * inv_albedo)
    )
    srow_ref[0:8, :] = srow0_ref[0:8, :] - changes
    srow_ref[8:16, :] = srow0_ref[8:16, :]
    fill_context(ctx_ref, surface, albedo, srow_ref[1:2, :], srow_ref[4:5, :])
    n = obs_refs[0].shape[0] // rows
    bases = tuple(k * n for k in range(nl))
    for k in range(nl):
        fill_params(pb_ref, bases[k], obs_refs[k], n, w, place, total)
    sweep(ctx_ref, pb_ref, obs_refs, bases, total, lambda at: None, state_store(state_ref, w))
    depth, grad_albedo = finish(
        state_ref, ctx_ref, albedo, tile_ref[2], small_refs, srow_ref, None, None, pay_ref
    )
    out_ref[2] = depth
    out_ref[3] = grad_albedo


def final_body(nl, recv_ref, *rest):
    parts, (depth_ref, albedo_ref) = rest[:nl], rest[nl:]
    li, _, _, count = position()
    rows, w = parts[0].shape[1:]
    inv_depth, inv_albedo = inverse_scales(recv_ref, 0, float(rows * w * count))
    for k in range(nl):
        at = pl.ds(pl.multiple_of((li ^ k) * w, w), w)
        depth_ref[:, at] = parts[k][0] - STEP_DEPTH * jnp.tanh(parts[k][2] * inv_depth)
        albedo_ref[:, at] = parts[k][1] - STEP_ALBEDO * jnp.tanh(parts[k][3] * inv_albedo)


def shape(*dims, dtype=F32):
    return jax.ShapeDtypeStruct(dims, dtype)


def program(depth_start, albedo_start, observations, light_table, valid_mask):
    nl, ns = lax.axis_size("light"), lax.axis_size("strip")
    nd = nl * ns
    lights, rows, cols = observations.shape
    w = cols // nl

    def swap(x, k):
        return lax.ppermute(x, "light", [(i, i ^ k) for i in range(nl)])

    hbm = pl.BlockSpec(memory_space=pltpu.HBM)
    field = (rows, w)
    whole = (observations, light_table.T, depth_start, albedo_start, valid_mask)
    *blocks, tile, surf, sr = call(
        functools.partial(cut_body, nl),
        tuple(shape(lights * rows + 16, w, dtype=jnp.bfloat16) for _ in range(nl))
        + (shape(3, *field), shape(8, rows), shape(16, rows)),
        [
            pltpu.VMEM((4, lights), jnp.int32),
            pltpu.VMEM((2, 3, *field), F32),
            pltpu.VMEM((3, *field), jnp.int32),
            pltpu.SemaphoreType.DMA((nl * lights,)),
            pltpu.SemaphoreType.DMA((10,)),
        ],
        vmem=CUT_VMEM,
        in_specs=[hbm] * 5,
    )(*(pltpu.with_memory_space_constraint(x, pltpu.HBM) for x in whole))
    obs2 = swap(blocks[2], 2)
    obs3 = swap(blocks[3], 3)
    obs1 = swap(blocks[1], 1)
    obs0 = blocks[0]
    up = [((nl - 1) * ns + i, i + 1) for i in range(ns - 1)]
    surf = lax.ppermute(surf, AXES, up + [(target, source) for source, target in up])
    fwd, bwd, eh = call(
        functools.partial(edges_body, nl), (shape(lights, rows), shape(lights, rows), shape(nl + 2, 2 * lights, rows))
    )(*blocks)
    low = lax.ppermute(fwd, "strip", [(i, i + 1) for i in range(ns - 1)])
    high = lax.ppermute(bwd, "strip", [(i + 1, i) for i in range(ns - 1)])
    small = call(
        functools.partial(halos_body, nl), tuple(shape(3 * lights, rows) for _ in range(nl))
    )(eh, low, high, light_table)
    small = [small[0]] + [swap(small[k], k) for k in range(1, nl)]

    pb = pltpu.VMEM((2 * lights, 5, 8, w), F32)
    ctx, srow, state = call(
        functools.partial(first_body, nl), (shape(4, *field), shape(16, rows), shape(7, *field)), [pb]
    )(tile, sr, surf, obs0, obs1)
    state = call(more_body, shape(7, *field), [pb])(ctx, state, obs2)
    state = call(more_body, shape(7, *field), [pb])(ctx, state, obs3)
    grad, edge, pay = call(
        functools.partial(last_body, nl), (shape(2, *field), shape(8, rows), shape(nd, 4, rows))
    )(ctx, tile, state, srow, *small)
    recv = lax.all_to_all(pay, AXES, 0, 0, tiled=True)
    own, pay = call(
        functools.partial(second_body, nl),
        (shape(4, *field), shape(nd, 1, rows)),
        [
            pltpu.VMEM((4, *field), F32),
            pltpu.VMEM((7, *field), F32),
            pltpu.VMEM((nl * lights, 5, 8, w), F32),
            pltpu.VMEM((16, rows), F32),
        ],
    )(recv, grad, edge, tile, srow, *small, obs0, obs1, obs2, obs3)
    part2 = swap(own, 2)
    part1 = swap(own, 1)
    recv = lax.all_to_all(pay, AXES, 0, 0, tiled=True)
    recv, part2 = lax.optimization_barrier((recv, part2))
    part3 = swap(part2, 1)
    return tuple(
        call(functools.partial(final_body, nl), (shape(rows, cols), shape(rows, cols)))(recv, own, part1, part2, part3)
    )


def solution(mesh):
    in_specs = (
        P(None, "strip"),
        P(None, "strip"),
        P("light", None, "strip"),
        P("light", None),
        P(None, "strip"),
    )
    out_specs = (P(None, "strip"), P(None, "strip"))
    return jax.shard_map(program, mesh=mesh, in_specs=in_specs, out_specs=out_specs, check_vma=False)
```

```python
import functools
import math

import jax
import jax.numpy as jnp
from jax import lax
from jax.experimental import pallas as pl
from jax.experimental.pallas import tpu as pltpu
from jax.sharding import PartitionSpec as P


AXES = ("light", "strip")
STEP_DEPTH = 0.1
STEP_ALBEDO = 0.2
EPS = 1e-06
HALF_LOG2E = 0.5 * math.log2(math.e)
F32 = jnp.float32
VM = pl.BlockSpec(memory_space=pltpu.VMEM)
TR = 16


def iota(shape, dim):
    return lax.broadcasted_iota(jnp.int32, shape, dim)


def position():
    nl, ns = lax.axis_size("light"), lax.axis_size("strip")
    li, si = lax.axis_index("light"), lax.axis_index("strip")
    return li, si, si * nl + li, nl * ns


def exchange_index(place):
    nl, ns = lax.axis_size("light"), lax.axis_size("strip")
    return lax.rem(place, nl) * ns + lax.div(place, nl)


def call(body, out, scratch=(), vmem=40 << 20, **more):
    return pl.pallas_call(
        body,
        out_shape=out,
        scratch_shapes=list(scratch),
        compiler_params=pltpu.CompilerParams(vmem_limit_bytes=vmem),
        **more,
    )


UNDER = 16


def block_rows(lights, rows, k):
    return lights * rows + UNDER + 2 * lights + (2 * lights if k == 1 else 0)


def cut_body(nl, obs_ref, table_ref, depth_ref, albedo_ref, valid_ref, *rest):
    blocks, (tile_ref, surf_ref, sr_ref, end_ref) = rest[:nl], rest[nl : nl + 4]
    table, near, mask, eh_ref, sems, extra = rest[nl + 4 :]
    lights, rows, cols = obs_ref.shape
    w = cols // nl
    li = lax.axis_index("light")

    def columns(q):
        return pl.ds(pl.multiple_of(q * w, w), w)

    order = (2, 3, 1, 0)
    copies = {}
    for k in order:
        for l in range(lights):
            copies[k, l] = pltpu.make_async_copy(
                obs_ref.at[l, :, columns(li ^ k)], blocks[k].at[pl.ds(l * rows, rows)], sems.at[k * lights + l]
            )
            copies[k, l].start()
    fetch = pltpu.make_async_copy(table_ref, table, extra.at[0])
    fetch.start()
    right = lax.rem(li, 2) == 0
    sides = (jnp.maximum(li - 1, 0), li, jnp.minimum(li + 1, nl - 1), jnp.where(right, nl - 1, 0))
    edges = []
    for f, (source, target) in enumerate(((depth_ref, near), (albedo_ref, near), (valid_ref, mask))):
        for side, q in enumerate(sides):
            slot = target.at[side] if f == 2 else target.at[f, side]
            edges.append(pltpu.make_async_copy(source.at[:, columns(q)], slot, extra.at[1 + 4 * f + side]))
            edges[-1].start()
    fetch.wait()
    entries = table[...]
    high = lax.shift_right_logical(entries, 5)
    both = jnp.concatenate([high, entries - high * 32], axis=0).astype(F32)
    wide = jnp.concatenate([both, jnp.zeros((8, w - lights), F32)], axis=1)
    under = jnp.concatenate([wide, jnp.zeros((UNDER - 8, w), F32)], axis=0).astype(jnp.bfloat16)
    for k in range(nl):
        blocks[k][pl.ds(lights * rows, UNDER), :] = under
    eh_ref[...] = jnp.zeros_like(eh_ref)
    at, col = iota((8, w), 0), iota((8, w), 1)
    pick = (((at == 0) & (col == 0)) | ((at == 1) & (col == w - 1))).astype(jnp.bfloat16)
    for k in order:
        q = li ^ k
        for l in range(lights):
            copies[k, l].wait()
            e = lax.dot_general(
                pick,
                blocks[k][pl.ds(l * rows, rows), :],
                (((1,), (1,)), ((), ())),
                preferred_element_type=F32,
            )
            eh_ref[q, lights + l : lights + l + 1, :] = e[0:1]
            eh_ref[q + 2, l : l + 1, :] = e[1:2]
    ends = jnp.concatenate([eh_ref[nl + 1, 0:lights, :], eh_ref[0, lights:, :]], axis=0)
    end_ref[...] = ends
    halo = pl.ds(lights * rows + UNDER, 2 * lights)
    for k in range(nl):
        blocks[k][halo, :] = eh_ref[(li ^ k) + 1].astype(jnp.bfloat16)
    blocks[1][pl.ds(lights * rows + UNDER + 2 * lights, 2 * lights), :] = ends.astype(jnp.bfloat16)
    for copy in edges:
        copy.wait()
    lane = iota((rows, w), 1)
    surf_ref[...] = jnp.zeros_like(surf_ref)
    sr_ref[...] = jnp.zeros_like(sr_ref)
    for f in range(3):
        before, own, after, edge = (mask[s].astype(F32) if f == 2 else near[f, s] for s in range(4))
        tile_ref[f] = own
        inner = jnp.transpose(own)
        outer = jnp.transpose(jnp.where(lane < w // 2, after, before))
        edge = jnp.transpose(edge)
        low = jnp.where(li == 0, 0.0, outer[w - 2 : w])
        high = jnp.where(li == nl - 1, 0.0, outer[0:2])
        if f == 0:
            sr_ref[0:2, :] = low
            sr_ref[2:3, :] = inner[0:1]
            sr_ref[3:4, :] = inner[w - 1 : w]
            sr_ref[4:6, :] = high
            surf_ref[0:2, :] = jnp.where(right, edge[w - 2 : w], edge[0:2])
        else:
            at = 4 + 2 * f
            sr_ref[at : at + 1, :] = low[1:2]
            sr_ref[at + 1 : at + 2, :] = high[0:1]
            surf_ref[1 + f : 2 + f, :] = jnp.where(right, edge[w - 1 : w], edge[0:1])


def join_body(block_ref, end_ref, surf_ref, out_ref):
    n = end_ref.shape[0] // 2
    other = block_ref[pl.ds(block_ref.shape[0] - 2 * n, 2 * n), :].astype(F32)
    right = lax.rem(lax.axis_index("light"), 2) == 0
    out_ref[0:n, :] = jnp.where(right, end_ref[0:n, :], end_ref[n:, :])
    out_ref[n : 2 * n, :] = jnp.where(right, other[0:n], other[n:])
    out_ref[2 * n :, :] = surf_ref[...]


def decode(table):
    return (
        table[:, 0:1] / 500.0 - 1.0,
        table[:, 1:2] / 500.0 - 1.0,
        1.0 + table[:, 2:3] / 1000.0,
        0.5 + table[:, 3:4] / 1000.0,
    )


def decode_rows(table):
    return (
        table[0:1] / 500.0 - 1.0,
        table[1:2] / 500.0 - 1.0,
        1.0 + table[2:3] / 1000.0,
        0.5 + table[3:4] / 1000.0,
    )


def columns_from(left, right, shape):
    rows, w = shape
    at = iota((w, rows), 0)
    return jnp.transpose(jnp.where(at == 0, left, jnp.where(at == w - 1, right, 0.0)))


def shifts_rows(x):
    r = iota(x.shape, 0)
    n = x.shape[0]
    above = jnp.where(r == 0, 0.0, pltpu.roll(x, 1, 0))
    below = jnp.where(r == n - 1, 0.0, pltpu.roll(x, n - 1, 0))
    return above, below


def shifts_cols(x, ends):
    c = iota(x.shape, 1)
    n = x.shape[1]
    before = jnp.where(c == 0, ends, pltpu.roll(x, 1, 1))
    after = jnp.where(c == n - 1, ends, pltpu.roll(x, n - 1, 1))
    return before, after


def fill_context(ctx_ref, surface, albedo, left, right):
    ends = columns_from(left, right, surface.shape)
    before, after = shifts_cols(surface, ends)
    above, below = shifts_rows(surface)
    sx = 0.5 * (after - before)
    sy = 0.5 * (below - above)
    ctx_ref[0] = surface
    ctx_ref[1] = sx
    ctx_ref[2] = sy
    ctx_ref[3] = albedo * lax.rsqrt(1.0 + sx * sx + sy * sy)


def lights_of(block_ref, rows):
    return block_ref.shape[0] // rows


def table_rows(block_ref, n, rows):
    under = block_ref[pl.ds(n * rows, UNDER), :].astype(F32)
    return under[0:4] * 32.0 + under[4:8]


def fill_params(pb_ref, base, block_ref, n, rows, w, place, total):
    lx, ly, lz, le = decode_rows(table_rows(block_ref, n, rows))
    col = iota((8, w), 1) + place * w
    px = (col.astype(F32) + 0.5) / total - 0.5
    for j in range(n):
        dx = jnp.broadcast_to(lx[:, j : j + 1], (8, w)) - px
        pb_ref[base + j, 0] = dx
        pb_ref[base + j, 1] = dx * dx
        pb_ref[base + j, 2] = jnp.broadcast_to(ly[:, j : j + 1], (8, w))
        pb_ref[base + j, 3] = jnp.broadcast_to(lz[:, j : j + 1], (8, w))
        pb_ref[base + j, 4] = jnp.broadcast_to(le[:, j : j + 1], (8, w))


def accumulate(state, tile, py, obs, pb_ref, base):
    surface, sx, sy, scaled = tile
    kept = []
    least = None
    for j in range(len(obs)):
        dx, dx2 = pb_ref[base + j, 0], pb_ref[base + j, 1]
        dy = pb_ref[base + j, 2] - py
        dz = pb_ref[base + j, 3] - surface
        dist = (dx2 + dy * dy) + dz * dz
        facing = dz - (sx * dx + sy * dy)
        r = lax.rsqrt(dist)
        r2 = r * r
        g = (r2 * r) * pb_ref[base + j, 4]
        residual = scaled * (g * facing) - obs[j]
        square = residual * residual
        least = square if least is None else jnp.minimum(least, square)
        kept.append((square, residual * g, facing, dz * r2, dx, dy))
    if state is not None:
        before = state[0]
        least = jnp.minimum(least, before)
    sums = None
    for square, q, facing, drop, dx, dy in kept:
        w = jnp.exp2((least - square) * HALF_LOG2E)
        p = w * q
        pf = p * facing
        terms = (w, p, p * dx, p * dy, pf, pf * drop)
        sums = terms if sums is None else tuple(a + b for a, b in zip(sums, terms))
    if state is not None:
        fade = jnp.exp2((least - before) * HALF_LOG2E)
        sums = tuple(a * fade + b for a, b in zip(state[1:], sums))
    return (least,) + sums


def sweep(ctx_ref, pb_ref, obs_refs, bases, total, load, store):
    rows, w = ctx_ref.shape[1:]
    lights = lights_of(obs_refs[0], rows)
    split = (TR // 8, 8, w)

    def step(i, carry):
        at = pl.ds(pl.multiple_of(i * TR, TR), TR)
        tile = tuple(ctx_ref[f, at, :].reshape(split) for f in range(4))
        row = iota(split, 0) * 8 + iota(split, 1) + i * TR
        py = (row.astype(F32) + (0.5 - rows / 2.0)) / total
        state = load(at)
        for obs_ref, base in zip(obs_refs, bases):
            obs = [
                obs_ref[pl.ds(pl.multiple_of(j * rows + i * TR, TR), TR), :].astype(F32).reshape(split)
                for j in range(lights)
            ]
            state = accumulate(state, tile, py, obs, pb_ref, base)
        store(at, state)
        return carry

    lax.fori_loop(0, rows // TR, step, 0)


def state_load(state_ref, w):
    return lambda at: tuple(state_ref[f, at, :].reshape(TR // 8, 8, w) for f in range(7))


def state_store(state_ref, w):
    def store(at, state):
        for f in range(7):
            state_ref[f, at, :] = state[f].reshape(TR, w)

    return store


def halo_slope(column, side, pack_ref, srow_ref, rows, total):
    obs = pack_ref[side]
    lx, ly, lz, le = decode(pack_ref[2])
    outer, inner = (0, 2) if side == 0 else (5, 3)
    here = 1 if side == 0 else 4
    surface = srow_ref[here : here + 1, :]
    toward = srow_ref[inner : inner + 1, :] - srow_ref[outer : outer + 1, :]
    sx = 0.5 * toward if side == 0 else -0.5 * toward
    lane = iota((8, rows), 1)
    wide = jnp.broadcast_to(surface, (8, rows))
    above = jnp.where(lane == 0, 0.0, pltpu.roll(wide, 1, 1))
    below = jnp.where(lane == rows - 1, 0.0, pltpu.roll(wide, rows - 1, 1))
    sy = (0.5 * (below - above))[0:1]
    albedo = srow_ref[6 + side : 7 + side, :]
    valid = srow_ref[8 + side : 9 + side, :]
    px = (column.astype(F32) + 0.5) / total - 0.5
    py = (iota((1, rows), 1).astype(F32) + (0.5 - rows / 2.0)) / total
    rn = lax.rsqrt(1.0 + sx * sx + sy * sy)
    dx = jnp.broadcast_to(lx - px, obs.shape)
    dy = ly - py
    dz = lz - surface
    dist = dx * dx + dy * dy + dz * dz
    facing = dz - (sx * dx + sy * dy)
    r = lax.rsqrt(dist)
    g = (r * r) * r * le
    residual = (albedo * rn) * (g * facing) - obs
    square = residual * residual
    least = jnp.min(square, axis=0, keepdims=True)
    w = jnp.exp2((least - square) * HALF_LOG2E)
    p = w * residual * g
    total_w = jnp.sum(w, axis=0, keepdims=True)
    px_sum = jnp.sum(p * dx, axis=0, keepdims=True)
    pf_sum = jnp.sum(p * facing, axis=0, keepdims=True)
    return -(valid * albedo * rn / total_w) * (px_sum + (sx * rn * rn) * pf_sum)


def gradients(state_ref, ctx_ref, albedo, valid, slope_low, slope_high):
    sx, sy = ctx_ref[1], ctx_ref[2]
    rn = lax.rsqrt(1.0 + sx * sx + sy * sy)
    inverse = valid * rn / state_ref[1]
    factor = inverse * albedo
    pf = state_ref[5]
    rn2pf = rn * rn * pf
    grad_albedo = inverse * pf
    direct = factor * (3.0 * state_ref[6] - state_ref[2])
    grad_x = -factor * (state_ref[3] + sx * rn2pf)
    grad_y = -factor * (state_ref[4] + sy * rn2pf)
    before, after = shifts_cols(grad_x, columns_from(slope_low, slope_high, grad_x.shape))
    above, below = shifts_rows(grad_y)
    return direct + 0.5 * (before - after) + 0.5 * (above - below), grad_albedo


def partial_sums(depth, albedo):
    n = depth.shape[1]
    d = jnp.sum(depth * depth, axis=0, keepdims=True)
    a = jnp.sum(albedo * albedo, axis=0, keepdims=True)
    d = jnp.broadcast_to(d, (8, n))
    a = jnp.broadcast_to(a, (8, n))
    d = d + pltpu.roll(d, n // 2, 1)
    a = a + pltpu.roll(a, n // 2, 1)
    return jnp.where(iota((8, n), 1) < n // 2, d, a)[0:1]


def inverse_scales(recv_ref, row, count):
    rows = recv_ref[:, row, :]
    n = rows.shape[1]
    lane = iota(rows.shape, 1)
    d = jnp.sum(jnp.where(lane < n // 2, rows, 0.0), keepdims=True)
    a = jnp.sum(jnp.where(lane < n // 2, 0.0, rows), keepdims=True)
    return lax.rsqrt(d / count + EPS), lax.rsqrt(a / count + EPS)


def first_body(nl, tile_ref, sr_ref, strip_ref, obs0, obs1, ctx_ref, srow_ref, state_ref, pb_ref):
    li, _, place, count = position()
    rows, w = ctx_ref.shape[1:]
    srow_ref[...] = sr_ref[...]
    at = strip_ref.shape[0] - 8

    @pl.when(li == 0)
    def _():
        srow_ref[0:2, :] = strip_ref[at : at + 2, :]
        srow_ref[6:7, :] = strip_ref[at + 2 : at + 3, :]
        srow_ref[8:9, :] = strip_ref[at + 3 : at + 4, :]

    @pl.when(li == nl - 1)
    def _():
        srow_ref[4:6, :] = strip_ref[at : at + 2, :]
        srow_ref[7:8, :] = strip_ref[at + 2 : at + 3, :]
        srow_ref[9:10, :] = strip_ref[at + 3 : at + 4, :]

    fill_context(ctx_ref, tile_ref[0], tile_ref[1], srow_ref[1:2, :], srow_ref[4:5, :])
    total = w * count
    n = lights_of(obs0, rows)
    fill_params(pb_ref, 0, obs0, n, rows, w, place, total)
    fill_params(pb_ref, n, obs1, n, rows, w, place, total)
    sweep(ctx_ref, pb_ref, (obs0, obs1), (0, n), total, lambda at: None, state_store(state_ref, w))


def more_body(ctx_ref, in_ref, obs, state_ref, pb_ref):
    _, _, place, count = position()
    rows, w = ctx_ref.shape[1:]
    total = w * count
    fill_params(pb_ref, 0, obs, lights_of(obs, rows), rows, w, place, total)
    sweep(ctx_ref, pb_ref, (obs,), (0,), total, state_load(in_ref, w), state_store(state_ref, w))


def finish(state_ref, ctx_ref, albedo, valid, pack_ref, srow_ref, grad_ref, edge_ref, pay_ref):
    _, _, place, count = position()
    rows, w = ctx_ref.shape[1:]
    total = w * count
    low = halo_slope(place * w - 1, 0, pack_ref, srow_ref, rows, total)
    high = halo_slope(place * w + w, 1, pack_ref, srow_ref, rows, total)
    depth, grad_albedo = gradients(state_ref, ctx_ref, albedo, valid, low, high)
    sums = partial_sums(depth, grad_albedo)
    if edge_ref is None:
        pay_ref[...] = jnp.broadcast_to(sums[None], pay_ref.shape)
        return depth, grad_albedo
    grad_ref[0] = depth
    grad_ref[1] = grad_albedo
    dt = jnp.transpose(depth)
    at = jnp.transpose(grad_albedo)
    edge_ref[0:1, :] = dt[0:1]
    edge_ref[1:2, :] = dt[w - 1 : w]
    pay_ref[:, 0:2, :] = jnp.broadcast_to(dt[0:2][None], (count, 2, rows))
    pay_ref[:, 2:3, :] = jnp.broadcast_to(at[0:1][None], (count, 1, rows))
    pay_ref[:, 3:4, :] = jnp.broadcast_to(sums[None], (count, 1, w))

    @pl.when(place < count - 1)
    def _():
        to = exchange_index(place + 1)
        pay_ref[to, 0:2, :] = dt[w - 2 : w]
        pay_ref[to, 2:3, :] = at[w - 1 : w]

    return depth, grad_albedo


def fill_pack(nl, pack_ref, block_refs, direct_ref, relayed_ref, rows, w):
    li = lax.axis_index("light")
    n = lights_of(block_refs[0], rows)
    table = jnp.zeros((4, w), F32)
    for k in range(nl):
        halo = block_refs[k][pl.ds(n * rows + UNDER, 2 * n), :].astype(F32)
        beyond = (relayed_ref if k < 2 else direct_ref)[(k % 2) * n : (k % 2 + 1) * n, :]
        pack_ref[0, k * n : (k + 1) * n, :] = jnp.where(li == 0, beyond, halo[0:n])
        pack_ref[1, k * n : (k + 1) * n, :] = jnp.where(li == nl - 1, beyond, halo[n:])
        entries = jnp.concatenate([table_rows(block_refs[k], n, rows)] * 2, axis=0)
        table = table + (pltpu.roll(entries, k * n, 1) if k else entries)[0:4]
    tall = jnp.concatenate([table, jnp.zeros((w - 4, w), F32)], axis=0)
    pack_ref[2] = jnp.transpose(tall)[0 : nl * n]


def last_body(nl, ctx_ref, tile_ref, state_ref, srow_ref, direct_ref, relayed_ref, *rest):
    block_refs, (grad_ref, edge_ref, pay_ref, pack_ref) = rest[:nl], rest[nl:]
    rows, w = ctx_ref.shape[1:]
    fill_pack(nl, pack_ref, block_refs, direct_ref, relayed_ref, rows, w)
    edge_ref[...] = jnp.zeros_like(edge_ref)
    finish(state_ref, ctx_ref, tile_ref[1], tile_ref[2], pack_ref, srow_ref, grad_ref, edge_ref, pay_ref)


def second_body(nl, recv_ref, grad_ref, edge_ref, tile_ref, srow0_ref, pack_ref, *rest):
    obs_refs = rest[:nl]
    out_ref, pay_ref, ctx_ref, state_ref, pb_ref, srow_ref = rest[nl:]
    _, _, place, count = position()
    rows, w = ctx_ref.shape[1:]
    total = w * count
    inv_depth, inv_albedo = inverse_scales(recv_ref, 3, float(rows * total))
    surface = tile_ref[0] - STEP_DEPTH * jnp.tanh(grad_ref[0] * inv_depth)
    albedo = tile_ref[1] - STEP_ALBEDO * jnp.tanh(grad_ref[1] * inv_albedo)
    out_ref[0] = surface
    out_ref[1] = albedo
    srow_ref[...] = jnp.zeros_like(srow_ref)
    srow_ref[2:4, :] = edge_ref[0:2, :]

    @pl.when(place > 0)
    def _():
        frm = exchange_index(jnp.maximum(place - 1, 0))
        srow_ref[0:2, :] = recv_ref[frm, 0:2, :]
        srow_ref[6:7, :] = recv_ref[frm, 2:3, :]

    @pl.when(place < count - 1)
    def _():
        frm = exchange_index(jnp.minimum(place + 1, count - 1))
        srow_ref[4:6, :] = recv_ref[frm, 0:2, :]
        srow_ref[7:8, :] = recv_ref[frm, 2:3, :]

    changes = srow_ref[0:8, :]
    kind = iota(changes.shape, 0) < 6
    changes = jnp.where(
        kind, STEP_DEPTH * jnp.tanh(changes * inv_depth), STEP_ALBEDO * jnp.tanh(changes * inv_albedo)
    )
    srow_ref[0:8, :] = srow0_ref[0:8, :] - changes
    srow_ref[8:16, :] = srow0_ref[8:16, :]
    fill_context(ctx_ref, surface, albedo, srow_ref[1:2, :], srow_ref[4:5, :])
    n = lights_of(obs_refs[0], rows)
    bases = tuple(k * n for k in range(nl))
    for k in range(nl):
        fill_params(pb_ref, bases[k], obs_refs[k], n, rows, w, place, total)
    sweep(ctx_ref, pb_ref, obs_refs, bases, total, lambda at: None, state_store(state_ref, w))
    depth, grad_albedo = finish(
        state_ref, ctx_ref, albedo, tile_ref[2], pack_ref, srow_ref, None, None, pay_ref
    )
    out_ref[2] = depth
    out_ref[3] = grad_albedo


def final_body(nl, recv_ref, *rest):
    parts, (depth_ref, albedo_ref) = rest[:nl], rest[nl:]
    li, _, _, count = position()
    rows, w = parts[0].shape[1:]
    inv_depth, inv_albedo = inverse_scales(recv_ref, 0, float(rows * w * count))
    for k in range(nl):
        at = pl.ds(pl.multiple_of((li ^ k) * w, w), w)
        depth_ref[:, at] = parts[k][0] - STEP_DEPTH * jnp.tanh(parts[k][2] * inv_depth)
        albedo_ref[:, at] = parts[k][1] - STEP_ALBEDO * jnp.tanh(parts[k][3] * inv_albedo)


def shape(*dims, dtype=F32):
    return jax.ShapeDtypeStruct(dims, dtype)


def program(depth_start, albedo_start, observations, light_table, valid_mask):
    nl, ns = lax.axis_size("light"), lax.axis_size("strip")
    nd = nl * ns
    lights, rows, cols = observations.shape
    w = cols // nl

    def swap(x, k):
        return lax.ppermute(x, "light", [(i, i ^ k) for i in range(nl)])

    hbm = pl.BlockSpec(memory_space=pltpu.HBM)
    field = (rows, w)
    whole = (observations, light_table.T, depth_start, albedo_start, valid_mask)
    *blocks, tile, surf, sr, end = call(
        functools.partial(cut_body, nl),
        tuple(shape(block_rows(lights, rows, k), w, dtype=jnp.bfloat16) for k in range(nl))
        + (shape(3, *field), shape(8, rows), shape(16, rows), shape(2 * lights, rows)),
        [
            pltpu.VMEM((4, lights), jnp.int32),
            pltpu.VMEM((2, 4, *field), F32),
            pltpu.VMEM((4, *field), jnp.int32),
            pltpu.VMEM((nl + 2, 2 * lights, rows), F32),
            pltpu.SemaphoreType.DMA((nl * lights,)),
            pltpu.SemaphoreType.DMA((13,)),
        ],
        in_specs=[hbm] * 5,
    )(*(pltpu.with_memory_space_constraint(x, pltpu.HBM) for x in whole))
    obs2 = swap(blocks[2], 2)
    obs3 = swap(blocks[3], 3)
    obs1 = swap(blocks[1], 1)
    obs0 = blocks[0]
    strip = call(join_body, shape(2 * lights + 8, rows))(obs1, end, surf)
    pairs = []
    for i in range(ns - 1):
        pairs += [(2 * ns + i, i + 1), (i, ns + i + 1), (ns + i + 1, 3 * ns + i), (3 * ns + i + 1, 2 * ns + i)]
    direct = lax.ppermute(strip, AXES, pairs)
    relayed = swap(direct, 1)

    pb = pltpu.VMEM((2 * lights, 5, 8, w), F32)
    ctx, srow, state = call(
        functools.partial(first_body, nl), (shape(4, *field), shape(16, rows), shape(7, *field)), [pb]
    )(tile, sr, direct, obs0, obs1)
    state = call(more_body, shape(7, *field), [pb])(ctx, state, obs2)
    state = call(more_body, shape(7, *field), [pb])(ctx, state, obs3)
    grad, edge, pay, pack = call(
        functools.partial(last_body, nl),
        (shape(2, *field), shape(8, rows), shape(nd, 4, rows), shape(3, nl * lights, rows)),
    )(ctx, tile, state, srow, direct, relayed, obs0, obs1, obs2, obs3)
    recv = lax.all_to_all(pay, AXES, 0, 0, tiled=True)
    own, pay = call(
        functools.partial(second_body, nl),
        (shape(4, *field), shape(nd, 1, rows)),
        [
            pltpu.VMEM((4, *field), F32),
            pltpu.VMEM((7, *field), F32),
            pltpu.VMEM((nl * lights, 5, 8, w), F32),
            pltpu.VMEM((16, rows), F32),
        ],
    )(recv, grad, edge, tile, srow, pack, obs0, obs1, obs2, obs3)
    part2 = swap(own, 2)
    part1 = swap(own, 1)
    recv = lax.all_to_all(pay, AXES, 0, 0, tiled=True)
    recv, part2 = lax.optimization_barrier((recv, part2))
    part3 = swap(part2, 1)
    return tuple(
        call(functools.partial(final_body, nl), (shape(rows, cols), shape(rows, cols)))(recv, own, part1, part2, part3)
    )


def solution(mesh):
    in_specs = (
        P(None, "strip"),
        P(None, "strip"),
        P("light", None, "strip"),
        P("light", None),
        P(None, "strip"),
    )
    out_specs = (P(None, "strip"), P(None, "strip"))
    return jax.shard_map(program, mesh=mesh, in_specs=in_specs, out_specs=out_specs, check_vma=False)
```

```python
import functools
import math

import jax
import jax.numpy as jnp
from jax import lax
from jax.experimental import pallas as pl
from jax.experimental.pallas import tpu as pltpu
from jax.sharding import PartitionSpec as P


AXES = ("light", "strip")
STEP_DEPTH = 0.1
STEP_ALBEDO = 0.2
EPS = 1e-06
HALF_LOG2E = 0.5 * math.log2(math.e)
F32 = jnp.float32
VM = pl.BlockSpec(memory_space=pltpu.VMEM)
TR = 16


def iota(shape, dim):
    return lax.broadcasted_iota(jnp.int32, shape, dim)


def position():
    nl, ns = lax.axis_size("light"), lax.axis_size("strip")
    li, si = lax.axis_index("light"), lax.axis_index("strip")
    return li, si, si * nl + li, nl * ns


def exchange_index(place):
    nl, ns = lax.axis_size("light"), lax.axis_size("strip")
    return lax.rem(place, nl) * ns + lax.div(place, nl)


def call(body, out, scratch=(), vmem=40 << 20, **more):
    return pl.pallas_call(
        body,
        out_shape=out,
        scratch_shapes=list(scratch),
        compiler_params=pltpu.CompilerParams(vmem_limit_bytes=vmem),
        **more,
    )


UNDER = 16


def block_rows(lights, rows, k):
    return lights * rows + UNDER + 2 * lights + (2 * lights if k == 1 else 0)


def cut_body(nl, obs_ref, table_ref, *rest):
    blocks, (end_ref, table, eh_ref, sems, extra) = rest[:nl], rest[nl:]
    lights, rows, cols = obs_ref.shape
    w = cols // nl
    li = lax.axis_index("light")
    copies = []
    for k in (2, 3, 1, 0):
        for l in range(lights):
            at = pl.ds(pl.multiple_of((li ^ k) * w, w), w)
            copies.append(
                pltpu.make_async_copy(
                    obs_ref.at[l, :, at], blocks[k].at[pl.ds(l * rows, rows)], sems.at[k * lights + l]
                )
            )
            copies[-1].start()
    fetch = pltpu.make_async_copy(table_ref, table, extra.at[0])
    fetch.start()
    eh_ref[...] = jnp.zeros_like(eh_ref)
    at, col = iota((8, w), 0), iota((8, w), 1)
    pick = (((at == 0) & (col == 0)) | ((at == 1) & (col == w - 1))).astype(jnp.bfloat16)
    fetch.wait()
    entries = table[...]
    high = lax.shift_right_logical(entries, 5)
    both = jnp.concatenate([high, entries - high * 32], axis=0).astype(F32)
    wide = jnp.concatenate([both, jnp.zeros((8, w - lights), F32)], axis=1)
    under = jnp.concatenate([wide, jnp.zeros((UNDER - 8, w), F32)], axis=0).astype(jnp.bfloat16)
    for k in range(nl):
        blocks[k][pl.ds(lights * rows, UNDER), :] = under
    for copy in copies:
        copy.wait()
    for k in range(nl):
        q = li ^ k
        for l in range(lights):
            e = lax.dot_general(
                pick,
                blocks[k][pl.ds(l * rows, rows), :],
                (((1,), (1,)), ((), ())),
                preferred_element_type=F32,
            )
            eh_ref[q, lights + l : lights + l + 1, :] = e[0:1]
            eh_ref[q + 2, l : l + 1, :] = e[1:2]
    ends = jnp.concatenate([eh_ref[nl + 1, 0:lights, :], eh_ref[0, lights:, :]], axis=0)
    end_ref[...] = ends
    halo = pl.ds(lights * rows + UNDER, 2 * lights)
    for k in range(nl):
        blocks[k][halo, :] = eh_ref[(li ^ k) + 1].astype(jnp.bfloat16)
    blocks[1][pl.ds(lights * rows + UNDER + 2 * lights, 2 * lights), :] = ends.astype(jnp.bfloat16)


def join_body(nl, depth_ref, albedo_ref, valid_ref, block_ref, end_ref, tile_ref, sr_ref, out_ref):
    rows, w = tile_ref.shape[1:]
    n = end_ref.shape[0] // 2
    li = lax.axis_index("light")
    right = lax.rem(li, 2) == 0
    other = block_ref[pl.ds(block_ref.shape[0] - 2 * n, 2 * n), :].astype(F32)
    out_ref[0:n, :] = jnp.where(right, end_ref[0:n, :], end_ref[n:, :])
    out_ref[n : 2 * n, :] = jnp.where(right, other[0:n], other[n:])
    out_ref[2 * n :, :] = jnp.zeros((8, rows), F32)
    sr_ref[...] = jnp.zeros_like(sr_ref)
    lane = iota((rows, w), 1)

    def columns(ref, q):
        return ref[:, pl.ds(pl.multiple_of(q * w, w), w)].astype(F32)

    for f, ref in enumerate((depth_ref, albedo_ref, valid_ref)):
        own = columns(ref, li)
        before = columns(ref, jnp.maximum(li - 1, 0))
        after = columns(ref, jnp.minimum(li + 1, nl - 1))
        tile_ref[f] = own
        inner = jnp.transpose(own)
        outer = jnp.transpose(jnp.where(lane < w // 2, after, before))
        edge = jnp.transpose(columns(ref, jnp.where(right, nl - 1, 0)))
        low = jnp.where(li == 0, 0.0, outer[w - 2 : w])
        high = jnp.where(li == nl - 1, 0.0, outer[0:2])
        if f == 0:
            sr_ref[0:2, :] = low
            sr_ref[2:3, :] = inner[0:1]
            sr_ref[3:4, :] = inner[w - 1 : w]
            sr_ref[4:6, :] = high
            out_ref[2 * n : 2 * n + 2, :] = jnp.where(right, edge[w - 2 : w], edge[0:2])
        else:
            at = 4 + 2 * f
            sr_ref[at : at + 1, :] = low[1:2]
            sr_ref[at + 1 : at + 2, :] = high[0:1]
            at = 2 * n + 1 + f
            out_ref[at : at + 1, :] = jnp.where(right, edge[w - 1 : w], edge[0:1])


def decode(table):
    return (
        table[:, 0:1] / 500.0 - 1.0,
        table[:, 1:2] / 500.0 - 1.0,
        1.0 + table[:, 2:3] / 1000.0,
        0.5 + table[:, 3:4] / 1000.0,
    )


def decode_rows(table):
    return (
        table[0:1] / 500.0 - 1.0,
        table[1:2] / 500.0 - 1.0,
        1.0 + table[2:3] / 1000.0,
        0.5 + table[3:4] / 1000.0,
    )


def columns_from(left, right, shape):
    rows, w = shape
    at = iota((w, rows), 0)
    return jnp.transpose(jnp.where(at == 0, left, jnp.where(at == w - 1, right, 0.0)))


def shifts_rows(x):
    r = iota(x.shape, 0)
    n = x.shape[0]
    above = jnp.where(r == 0, 0.0, pltpu.roll(x, 1, 0))
    below = jnp.where(r == n - 1, 0.0, pltpu.roll(x, n - 1, 0))
    return above, below


def shifts_cols(x, ends):
    c = iota(x.shape, 1)
    n = x.shape[1]
    before = jnp.where(c == 0, ends, pltpu.roll(x, 1, 1))
    after = jnp.where(c == n - 1, ends, pltpu.roll(x, n - 1, 1))
    return before, after


def fill_context(ctx_ref, surface, albedo, left, right):
    ends = columns_from(left, right, surface.shape)
    before, after = shifts_cols(surface, ends)
    above, below = shifts_rows(surface)
    sx = 0.5 * (after - before)
    sy = 0.5 * (below - above)
    ctx_ref[0] = surface
    ctx_ref[1] = sx
    ctx_ref[2] = sy
    ctx_ref[3] = albedo * lax.rsqrt(1.0 + sx * sx + sy * sy)


def lights_of(block_ref, rows):
    return block_ref.shape[0] // rows


def table_rows(block_ref, n, rows):
    under = block_ref[pl.ds(n * rows, UNDER), :].astype(F32)
    return under[0:4] * 32.0 + under[4:8]


def fill_params(pb_ref, base, block_ref, n, rows, w, place, total):
    lx, ly, lz, le = decode_rows(table_rows(block_ref, n, rows))
    col = iota((8, w), 1) + place * w
    px = (col.astype(F32) + 0.5) / total - 0.5
    for j in range(n):
        dx = jnp.broadcast_to(lx[:, j : j + 1], (8, w)) - px
        pb_ref[base + j, 0] = dx
        pb_ref[base + j, 1] = dx * dx
        pb_ref[base + j, 2] = jnp.broadcast_to(ly[:, j : j + 1], (8, w))
        pb_ref[base + j, 3] = jnp.broadcast_to(lz[:, j : j + 1], (8, w))
        pb_ref[base + j, 4] = jnp.broadcast_to(le[:, j : j + 1], (8, w))


def accumulate(state, tile, py, obs, pb_ref, base):
    surface, sx, sy, scaled = tile
    kept = []
    least = None
    for j in range(len(obs)):
        dx, dx2 = pb_ref[base + j, 0], pb_ref[base + j, 1]
        dy = pb_ref[base + j, 2] - py
        dz = pb_ref[base + j, 3] - surface
        dist = (dx2 + dy * dy) + dz * dz
        facing = dz - (sx * dx + sy * dy)
        r = lax.rsqrt(dist)
        r2 = r * r
        g = (r2 * r) * pb_ref[base + j, 4]
        residual = scaled * (g * facing) - obs[j]
        square = residual * residual
        least = square if least is None else jnp.minimum(least, square)
        kept.append((square, residual * g, facing, dz * r2, dx, dy))
    if state is not None:
        before = state[0]
        least = jnp.minimum(least, before)
    sums = None
    for square, q, facing, drop, dx, dy in kept:
        w = jnp.exp2((least - square) * HALF_LOG2E)
        p = w * q
        pf = p * facing
        terms = (w, p, p * dx, p * dy, pf, pf * drop)
        sums = terms if sums is None else tuple(a + b for a, b in zip(sums, terms))
    if state is not None:
        fade = jnp.exp2((least - before) * HALF_LOG2E)
        sums = tuple(a * fade + b for a, b in zip(state[1:], sums))
    return (least,) + sums


def sweep(ctx_ref, pb_ref, obs_refs, bases, total, load, store):
    rows, w = ctx_ref.shape[1:]
    lights = lights_of(obs_refs[0], rows)
    split = (TR // 8, 8, w)

    def step(i, carry):
        at = pl.ds(pl.multiple_of(i * TR, TR), TR)
        tile = tuple(ctx_ref[f, at, :].reshape(split) for f in range(4))
        row = iota(split, 0) * 8 + iota(split, 1) + i * TR
        py = (row.astype(F32) + (0.5 - rows / 2.0)) / total
        state = load(at)
        for obs_ref, base in zip(obs_refs, bases):
            obs = [
                obs_ref[pl.ds(pl.multiple_of(j * rows + i * TR, TR), TR), :].astype(F32).reshape(split)
                for j in range(lights)
            ]
            state = accumulate(state, tile, py, obs, pb_ref, base)
        store(at, state)
        return carry

    lax.fori_loop(0, rows // TR, step, 0)


def state_load(state_ref, w):
    return lambda at: tuple(state_ref[f, at, :].reshape(TR // 8, 8, w) for f in range(7))


def state_store(state_ref, w):
    def store(at, state):
        for f in range(7):
            state_ref[f, at, :] = state[f].reshape(TR, w)

    return store


def halo_slope(column, side, pack_ref, srow_ref, rows, total):
    obs = pack_ref[side]
    lx, ly, lz, le = decode(pack_ref[2])
    outer, inner = (0, 2) if side == 0 else (5, 3)
    here = 1 if side == 0 else 4
    surface = srow_ref[here : here + 1, :]
    toward = srow_ref[inner : inner + 1, :] - srow_ref[outer : outer + 1, :]
    sx = 0.5 * toward if side == 0 else -0.5 * toward
    lane = iota((8, rows), 1)
    wide = jnp.broadcast_to(surface, (8, rows))
    above = jnp.where(lane == 0, 0.0, pltpu.roll(wide, 1, 1))
    below = jnp.where(lane == rows - 1, 0.0, pltpu.roll(wide, rows - 1, 1))
    sy = (0.5 * (below - above))[0:1]
    albedo = srow_ref[6 + side : 7 + side, :]
    valid = srow_ref[8 + side : 9 + side, :]
    px = (column.astype(F32) + 0.5) / total - 0.5
    py = (iota((1, rows), 1).astype(F32) + (0.5 - rows / 2.0)) / total
    rn = lax.rsqrt(1.0 + sx * sx + sy * sy)
    dx = jnp.broadcast_to(lx - px, obs.shape)
    dy = ly - py
    dz = lz - surface
    dist = dx * dx + dy * dy + dz * dz
    facing = dz - (sx * dx + sy * dy)
    r = lax.rsqrt(dist)
    g = (r * r) * r * le
    residual = (albedo * rn) * (g * facing) - obs
    square = residual * residual
    least = jnp.min(square, axis=0, keepdims=True)
    w = jnp.exp2((least - square) * HALF_LOG2E)
    p = w * residual * g
    total_w = jnp.sum(w, axis=0, keepdims=True)
    px_sum = jnp.sum(p * dx, axis=0, keepdims=True)
    pf_sum = jnp.sum(p * facing, axis=0, keepdims=True)
    return -(valid * albedo * rn / total_w) * (px_sum + (sx * rn * rn) * pf_sum)


def gradients(state_ref, ctx_ref, albedo, valid, slope_low, slope_high):
    sx, sy = ctx_ref[1], ctx_ref[2]
    rn = lax.rsqrt(1.0 + sx * sx + sy * sy)
    inverse = valid * rn / state_ref[1]
    factor = inverse * albedo
    pf = state_ref[5]
    rn2pf = rn * rn * pf
    grad_albedo = inverse * pf
    direct = factor * (3.0 * state_ref[6] - state_ref[2])
    grad_x = -factor * (state_ref[3] + sx * rn2pf)
    grad_y = -factor * (state_ref[4] + sy * rn2pf)
    before, after = shifts_cols(grad_x, columns_from(slope_low, slope_high, grad_x.shape))
    above, below = shifts_rows(grad_y)
    return direct + 0.5 * (before - after) + 0.5 * (above - below), grad_albedo


def partial_sums(depth, albedo):
    n = depth.shape[1]
    d = jnp.sum(depth * depth, axis=0, keepdims=True)
    a = jnp.sum(albedo * albedo, axis=0, keepdims=True)
    d = jnp.broadcast_to(d, (8, n))
    a = jnp.broadcast_to(a, (8, n))
    d = d + pltpu.roll(d, n // 2, 1)
    a = a + pltpu.roll(a, n // 2, 1)
    return jnp.where(iota((8, n), 1) < n // 2, d, a)[0:1]


def inverse_scales(recv_ref, row, count):
    rows = recv_ref[:, row, :]
    n = rows.shape[1]
    lane = iota(rows.shape, 1)
    d = jnp.sum(jnp.where(lane < n // 2, rows, 0.0), keepdims=True)
    a = jnp.sum(jnp.where(lane < n // 2, 0.0, rows), keepdims=True)
    return lax.rsqrt(d / count + EPS), lax.rsqrt(a / count + EPS)


def first_body(nl, tile_ref, sr_ref, strip_ref, obs0, obs1, ctx_ref, srow_ref, state_ref, pb_ref):
    li, _, place, count = position()
    rows, w = ctx_ref.shape[1:]
    srow_ref[...] = sr_ref[...]
    at = strip_ref.shape[0] - 8

    @pl.when(li == 0)
    def _():
        srow_ref[0:2, :] = strip_ref[at : at + 2, :]
        srow_ref[6:7, :] = strip_ref[at + 2 : at + 3, :]
        srow_ref[8:9, :] = strip_ref[at + 3 : at + 4, :]

    @pl.when(li == nl - 1)
    def _():
        srow_ref[4:6, :] = strip_ref[at : at + 2, :]
        srow_ref[7:8, :] = strip_ref[at + 2 : at + 3, :]
        srow_ref[9:10, :] = strip_ref[at + 3 : at + 4, :]

    fill_context(ctx_ref, tile_ref[0], tile_ref[1], srow_ref[1:2, :], srow_ref[4:5, :])
    total = w * count
    n = lights_of(obs0, rows)
    fill_params(pb_ref, 0, obs0, n, rows, w, place, total)
    fill_params(pb_ref, n, obs1, n, rows, w, place, total)
    sweep(ctx_ref, pb_ref, (obs0, obs1), (0, n), total, lambda at: None, state_store(state_ref, w))


def more_body(ctx_ref, in_ref, obs, state_ref, pb_ref):
    _, _, place, count = position()
    rows, w = ctx_ref.shape[1:]
    total = w * count
    fill_params(pb_ref, 0, obs, lights_of(obs, rows), rows, w, place, total)
    sweep(ctx_ref, pb_ref, (obs,), (0,), total, state_load(in_ref, w), state_store(state_ref, w))


def finish(state_ref, ctx_ref, albedo, valid, pack_ref, srow_ref, grad_ref, edge_ref, pay_ref):
    _, _, place, count = position()
    rows, w = ctx_ref.shape[1:]
    total = w * count
    low = halo_slope(place * w - 1, 0, pack_ref, srow_ref, rows, total)
    high = halo_slope(place * w + w, 1, pack_ref, srow_ref, rows, total)
    depth, grad_albedo = gradients(state_ref, ctx_ref, albedo, valid, low, high)
    sums = partial_sums(depth, grad_albedo)
    if edge_ref is None:
        pay_ref[...] = jnp.broadcast_to(sums[None], pay_ref.shape)
        return depth, grad_albedo
    grad_ref[0] = depth
    grad_ref[1] = grad_albedo
    dt = jnp.transpose(depth)
    at = jnp.transpose(grad_albedo)
    edge_ref[0:1, :] = dt[0:1]
    edge_ref[1:2, :] = dt[w - 1 : w]
    pay_ref[:, 0:2, :] = jnp.broadcast_to(dt[0:2][None], (count, 2, rows))
    pay_ref[:, 2:3, :] = jnp.broadcast_to(at[0:1][None], (count, 1, rows))
    pay_ref[:, 3:4, :] = jnp.broadcast_to(sums[None], (count, 1, w))

    @pl.when(place < count - 1)
    def _():
        to = exchange_index(place + 1)
        pay_ref[to, 0:2, :] = dt[w - 2 : w]
        pay_ref[to, 2:3, :] = at[w - 1 : w]

    return depth, grad_albedo


def fill_pack(nl, pack_ref, block_refs, direct_ref, relayed_ref, rows, w):
    li = lax.axis_index("light")
    n = lights_of(block_refs[0], rows)
    table = jnp.zeros((4, w), F32)
    for k in range(nl):
        halo = block_refs[k][pl.ds(n * rows + UNDER, 2 * n), :].astype(F32)
        beyond = (relayed_ref if k < 2 else direct_ref)[(k % 2) * n : (k % 2 + 1) * n, :]
        pack_ref[0, k * n : (k + 1) * n, :] = jnp.where(li == 0, beyond, halo[0:n])
        pack_ref[1, k * n : (k + 1) * n, :] = jnp.where(li == nl - 1, beyond, halo[n:])
        entries = jnp.concatenate([table_rows(block_refs[k], n, rows)] * 2, axis=0)
        table = table + (pltpu.roll(entries, k * n, 1) if k else entries)[0:4]
    tall = jnp.concatenate([table, jnp.zeros((w - 4, w), F32)], axis=0)
    pack_ref[2] = jnp.transpose(tall)[0 : nl * n]


def last_body(nl, ctx_ref, tile_ref, state_ref, srow_ref, direct_ref, relayed_ref, *rest):
    block_refs, (grad_ref, edge_ref, pay_ref, pack_ref) = rest[:nl], rest[nl:]
    rows, w = ctx_ref.shape[1:]
    fill_pack(nl, pack_ref, block_refs, direct_ref, relayed_ref, rows, w)
    edge_ref[...] = jnp.zeros_like(edge_ref)
    finish(state_ref, ctx_ref, tile_ref[1], tile_ref[2], pack_ref, srow_ref, grad_ref, edge_ref, pay_ref)


def second_body(nl, recv_ref, grad_ref, edge_ref, tile_ref, srow0_ref, pack_ref, *rest):
    obs_refs = rest[:nl]
    out_ref, pay_ref, ctx_ref, state_ref, pb_ref, srow_ref = rest[nl:]
    _, _, place, count = position()
    rows, w = ctx_ref.shape[1:]
    total = w * count
    inv_depth, inv_albedo = inverse_scales(recv_ref, 3, float(rows * total))
    surface = tile_ref[0] - STEP_DEPTH * jnp.tanh(grad_ref[0] * inv_depth)
    albedo = tile_ref[1] - STEP_ALBEDO * jnp.tanh(grad_ref[1] * inv_albedo)
    out_ref[0] = surface
    out_ref[1] = albedo
    srow_ref[...] = jnp.zeros_like(srow_ref)
    srow_ref[2:4, :] = edge_ref[0:2, :]

    @pl.when(place > 0)
    def _():
        frm = exchange_index(jnp.maximum(place - 1, 0))
        srow_ref[0:2, :] = recv_ref[frm, 0:2, :]
        srow_ref[6:7, :] = recv_ref[frm, 2:3, :]

    @pl.when(place < count - 1)
    def _():
        frm = exchange_index(jnp.minimum(place + 1, count - 1))
        srow_ref[4:6, :] = recv_ref[frm, 0:2, :]
        srow_ref[7:8, :] = recv_ref[frm, 2:3, :]

    changes = srow_ref[0:8, :]
    kind = iota(changes.shape, 0) < 6
    changes = jnp.where(
        kind, STEP_DEPTH * jnp.tanh(changes * inv_depth), STEP_ALBEDO * jnp.tanh(changes * inv_albedo)
    )
    srow_ref[0:8, :] = srow0_ref[0:8, :] - changes
    srow_ref[8:16, :] = srow0_ref[8:16, :]
    fill_context(ctx_ref, surface, albedo, srow_ref[1:2, :], srow_ref[4:5, :])
    n = lights_of(obs_refs[0], rows)
    bases = tuple(k * n for k in range(nl))
    for k in range(nl):
        fill_params(pb_ref, bases[k], obs_refs[k], n, rows, w, place, total)
    sweep(ctx_ref, pb_ref, obs_refs, bases, total, lambda at: None, state_store(state_ref, w))
    depth, grad_albedo = finish(
        state_ref, ctx_ref, albedo, tile_ref[2], pack_ref, srow_ref, None, None, pay_ref
    )
    out_ref[2] = depth
    out_ref[3] = grad_albedo


def final_body(nl, recv_ref, *rest):
    parts, (depth_ref, albedo_ref) = rest[:nl], rest[nl:]
    li, _, _, count = position()
    rows, w = parts[0].shape[1:]
    inv_depth, inv_albedo = inverse_scales(recv_ref, 0, float(rows * w * count))
    for k in range(nl):
        at = pl.ds(pl.multiple_of((li ^ k) * w, w), w)
        depth_ref[:, at] = parts[k][0] - STEP_DEPTH * jnp.tanh(parts[k][2] * inv_depth)
        albedo_ref[:, at] = parts[k][1] - STEP_ALBEDO * jnp.tanh(parts[k][3] * inv_albedo)


def shape(*dims, dtype=F32):
    return jax.ShapeDtypeStruct(dims, dtype)


def program(depth_start, albedo_start, observations, light_table, valid_mask):
    nl, ns = lax.axis_size("light"), lax.axis_size("strip")
    nd = nl * ns
    lights, rows, cols = observations.shape
    w = cols // nl

    def swap(x, k):
        return lax.ppermute(x, "light", [(i, i ^ k) for i in range(nl)])

    hbm = pl.BlockSpec(memory_space=pltpu.HBM)
    field = (rows, w)
    *blocks, end = call(
        functools.partial(cut_body, nl),
        tuple(shape(block_rows(lights, rows, k), w, dtype=jnp.bfloat16) for k in range(nl))
        + (shape(2 * lights, rows),),
        [
            pltpu.VMEM((4, lights), jnp.int32),
            pltpu.VMEM((nl + 2, 2 * lights, rows), F32),
            pltpu.SemaphoreType.DMA((nl * lights,)),
            pltpu.SemaphoreType.DMA((1,)),
        ],
        in_specs=[hbm] * 2,
    )(*(pltpu.with_memory_space_constraint(x, pltpu.HBM) for x in (observations, light_table.T)))
    obs2 = swap(blocks[2], 2)
    obs3 = swap(blocks[3], 3)
    obs1 = swap(blocks[1], 1)
    obs0 = blocks[0]
    tile, sr, strip = call(
        functools.partial(join_body, nl), (shape(3, *field), shape(16, rows), shape(2 * lights + 8, rows))
    )(depth_start, albedo_start, valid_mask, obs1, end)
    pairs = []
    for i in range(ns - 1):
        pairs += [(2 * ns + i, i + 1), (i, ns + i + 1), (ns + i + 1, 3 * ns + i), (3 * ns + i + 1, 2 * ns + i)]
    direct = lax.ppermute(strip, AXES, pairs)
    relayed = swap(direct, 1)

    pb = pltpu.VMEM((2 * lights, 5, 8, w), F32)
    ctx, srow, state = call(
        functools.partial(first_body, nl), (shape(4, *field), shape(16, rows), shape(7, *field)), [pb]
    )(tile, sr, direct, obs0, obs1)
    state = call(more_body, shape(7, *field), [pb])(ctx, state, obs2)
    state = call(more_body, shape(7, *field), [pb])(ctx, state, obs3)
    grad, edge, pay, pack = call(
        functools.partial(last_body, nl),
        (shape(2, *field), shape(8, rows), shape(nd, 4, rows), shape(3, nl * lights, rows)),
    )(ctx, tile, state, srow, direct, relayed, obs0, obs1, obs2, obs3)
    recv = lax.all_to_all(pay, AXES, 0, 0, tiled=True)
    own, pay = call(
        functools.partial(second_body, nl),
        (shape(4, *field), shape(nd, 1, rows)),
        [
            pltpu.VMEM((4, *field), F32),
            pltpu.VMEM((7, *field), F32),
            pltpu.VMEM((nl * lights, 5, 8, w), F32),
            pltpu.VMEM((16, rows), F32),
        ],
    )(recv, grad, edge, tile, srow, pack, obs0, obs1, obs2, obs3)
    part2 = swap(own, 2)
    part1 = swap(own, 1)
    recv = lax.all_to_all(pay, AXES, 0, 0, tiled=True)
    recv, part2 = lax.optimization_barrier((recv, part2))
    part3 = swap(part2, 1)
    return tuple(
        call(functools.partial(final_body, nl), (shape(rows, cols), shape(rows, cols)))(recv, own, part1, part2, part3)
    )


def solution(mesh):
    in_specs = (
        P(None, "strip"),
        P(None, "strip"),
        P("light", None, "strip"),
        P("light", None),
        P(None, "strip"),
    )
    out_specs = (P(None, "strip"), P(None, "strip"))
    return jax.shard_map(program, mesh=mesh, in_specs=in_specs, out_specs=out_specs, check_vma=False)
```

```python
import functools
import math

import jax
import jax.numpy as jnp
from jax import lax
from jax.experimental import pallas as pl
from jax.experimental.pallas import tpu as pltpu
from jax.sharding import PartitionSpec as P


AXES = ("light", "strip")
STEP_DEPTH = 0.1
STEP_ALBEDO = 0.2
EPS = 1e-06
HALF_LOG2E = 0.5 * math.log2(math.e)
F32 = jnp.float32
VM = pl.BlockSpec(memory_space=pltpu.VMEM)
TR = 16


def iota(shape, dim):
    return lax.broadcasted_iota(jnp.int32, shape, dim)


def position():
    nl, ns = lax.axis_size("light"), lax.axis_size("strip")
    li, si = lax.axis_index("light"), lax.axis_index("strip")
    return li, si, si * nl + li, nl * ns


def exchange_index(place):
    nl, ns = lax.axis_size("light"), lax.axis_size("strip")
    return lax.rem(place, nl) * ns + lax.div(place, nl)


def call(body, out, scratch=(), vmem=40 << 20, **more):
    return pl.pallas_call(
        body,
        out_shape=out,
        scratch_shapes=list(scratch),
        compiler_params=pltpu.CompilerParams(vmem_limit_bytes=vmem),
        **more,
    )


UNDER = 16


def block_rows(lights, rows, k):
    return lights * rows + UNDER + 2 * lights + (2 * lights if k == 1 else 0)


def cut_body(nl, obs_ref, table_ref, *rest):
    blocks, (end_ref, table, eh_ref, sems, extra) = rest[:nl], rest[nl:]
    lights, rows, cols = obs_ref.shape
    w = cols // nl
    li = lax.axis_index("light")
    copies = []
    for k in (2, 3, 1, 0):
        for l in range(lights):
            at = pl.ds(pl.multiple_of((li ^ k) * w, w), w)
            copies.append(
                pltpu.make_async_copy(
                    obs_ref.at[l, :, at], blocks[k].at[pl.ds(l * rows, rows)], sems.at[k * lights + l]
                )
            )
            copies[-1].start()
    fetch = pltpu.make_async_copy(table_ref, table, extra.at[0])
    fetch.start()
    eh_ref[...] = jnp.zeros_like(eh_ref)
    at, col = iota((8, w), 0), iota((8, w), 1)
    pick = (((at == 0) & (col == 0)) | ((at == 1) & (col == w - 1))).astype(jnp.bfloat16)
    fetch.wait()
    entries = table[...]
    high = lax.shift_right_logical(entries, 5)
    both = jnp.concatenate([high, entries - high * 32], axis=0).astype(F32)
    wide = jnp.concatenate([both, jnp.zeros((8, w - lights), F32)], axis=1)
    under = jnp.concatenate([wide, jnp.zeros((UNDER - 8, w), F32)], axis=0).astype(jnp.bfloat16)
    for k in range(nl):
        blocks[k][pl.ds(lights * rows, UNDER), :] = under
    for copy in copies:
        copy.wait()
    for k in range(nl):
        q = li ^ k
        for l in range(lights):
            e = lax.dot_general(
                pick,
                blocks[k][pl.ds(l * rows, rows), :],
                (((1,), (1,)), ((), ())),
                preferred_element_type=F32,
            )
            eh_ref[q, lights + l : lights + l + 1, :] = e[0:1]
            eh_ref[q + 2, l : l + 1, :] = e[1:2]
    ends = jnp.concatenate([eh_ref[nl + 1, 0:lights, :], eh_ref[0, lights:, :]], axis=0)
    end_ref[...] = ends
    halo = pl.ds(lights * rows + UNDER, 2 * lights)
    for k in range(nl):
        blocks[k][halo, :] = eh_ref[(li ^ k) + 1].astype(jnp.bfloat16)
    blocks[1][pl.ds(lights * rows + UNDER + 2 * lights, 2 * lights), :] = ends.astype(jnp.bfloat16)


def join_body(nl, depth_ref, albedo_ref, valid_ref, block_ref, end_ref, tile_ref, sr_ref, out_ref):
    rows, w = tile_ref.shape[1:]
    n = end_ref.shape[0] // 2
    li = lax.axis_index("light")
    right = lax.rem(li, 2) == 0
    other = block_ref[pl.ds(block_ref.shape[0] - 2 * n, 2 * n), :].astype(F32)
    out_ref[0:n, :] = jnp.where(right, end_ref[0:n, :], end_ref[n:, :])
    out_ref[n : 2 * n, :] = jnp.where(right, other[0:n], other[n:])
    out_ref[2 * n :, :] = jnp.zeros((8, rows), F32)
    sr_ref[...] = jnp.zeros_like(sr_ref)
    lane = iota((rows, w), 1)

    def columns(ref, q):
        return ref[:, pl.ds(pl.multiple_of(q * w, w), w)].astype(F32)

    for f, ref in enumerate((depth_ref, albedo_ref, valid_ref)):
        own = columns(ref, li)
        before = columns(ref, jnp.maximum(li - 1, 0))
        after = columns(ref, jnp.minimum(li + 1, nl - 1))
        tile_ref[f] = own
        inner = jnp.transpose(own)
        outer = jnp.transpose(jnp.where(lane < w // 2, after, before))
        edge = jnp.transpose(columns(ref, jnp.where(right, nl - 1, 0)))
        low = jnp.where(li == 0, 0.0, outer[w - 2 : w])
        high = jnp.where(li == nl - 1, 0.0, outer[0:2])
        if f == 0:
            sr_ref[0:2, :] = low
            sr_ref[2:3, :] = inner[0:1]
            sr_ref[3:4, :] = inner[w - 1 : w]
            sr_ref[4:6, :] = high
            out_ref[2 * n : 2 * n + 2, :] = jnp.where(right, edge[w - 2 : w], edge[0:2])
        else:
            at = 4 + 2 * f
            sr_ref[at : at + 1, :] = low[1:2]
            sr_ref[at + 1 : at + 2, :] = high[0:1]
            at = 2 * n + 1 + f
            out_ref[at : at + 1, :] = jnp.where(right, edge[w - 1 : w], edge[0:1])


def decode(table):
    return (
        table[:, 0:1] / 500.0 - 1.0,
        table[:, 1:2] / 500.0 - 1.0,
        1.0 + table[:, 2:3] / 1000.0,
        0.5 + table[:, 3:4] / 1000.0,
    )


def decode_rows(table):
    return (
        table[0:1] / 500.0 - 1.0,
        table[1:2] / 500.0 - 1.0,
        1.0 + table[2:3] / 1000.0,
        0.5 + table[3:4] / 1000.0,
    )


def columns_from(left, right, shape):
    rows, w = shape
    at = iota((w, rows), 0)
    return jnp.transpose(jnp.where(at == 0, left, jnp.where(at == w - 1, right, 0.0)))


def shifts_rows(x):
    r = iota(x.shape, 0)
    n = x.shape[0]
    above = jnp.where(r == 0, 0.0, pltpu.roll(x, 1, 0))
    below = jnp.where(r == n - 1, 0.0, pltpu.roll(x, n - 1, 0))
    return above, below


def shifts_cols(x, ends):
    c = iota(x.shape, 1)
    n = x.shape[1]
    before = jnp.where(c == 0, ends, pltpu.roll(x, 1, 1))
    after = jnp.where(c == n - 1, ends, pltpu.roll(x, n - 1, 1))
    return before, after


def fill_context(ctx_ref, surface, albedo, left, right):
    ends = columns_from(left, right, surface.shape)
    before, after = shifts_cols(surface, ends)
    above, below = shifts_rows(surface)
    sx = 0.5 * (after - before)
    sy = 0.5 * (below - above)
    ctx_ref[0] = surface
    ctx_ref[1] = sx
    ctx_ref[2] = sy
    ctx_ref[3] = albedo * lax.rsqrt(1.0 + sx * sx + sy * sy)


def lights_of(block_ref, rows):
    return block_ref.shape[0] // rows


def table_rows(block_ref, n, rows):
    under = block_ref[pl.ds(n * rows, UNDER), :].astype(F32)
    return under[0:4] * 32.0 + under[4:8]


def fill_params(pb_ref, base, block_ref, n, rows, w, place, total):
    lx, ly, lz, le = decode_rows(table_rows(block_ref, n, rows))
    col = iota((8, w), 1) + place * w
    px = (col.astype(F32) + 0.5) / total - 0.5
    for j in range(n):
        dx = jnp.broadcast_to(lx[:, j : j + 1], (8, w)) - px
        pb_ref[base + j, 0] = dx
        pb_ref[base + j, 1] = dx * dx
        pb_ref[base + j, 2] = jnp.broadcast_to(ly[:, j : j + 1], (8, w))
        pb_ref[base + j, 3] = jnp.broadcast_to(lz[:, j : j + 1], (8, w))
        pb_ref[base + j, 4] = jnp.broadcast_to(le[:, j : j + 1], (8, w))


def accumulate(state, tile, py, obs, pb_ref, base):
    surface, sx, sy, scaled = tile
    kept = []
    least = None
    for j in range(len(obs)):
        dx, dx2 = pb_ref[base + j, 0], pb_ref[base + j, 1]
        dy = pb_ref[base + j, 2] - py
        dz = pb_ref[base + j, 3] - surface
        dist = (dx2 + dy * dy) + dz * dz
        facing = dz - (sx * dx + sy * dy)
        r = lax.rsqrt(dist)
        r2 = r * r
        g = (r2 * r) * pb_ref[base + j, 4]
        residual = scaled * (g * facing) - obs[j]
        square = residual * residual
        least = square if least is None else jnp.minimum(least, square)
        kept.append((square, residual * g, facing, dz * r2, dx, dy))
    if state is not None:
        before = state[0]
        least = jnp.minimum(least, before)
    sums = None
    for square, q, facing, drop, dx, dy in kept:
        w = jnp.exp2((least - square) * HALF_LOG2E)
        p = w * q
        pf = p * facing
        terms = (w, p, p * dx, p * dy, pf, pf * drop)
        sums = terms if sums is None else tuple(a + b for a, b in zip(sums, terms))
    if state is not None:
        fade = jnp.exp2((least - before) * HALF_LOG2E)
        sums = tuple(a * fade + b for a, b in zip(state[1:], sums))
    return (least,) + sums


def sweep(ctx_ref, params, obs_refs, total, load, store):
    rows, w = ctx_ref.shape[1:]
    lights = lights_of(obs_refs[0], rows)
    split = (TR // 8, 8, w)

    def step(i, carry):
        at = pl.ds(pl.multiple_of(i * TR, TR), TR)
        tile = tuple(ctx_ref[f, at, :].reshape(split) for f in range(4))
        row = iota(split, 0) * 8 + iota(split, 1) + i * TR
        py = (row.astype(F32) + (0.5 - rows / 2.0)) / total
        state = load(at)
        for obs_ref, (pb_ref, base) in zip(obs_refs, params):
            obs = [
                obs_ref[pl.ds(pl.multiple_of(j * rows + i * TR, TR), TR), :].astype(F32).reshape(split)
                for j in range(lights)
            ]
            state = accumulate(state, tile, py, obs, pb_ref, base)
        store(at, state)
        return carry

    lax.fori_loop(0, rows // TR, step, 0)


def state_load(state_ref, w):
    return lambda at: tuple(state_ref[f, at, :].reshape(TR // 8, 8, w) for f in range(7))


def state_store(state_ref, w):
    def store(at, state):
        for f in range(7):
            state_ref[f, at, :] = state[f].reshape(TR, w)

    return store


def halo_slope(column, side, pack_ref, srow_ref, rows, total):
    obs = pack_ref[side]
    lx, ly, lz, le = decode(pack_ref[2])
    outer, inner = (0, 2) if side == 0 else (5, 3)
    here = 1 if side == 0 else 4
    surface = srow_ref[here : here + 1, :]
    toward = srow_ref[inner : inner + 1, :] - srow_ref[outer : outer + 1, :]
    sx = 0.5 * toward if side == 0 else -0.5 * toward
    lane = iota((8, rows), 1)
    wide = jnp.broadcast_to(surface, (8, rows))
    above = jnp.where(lane == 0, 0.0, pltpu.roll(wide, 1, 1))
    below = jnp.where(lane == rows - 1, 0.0, pltpu.roll(wide, rows - 1, 1))
    sy = (0.5 * (below - above))[0:1]
    albedo = srow_ref[6 + side : 7 + side, :]
    valid = srow_ref[8 + side : 9 + side, :]
    px = (column.astype(F32) + 0.5) / total - 0.5
    py = (iota((1, rows), 1).astype(F32) + (0.5 - rows / 2.0)) / total
    rn = lax.rsqrt(1.0 + sx * sx + sy * sy)
    dx = jnp.broadcast_to(lx - px, obs.shape)
    dy = ly - py
    dz = lz - surface
    dist = dx * dx + dy * dy + dz * dz
    facing = dz - (sx * dx + sy * dy)
    r = lax.rsqrt(dist)
    g = (r * r) * r * le
    residual = (albedo * rn) * (g * facing) - obs
    square = residual * residual
    least = jnp.min(square, axis=0, keepdims=True)
    w = jnp.exp2((least - square) * HALF_LOG2E)
    p = w * residual * g
    total_w = jnp.sum(w, axis=0, keepdims=True)
    px_sum = jnp.sum(p * dx, axis=0, keepdims=True)
    pf_sum = jnp.sum(p * facing, axis=0, keepdims=True)
    return -(valid * albedo * rn / total_w) * (px_sum + (sx * rn * rn) * pf_sum)


def gradients(state_ref, ctx_ref, albedo, valid, slope_low, slope_high):
    sx, sy = ctx_ref[1], ctx_ref[2]
    rn = lax.rsqrt(1.0 + sx * sx + sy * sy)
    inverse = valid * rn / state_ref[1]
    factor = inverse * albedo
    pf = state_ref[5]
    rn2pf = rn * rn * pf
    grad_albedo = inverse * pf
    direct = factor * (3.0 * state_ref[6] - state_ref[2])
    grad_x = -factor * (state_ref[3] + sx * rn2pf)
    grad_y = -factor * (state_ref[4] + sy * rn2pf)
    before, after = shifts_cols(grad_x, columns_from(slope_low, slope_high, grad_x.shape))
    above, below = shifts_rows(grad_y)
    return direct + 0.5 * (before - after) + 0.5 * (above - below), grad_albedo


def partial_sums(depth, albedo):
    n = depth.shape[1]
    d = jnp.sum(depth * depth, axis=0, keepdims=True)
    a = jnp.sum(albedo * albedo, axis=0, keepdims=True)
    d = jnp.broadcast_to(d, (8, n))
    a = jnp.broadcast_to(a, (8, n))
    d = d + pltpu.roll(d, n // 2, 1)
    a = a + pltpu.roll(a, n // 2, 1)
    return jnp.where(iota((8, n), 1) < n // 2, d, a)[0:1]


def inverse_scales(recv_ref, row, count):
    rows = recv_ref[:, row, :]
    n = rows.shape[1]
    lane = iota(rows.shape, 1)
    d = jnp.sum(jnp.where(lane < n // 2, rows, 0.0), keepdims=True)
    a = jnp.sum(jnp.where(lane < n // 2, 0.0, rows), keepdims=True)
    return lax.rsqrt(d / count + EPS), lax.rsqrt(a / count + EPS)


def first_body(nl, tile_ref, sr_ref, strip_ref, obs0, obs1, ctx_ref, srow_ref, state_ref, pb_ref):
    li, _, place, count = position()
    rows, w = ctx_ref.shape[1:]
    srow_ref[...] = sr_ref[...]
    at = strip_ref.shape[0] - 8

    @pl.when(li == 0)
    def _():
        srow_ref[0:2, :] = strip_ref[at : at + 2, :]
        srow_ref[6:7, :] = strip_ref[at + 2 : at + 3, :]
        srow_ref[8:9, :] = strip_ref[at + 3 : at + 4, :]

    @pl.when(li == nl - 1)
    def _():
        srow_ref[4:6, :] = strip_ref[at : at + 2, :]
        srow_ref[7:8, :] = strip_ref[at + 2 : at + 3, :]
        srow_ref[9:10, :] = strip_ref[at + 3 : at + 4, :]

    fill_context(ctx_ref, tile_ref[0], tile_ref[1], srow_ref[1:2, :], srow_ref[4:5, :])
    total = w * count
    n = lights_of(obs0, rows)
    fill_params(pb_ref, 0, obs0, n, rows, w, place, total)
    fill_params(pb_ref, n, obs1, n, rows, w, place, total)
    sweep(ctx_ref, ((pb_ref, 0), (pb_ref, n)), (obs0, obs1), total, lambda at: None, state_store(state_ref, w))


def more_body(ctx_ref, in_ref, obs, state_ref, pb_ref):
    _, _, place, count = position()
    rows, w = ctx_ref.shape[1:]
    total = w * count
    fill_params(pb_ref, 0, obs, lights_of(obs, rows), rows, w, place, total)
    sweep(ctx_ref, ((pb_ref, 0),), (obs,), total, state_load(in_ref, w), state_store(state_ref, w))


def finish(state_ref, ctx_ref, albedo, valid, pack_ref, srow_ref, grad_ref, edge_ref, pay_ref):
    _, _, place, count = position()
    rows, w = ctx_ref.shape[1:]
    total = w * count
    low = halo_slope(place * w - 1, 0, pack_ref, srow_ref, rows, total)
    high = halo_slope(place * w + w, 1, pack_ref, srow_ref, rows, total)
    depth, grad_albedo = gradients(state_ref, ctx_ref, albedo, valid, low, high)
    sums = partial_sums(depth, grad_albedo)
    if edge_ref is None:
        pay_ref[...] = jnp.broadcast_to(sums[None], pay_ref.shape)
        return depth, grad_albedo
    grad_ref[0] = depth
    grad_ref[1] = grad_albedo
    dt = jnp.transpose(depth)
    at = jnp.transpose(grad_albedo)
    edge_ref[0:1, :] = dt[0:1]
    edge_ref[1:2, :] = dt[w - 1 : w]
    pay_ref[:, 0:2, :] = jnp.broadcast_to(dt[0:2][None], (count, 2, rows))
    pay_ref[:, 2:3, :] = jnp.broadcast_to(at[0:1][None], (count, 1, rows))
    pay_ref[:, 3:4, :] = jnp.broadcast_to(sums[None], (count, 1, w))

    @pl.when(place < count - 1)
    def _():
        to = exchange_index(place + 1)
        pay_ref[to, 0:2, :] = dt[w - 2 : w]
        pay_ref[to, 2:3, :] = at[w - 1 : w]

    return depth, grad_albedo


def fill_pack(nl, pack_ref, block_refs, direct_ref, relayed_ref, rows, w):
    li = lax.axis_index("light")
    n = lights_of(block_refs[0], rows)
    table = jnp.zeros((4, w), F32)
    for k in range(nl):
        halo = block_refs[k][pl.ds(n * rows + UNDER, 2 * n), :].astype(F32)
        beyond = (direct_ref if k < 2 else relayed_ref)[(k % 2) * n : (k % 2 + 1) * n, :]
        pack_ref[0, k * n : (k + 1) * n, :] = jnp.where(li == 0, beyond, halo[0:n])
        pack_ref[1, k * n : (k + 1) * n, :] = jnp.where(li == nl - 1, beyond, halo[n:])
        entries = jnp.concatenate([table_rows(block_refs[k], n, rows)] * 2, axis=0)
        table = table + (pltpu.roll(entries, k * n, 1) if k else entries)[0:4]
    tall = jnp.concatenate([table, jnp.zeros((w - 4, w), F32)], axis=0)
    pack_ref[2] = jnp.transpose(tall)[0 : nl * n]


def last_body(nl, ctx_ref, tile_ref, state_ref, srow_ref, direct_ref, relayed_ref, *rest):
    block_refs, (grad_ref, edge_ref, pay_ref, pack_ref) = rest[:nl], rest[nl:]
    rows, w = ctx_ref.shape[1:]
    fill_pack(nl, pack_ref, block_refs, direct_ref, relayed_ref, rows, w)
    edge_ref[...] = jnp.zeros_like(edge_ref)
    finish(state_ref, ctx_ref, tile_ref[1], tile_ref[2], pack_ref, srow_ref, grad_ref, edge_ref, pay_ref)


def second_body(nl, recv_ref, grad_ref, edge_ref, tile_ref, srow0_ref, pack_ref, *rest):
    obs_refs, pb_refs = rest[:nl], rest[nl : 2 * nl - 1]
    out_ref, pay_ref, ctx_ref, state_ref, srow_ref = rest[2 * nl - 1 :]
    _, _, place, count = position()
    rows, w = ctx_ref.shape[1:]
    total = w * count
    inv_depth, inv_albedo = inverse_scales(recv_ref, 3, float(rows * total))
    surface = tile_ref[0] - STEP_DEPTH * jnp.tanh(grad_ref[0] * inv_depth)
    albedo = tile_ref[1] - STEP_ALBEDO * jnp.tanh(grad_ref[1] * inv_albedo)
    out_ref[0] = surface
    out_ref[1] = albedo
    srow_ref[...] = jnp.zeros_like(srow_ref)
    srow_ref[2:4, :] = edge_ref[0:2, :]

    @pl.when(place > 0)
    def _():
        frm = exchange_index(jnp.maximum(place - 1, 0))
        srow_ref[0:2, :] = recv_ref[frm, 0:2, :]
        srow_ref[6:7, :] = recv_ref[frm, 2:3, :]

    @pl.when(place < count - 1)
    def _():
        frm = exchange_index(jnp.minimum(place + 1, count - 1))
        srow_ref[4:6, :] = recv_ref[frm, 0:2, :]
        srow_ref[7:8, :] = recv_ref[frm, 2:3, :]

    changes = srow_ref[0:8, :]
    kind = iota(changes.shape, 0) < 6
    changes = jnp.where(
        kind, STEP_DEPTH * jnp.tanh(changes * inv_depth), STEP_ALBEDO * jnp.tanh(changes * inv_albedo)
    )
    srow_ref[0:8, :] = srow0_ref[0:8, :] - changes
    srow_ref[8:16, :] = srow0_ref[8:16, :]
    fill_context(ctx_ref, surface, albedo, srow_ref[1:2, :], srow_ref[4:5, :])
    n = lights_of(obs_refs[0], rows)
    params = ((pb_refs[0], 0), (pb_refs[0], n)) + tuple((ref, 0) for ref in pb_refs[1:])
    sweep(ctx_ref, params, obs_refs, total, lambda at: None, state_store(state_ref, w))
    depth, grad_albedo = finish(
        state_ref, ctx_ref, albedo, tile_ref[2], pack_ref, srow_ref, None, None, pay_ref
    )
    out_ref[2] = depth
    out_ref[3] = grad_albedo


def final_body(nl, recv_ref, *rest):
    parts, (depth_ref, albedo_ref) = rest[:nl], rest[nl:]
    li, _, _, count = position()
    rows, w = parts[0].shape[1:]
    inv_depth, inv_albedo = inverse_scales(recv_ref, 0, float(rows * w * count))
    for k in range(nl):
        at = pl.ds(pl.multiple_of((li ^ k) * w, w), w)
        depth_ref[:, at] = parts[k][0] - STEP_DEPTH * jnp.tanh(parts[k][2] * inv_depth)
        albedo_ref[:, at] = parts[k][1] - STEP_ALBEDO * jnp.tanh(parts[k][3] * inv_albedo)


def shape(*dims, dtype=F32):
    return jax.ShapeDtypeStruct(dims, dtype)


def program(depth_start, albedo_start, observations, light_table, valid_mask):
    nl, ns = lax.axis_size("light"), lax.axis_size("strip")
    nd = nl * ns
    lights, rows, cols = observations.shape
    w = cols // nl

    def swap(x, k):
        return lax.ppermute(x, "light", [(i, i ^ k) for i in range(nl)])

    hbm = pl.BlockSpec(memory_space=pltpu.HBM)
    field = (rows, w)
    *blocks, end = call(
        functools.partial(cut_body, nl),
        tuple(shape(block_rows(lights, rows, k), w, dtype=jnp.bfloat16) for k in range(nl))
        + (shape(2 * lights, rows),),
        [
            pltpu.VMEM((4, lights), jnp.int32),
            pltpu.VMEM((nl + 2, 2 * lights, rows), F32),
            pltpu.SemaphoreType.DMA((nl * lights,)),
            pltpu.SemaphoreType.DMA((1,)),
        ],
        in_specs=[hbm] * 2,
    )(*(pltpu.with_memory_space_constraint(x, pltpu.HBM) for x in (observations, light_table.T)))
    obs2 = swap(blocks[2], 2)
    obs3 = swap(blocks[3], 3)
    obs1 = swap(blocks[1], 1)
    obs0 = blocks[0]
    tile, sr, strip = call(
        functools.partial(join_body, nl), (shape(3, *field), shape(16, rows), shape(2 * lights + 8, rows))
    )(depth_start, albedo_start, valid_mask, obs1, end)
    pairs = []
    for i in range(ns - 1):
        for l in range(nl):
            source, target = (i, i + 1) if l % 2 == 0 else (i + 1, i)
            pairs.append((l * ns + source, l * ns + target))
    direct = lax.ppermute(strip, AXES, pairs)
    relayed = swap(direct, 2)

    def tiles(n):
        return shape(n, 5, 8, w)

    ctx, srow, state, pb0 = call(
        functools.partial(first_body, nl), (shape(4, *field), shape(16, rows), shape(7, *field), tiles(2 * lights))
    )(tile, sr, direct, obs0, obs1)
    more = (shape(7, *field), tiles(lights))
    state, pb2 = call(more_body, more)(ctx, state, obs2)
    state, pb3 = call(more_body, more)(ctx, state, obs3)
    grad, edge, pay, pack = call(
        functools.partial(last_body, nl),
        (shape(2, *field), shape(8, rows), shape(nd, 4, rows), shape(3, nl * lights, rows)),
    )(ctx, tile, state, srow, direct, relayed, obs0, obs1, obs2, obs3)
    recv = lax.all_to_all(pay, AXES, 0, 0, tiled=True)
    own, pay = call(
        functools.partial(second_body, nl),
        (shape(4, *field), shape(nd, 1, rows)),
        [
            pltpu.VMEM((4, *field), F32),
            pltpu.VMEM((7, *field), F32),
            pltpu.VMEM((16, rows), F32),
        ],
    )(recv, grad, edge, tile, srow, pack, obs0, obs1, obs2, obs3, pb0, pb2, pb3)
    part2 = swap(own, 2)
    part1 = swap(own, 1)
    recv = lax.all_to_all(pay, AXES, 0, 0, tiled=True)
    recv, part2 = lax.optimization_barrier((recv, part2))
    part3 = swap(part2, 1)
    return tuple(
        call(functools.partial(final_body, nl), (shape(rows, cols), shape(rows, cols)))(recv, own, part1, part2, part3)
    )


def solution(mesh):
    in_specs = (
        P(None, "strip"),
        P(None, "strip"),
        P("light", None, "strip"),
        P("light", None),
        P(None, "strip"),
    )
    out_specs = (P(None, "strip"), P(None, "strip"))
    return jax.shard_map(program, mesh=mesh, in_specs=in_specs, out_specs=out_specs, check_vma=False)
```

```python
import functools
import math

import jax
import jax.numpy as jnp
from jax import lax
from jax.experimental import pallas as pl
from jax.experimental.pallas import tpu as pltpu
from jax.sharding import PartitionSpec as P


AXES = ("light", "strip")
STEP_DEPTH = 0.1
STEP_ALBEDO = 0.2
EPS = 1e-06
HALF_LOG2E = 0.5 * math.log2(math.e)
F32 = jnp.float32
VM = pl.BlockSpec(memory_space=pltpu.VMEM)
TR = 16


def iota(shape, dim):
    return lax.broadcasted_iota(jnp.int32, shape, dim)


def position():
    nl, ns = lax.axis_size("light"), lax.axis_size("strip")
    li, si = lax.axis_index("light"), lax.axis_index("strip")
    return li, si, si * nl + li, nl * ns


def exchange_index(place):
    nl, ns = lax.axis_size("light"), lax.axis_size("strip")
    return lax.rem(place, nl) * ns + lax.div(place, nl)


def call(body, out, scratch=(), vmem=40 << 20, **more):
    return pl.pallas_call(
        body,
        out_shape=out,
        scratch_shapes=list(scratch),
        compiler_params=pltpu.CompilerParams(vmem_limit_bytes=vmem),
        **more,
    )


UNDER = 16
LATE = 2


def block_rows(lights, rows, k, nl):
    here = lights - LATE if k == nl - 1 else lights
    return here * rows + UNDER + 2 * lights + (2 * lights if k == 1 else 0)


def cut_body(nl, obs_ref, table_ref, *rest):
    blocks, (late_ref, end_ref, table, eh_ref, sems, extra) = rest[:nl], rest[nl:]
    lights, rows, cols = obs_ref.shape
    w = cols // nl
    li = lax.axis_index("light")
    here = [lights_of(block, rows) for block in blocks]

    def slot(k, l):
        if l < here[k]:
            return blocks[k].at[pl.ds(l * rows, rows)]
        return late_ref.at[pl.ds((l - here[k]) * rows, rows)]

    copies = []
    for k in (2, 3, 1, 0):
        for l in range(lights):
            at = pl.ds(pl.multiple_of((li ^ k) * w, w), w)
            copies.append(pltpu.make_async_copy(obs_ref.at[l, :, at], slot(k, l), sems.at[k * lights + l]))
            copies[-1].start()
    fetch = pltpu.make_async_copy(table_ref, table, extra.at[0])
    fetch.start()
    eh_ref[...] = jnp.zeros_like(eh_ref)
    at, col = iota((8, w), 0), iota((8, w), 1)
    pick = (((at == 0) & (col == 0)) | ((at == 1) & (col == w - 1))).astype(jnp.bfloat16)
    fetch.wait()
    entries = table[...]
    high = lax.shift_right_logical(entries, 5)
    both = jnp.concatenate([high, entries - high * 32], axis=0).astype(F32)
    wide = jnp.concatenate([both, jnp.zeros((8, w - lights), F32)], axis=1)
    under = jnp.concatenate([wide, jnp.zeros((UNDER - 8, w), F32)], axis=0).astype(jnp.bfloat16)
    for k in range(nl):
        blocks[k][pl.ds(here[k] * rows, UNDER), :] = under
    for copy in copies:
        copy.wait()
    for k in range(nl):
        q = li ^ k
        for l in range(lights):
            e = lax.dot_general(
                pick,
                slot(k, l)[...],
                (((1,), (1,)), ((), ())),
                preferred_element_type=F32,
            )
            eh_ref[q, lights + l : lights + l + 1, :] = e[0:1]
            eh_ref[q + 2, l : l + 1, :] = e[1:2]
    ends = jnp.concatenate([eh_ref[nl + 1, 0:lights, :], eh_ref[0, lights:, :]], axis=0)
    end_ref[...] = ends
    for k in range(nl):
        halo = pl.ds(here[k] * rows + UNDER, 2 * lights)
        blocks[k][halo, :] = eh_ref[(li ^ k) + 1].astype(jnp.bfloat16)
    blocks[1][pl.ds(lights * rows + UNDER + 2 * lights, 2 * lights), :] = ends.astype(jnp.bfloat16)


def join_body(nl, depth_ref, albedo_ref, valid_ref, block_ref, end_ref, tile_ref, sr_ref, out_ref):
    rows, w = tile_ref.shape[1:]
    n = end_ref.shape[0] // 2
    li = lax.axis_index("light")
    right = lax.rem(li, 2) == 0
    other = block_ref[pl.ds(block_ref.shape[0] - 2 * n, 2 * n), :].astype(F32)
    out_ref[0:n, :] = jnp.where(right, end_ref[0:n, :], end_ref[n:, :])
    out_ref[n : 2 * n, :] = jnp.where(right, other[0:n], other[n:])
    out_ref[2 * n :, :] = jnp.zeros((8, rows), F32)
    sr_ref[...] = jnp.zeros_like(sr_ref)
    lane = iota((rows, w), 1)

    def columns(ref, q):
        return ref[:, pl.ds(pl.multiple_of(q * w, w), w)].astype(F32)

    for f, ref in enumerate((depth_ref, albedo_ref, valid_ref)):
        own = columns(ref, li)
        before = columns(ref, jnp.maximum(li - 1, 0))
        after = columns(ref, jnp.minimum(li + 1, nl - 1))
        tile_ref[f] = own
        inner = jnp.transpose(own)
        outer = jnp.transpose(jnp.where(lane < w // 2, after, before))
        edge = jnp.transpose(columns(ref, jnp.where(right, nl - 1, 0)))
        low = jnp.where(li == 0, 0.0, outer[w - 2 : w])
        high = jnp.where(li == nl - 1, 0.0, outer[0:2])
        if f == 0:
            sr_ref[0:2, :] = low
            sr_ref[2:3, :] = inner[0:1]
            sr_ref[3:4, :] = inner[w - 1 : w]
            sr_ref[4:6, :] = high
            out_ref[2 * n : 2 * n + 2, :] = jnp.where(right, edge[w - 2 : w], edge[0:2])
        else:
            at = 4 + 2 * f
            sr_ref[at : at + 1, :] = low[1:2]
            sr_ref[at + 1 : at + 2, :] = high[0:1]
            at = 2 * n + 1 + f
            out_ref[at : at + 1, :] = jnp.where(right, edge[w - 1 : w], edge[0:1])


def decode(table):
    return (
        table[:, 0:1] / 500.0 - 1.0,
        table[:, 1:2] / 500.0 - 1.0,
        1.0 + table[:, 2:3] / 1000.0,
        0.5 + table[:, 3:4] / 1000.0,
    )


def decode_rows(table):
    return (
        table[0:1] / 500.0 - 1.0,
        table[1:2] / 500.0 - 1.0,
        1.0 + table[2:3] / 1000.0,
        0.5 + table[3:4] / 1000.0,
    )


def columns_from(left, right, shape):
    rows, w = shape
    at = iota((w, rows), 0)
    return jnp.transpose(jnp.where(at == 0, left, jnp.where(at == w - 1, right, 0.0)))


def shifts_rows(x):
    r = iota(x.shape, 0)
    n = x.shape[0]
    above = jnp.where(r == 0, 0.0, pltpu.roll(x, 1, 0))
    below = jnp.where(r == n - 1, 0.0, pltpu.roll(x, n - 1, 0))
    return above, below


def shifts_cols(x, ends):
    c = iota(x.shape, 1)
    n = x.shape[1]
    before = jnp.where(c == 0, ends, pltpu.roll(x, 1, 1))
    after = jnp.where(c == n - 1, ends, pltpu.roll(x, n - 1, 1))
    return before, after


def fill_context(ctx_ref, surface, albedo, left, right):
    ends = columns_from(left, right, surface.shape)
    before, after = shifts_cols(surface, ends)
    above, below = shifts_rows(surface)
    sx = 0.5 * (after - before)
    sy = 0.5 * (below - above)
    ctx_ref[0] = surface
    ctx_ref[1] = sx
    ctx_ref[2] = sy
    ctx_ref[3] = albedo * lax.rsqrt(1.0 + sx * sx + sy * sy)


def lights_of(block_ref, rows):
    return block_ref.shape[0] // rows


def table_rows(block_ref, rows):
    under = block_ref[pl.ds(lights_of(block_ref, rows) * rows, UNDER), :].astype(F32)
    return under[0:4] * 32.0 + under[4:8]


def fill_params(pb_ref, base, block_ref, n, rows, w, place, total):
    lx, ly, lz, le = decode_rows(table_rows(block_ref, rows))
    col = iota((8, w), 1) + place * w
    px = (col.astype(F32) + 0.5) / total - 0.5
    for j in range(n):
        dx = jnp.broadcast_to(lx[:, j : j + 1], (8, w)) - px
        pb_ref[base + j, 0] = dx
        pb_ref[base + j, 1] = dx * dx
        pb_ref[base + j, 2] = jnp.broadcast_to(ly[:, j : j + 1], (8, w))
        pb_ref[base + j, 3] = jnp.broadcast_to(lz[:, j : j + 1], (8, w))
        pb_ref[base + j, 4] = jnp.broadcast_to(le[:, j : j + 1], (8, w))


def accumulate(state, tile, py, lights):
    surface, sx, sy, scaled = tile
    kept = []
    least = None
    for obs, pb, across in lights:
        dx = pb(0)
        dy = pb(2) - py
        dz = pb(3) - surface
        flat = across(None)
        if flat is None:
            flat = pb(1) + dy * dy
            across(flat)
        dist = flat + dz * dz
        facing = dz - (sx * dx + sy * dy)
        r = lax.rsqrt(dist)
        r2 = r * r
        g = (r2 * r) * pb(4)
        residual = scaled * (g * facing) - obs
        square = residual * residual
        least = square if least is None else jnp.minimum(least, square)
        kept.append((square, residual * g, facing, dz * r2, dx, dy))
    if state is not None:
        before = state[0]
        least = jnp.minimum(least, before)
    sums = None
    for square, q, facing, drop, dx, dy in kept:
        w = jnp.exp2((least - square) * HALF_LOG2E)
        p = w * q
        pf = p * facing
        terms = (w, p, p * dx, p * dy, pf, pf * drop)
        sums = terms if sums is None else tuple(a + b for a, b in zip(sums, terms))
    if state is not None:
        fade = jnp.exp2((least - before) * HALF_LOG2E)
        sums = tuple(a * fade + b for a, b in zip(state[1:], sums))
    return (least,) + sums


def sweep(ctx_ref, chunks, total, load, store, known):
    rows, w = ctx_ref.shape[1:]
    split = (TR // 8, 8, w)

    def step(i, carry):
        at = pl.ds(pl.multiple_of(i * TR, TR), TR)
        tile = tuple(ctx_ref[f, at, :].reshape(split) for f in range(4))
        row = iota(split, 0) * 8 + iota(split, 1) + i * TR
        py = (row.astype(F32) + (0.5 - rows / 2.0)) / total

        def light(entry):
            (obs_ref, j), (pb_ref, p), (flat_ref, f) = entry
            obs = obs_ref[pl.ds(pl.multiple_of(j * rows + i * TR, TR), TR), :].astype(F32).reshape(split)

            def across(value):
                if known:
                    return flat_ref[f, at, :].reshape(split)
                if value is not None:
                    flat_ref[f, at, :] = value.reshape(TR, w)
                return None

            return obs, lambda field: pb_ref[p, field], across

        state = load(at)
        for chunk in chunks:
            state = accumulate(state, tile, py, [light(entry) for entry in chunk])
        store(at, state)
        return carry

    lax.fori_loop(0, rows // TR, step, 0)


def chunk_of(obs_ref, pb_ref, flat_ref, count, pb_at=0, flat_at=0):
    return [((obs_ref, j), (pb_ref, pb_at + j), (flat_ref, flat_at + j)) for j in range(count)]


def state_load(state_ref, w):
    return lambda at: tuple(state_ref[f, at, :].reshape(TR // 8, 8, w) for f in range(7))


def state_store(state_ref, w):
    def store(at, state):
        for f in range(7):
            state_ref[f, at, :] = state[f].reshape(TR, w)

    return store


def halo_slope(column, side, pack_ref, srow_ref, rows, total):
    obs = pack_ref[side]
    lx, ly, lz, le = decode(pack_ref[2])
    outer, inner = (0, 2) if side == 0 else (5, 3)
    here = 1 if side == 0 else 4
    surface = srow_ref[here : here + 1, :]
    toward = srow_ref[inner : inner + 1, :] - srow_ref[outer : outer + 1, :]
    sx = 0.5 * toward if side == 0 else -0.5 * toward
    lane = iota((8, rows), 1)
    wide = jnp.broadcast_to(surface, (8, rows))
    above = jnp.where(lane == 0, 0.0, pltpu.roll(wide, 1, 1))
    below = jnp.where(lane == rows - 1, 0.0, pltpu.roll(wide, rows - 1, 1))
    sy = (0.5 * (below - above))[0:1]
    albedo = srow_ref[6 + side : 7 + side, :]
    valid = srow_ref[8 + side : 9 + side, :]
    px = (column.astype(F32) + 0.5) / total - 0.5
    py = (iota((1, rows), 1).astype(F32) + (0.5 - rows / 2.0)) / total
    rn = lax.rsqrt(1.0 + sx * sx + sy * sy)
    dx = jnp.broadcast_to(lx - px, obs.shape)
    dy = ly - py
    dz = lz - surface
    dist = dx * dx + dy * dy + dz * dz
    facing = dz - (sx * dx + sy * dy)
    r = lax.rsqrt(dist)
    g = (r * r) * r * le
    residual = (albedo * rn) * (g * facing) - obs
    square = residual * residual
    least = jnp.min(square, axis=0, keepdims=True)
    w = jnp.exp2((least - square) * HALF_LOG2E)
    p = w * residual * g
    total_w = jnp.sum(w, axis=0, keepdims=True)
    px_sum = jnp.sum(p * dx, axis=0, keepdims=True)
    pf_sum = jnp.sum(p * facing, axis=0, keepdims=True)
    return -(valid * albedo * rn / total_w) * (px_sum + (sx * rn * rn) * pf_sum)


def gradients(state_ref, ctx_ref, albedo, valid, slope_low, slope_high):
    sx, sy = ctx_ref[1], ctx_ref[2]
    rn = lax.rsqrt(1.0 + sx * sx + sy * sy)
    inverse = valid * rn / state_ref[1]
    factor = inverse * albedo
    pf = state_ref[5]
    rn2pf = rn * rn * pf
    grad_albedo = inverse * pf
    direct = factor * (3.0 * state_ref[6] - state_ref[2])
    grad_x = -factor * (state_ref[3] + sx * rn2pf)
    grad_y = -factor * (state_ref[4] + sy * rn2pf)
    before, after = shifts_cols(grad_x, columns_from(slope_low, slope_high, grad_x.shape))
    above, below = shifts_rows(grad_y)
    return direct + 0.5 * (before - after) + 0.5 * (above - below), grad_albedo


def partial_sums(depth, albedo):
    n = depth.shape[1]
    d = jnp.sum(depth * depth, axis=0, keepdims=True)
    a = jnp.sum(albedo * albedo, axis=0, keepdims=True)
    d = jnp.broadcast_to(d, (8, n))
    a = jnp.broadcast_to(a, (8, n))
    d = d + pltpu.roll(d, n // 2, 1)
    a = a + pltpu.roll(a, n // 2, 1)
    return jnp.where(iota((8, n), 1) < n // 2, d, a)[0:1]


def inverse_scales(recv_ref, row, count):
    rows = recv_ref[:, row, :]
    n = rows.shape[1]
    lane = iota(rows.shape, 1)
    d = jnp.sum(jnp.where(lane < n // 2, rows, 0.0), keepdims=True)
    a = jnp.sum(jnp.where(lane < n // 2, 0.0, rows), keepdims=True)
    return lax.rsqrt(d / count + EPS), lax.rsqrt(a / count + EPS)


def first_body(nl, tile_ref, sr_ref, strip_ref, obs0, obs1, ctx_ref, srow_ref, state_ref, pb_ref, flat_ref):
    li, _, place, count = position()
    rows, w = ctx_ref.shape[1:]
    srow_ref[...] = sr_ref[...]
    at = strip_ref.shape[0] - 8

    @pl.when(li == 0)
    def _():
        srow_ref[0:2, :] = strip_ref[at : at + 2, :]
        srow_ref[6:7, :] = strip_ref[at + 2 : at + 3, :]
        srow_ref[8:9, :] = strip_ref[at + 3 : at + 4, :]

    @pl.when(li == nl - 1)
    def _():
        srow_ref[4:6, :] = strip_ref[at : at + 2, :]
        srow_ref[7:8, :] = strip_ref[at + 2 : at + 3, :]
        srow_ref[9:10, :] = strip_ref[at + 3 : at + 4, :]

    fill_context(ctx_ref, tile_ref[0], tile_ref[1], srow_ref[1:2, :], srow_ref[4:5, :])
    total = w * count
    n = lights_of(obs0, rows)
    fill_params(pb_ref, 0, obs0, n, rows, w, place, total)
    fill_params(pb_ref, n, obs1, n, rows, w, place, total)
    chunks = [chunk_of(obs0, pb_ref, flat_ref, n), chunk_of(obs1, pb_ref, flat_ref, n, n, n)]
    sweep(ctx_ref, chunks, total, lambda at: None, state_store(state_ref, w), False)


def more_body(ctx_ref, in_ref, obs, state_ref, pb_ref, flat_ref):
    _, _, place, count = position()
    rows, w = ctx_ref.shape[1:]
    total = w * count
    fill_params(pb_ref, 0, obs, pb_ref.shape[0], rows, w, place, total)
    chunks = [chunk_of(obs, pb_ref, flat_ref, lights_of(obs, rows))]
    sweep(ctx_ref, chunks, total, state_load(in_ref, w), state_store(state_ref, w), False)


def late_body(ctx_ref, in_ref, obs, pb_ref, state_ref, flat_ref):
    _, _, _, count = position()
    rows, w = ctx_ref.shape[1:]
    n = lights_of(obs, rows)
    chunks = [chunk_of(obs, pb_ref, flat_ref, n, pb_ref.shape[0] - n)]
    sweep(ctx_ref, chunks, w * count, state_load(in_ref, w), state_store(state_ref, w), False)


def halo_slopes(pack_ref, srow_ref, rows, w):
    _, _, place, count = position()
    total = w * count
    low = halo_slope(place * w - 1, 0, pack_ref, srow_ref, rows, total)
    high = halo_slope(place * w + w, 1, pack_ref, srow_ref, rows, total)
    return low, high


def finish(state_ref, ctx_ref, albedo, valid, low, high, grad_ref, edge_ref, pay_ref):
    _, _, place, count = position()
    rows, w = ctx_ref.shape[1:]
    depth, grad_albedo = gradients(state_ref, ctx_ref, albedo, valid, low, high)
    sums = partial_sums(depth, grad_albedo)
    if edge_ref is None:
        pay_ref[...] = jnp.broadcast_to(sums[None], pay_ref.shape)
        return depth, grad_albedo
    grad_ref[0] = depth
    grad_ref[1] = grad_albedo
    dt = jnp.transpose(depth)
    at = jnp.transpose(grad_albedo)
    edge_ref[0:1, :] = dt[0:1]
    edge_ref[1:2, :] = dt[w - 1 : w]
    pay_ref[:, 0:2, :] = jnp.broadcast_to(dt[0:2][None], (count, 2, rows))
    pay_ref[:, 2:3, :] = jnp.broadcast_to(at[0:1][None], (count, 1, rows))
    pay_ref[:, 3:4, :] = jnp.broadcast_to(sums[None], (count, 1, w))

    @pl.when(place < count - 1)
    def _():
        to = exchange_index(place + 1)
        pay_ref[to, 0:2, :] = dt[w - 2 : w]
        pay_ref[to, 2:3, :] = at[w - 1 : w]

    return depth, grad_albedo


def sides_body(nl, srow_ref, direct_ref, relayed_ref, *rest):
    block_refs, (pack_ref, slope_ref) = rest[:nl], rest[nl:]
    li = lax.axis_index("light")
    w = block_refs[0].shape[1]
    rows = srow_ref.shape[1]
    n = (direct_ref.shape[0] - 8) // 2
    table = jnp.zeros((4, w), F32)
    for k in range(nl):
        halo = block_refs[k][pl.ds(lights_of(block_refs[k], rows) * rows + UNDER, 2 * n), :].astype(F32)
        beyond = (direct_ref if k < 2 else relayed_ref)[(k % 2) * n : (k % 2 + 1) * n, :]
        pack_ref[0, k * n : (k + 1) * n, :] = jnp.where(li == 0, beyond, halo[0:n])
        pack_ref[1, k * n : (k + 1) * n, :] = jnp.where(li == nl - 1, beyond, halo[n:])
        entries = jnp.concatenate([table_rows(block_refs[k], rows)] * 2, axis=0)
        table = table + (pltpu.roll(entries, k * n, 1) if k else entries)[0:4]
    tall = jnp.concatenate([table, jnp.zeros((w - 4, w), F32)], axis=0)
    pack_ref[2] = jnp.transpose(tall)[0 : nl * n]
    slope_ref[0:1, :], slope_ref[1:2, :] = halo_slopes(pack_ref, srow_ref, rows, w)


def last_body(ctx_ref, tile_ref, state_ref, slope_ref, grad_ref, edge_ref, pay_ref):
    edge_ref[...] = jnp.zeros_like(edge_ref)
    finish(
        state_ref, ctx_ref, tile_ref[1], tile_ref[2], slope_ref[0:1, :], slope_ref[1:2, :], grad_ref, edge_ref, pay_ref
    )


def second_body(nl, recv_ref, grad_ref, edge_ref, tile_ref, srow0_ref, pack_ref, *rest):
    obs_refs, pb_refs, flat_refs = rest[: nl + 1], rest[nl + 1 : 2 * nl], rest[2 * nl : 3 * nl]
    out_ref, pay_ref, ctx_ref, state_ref, srow_ref = rest[3 * nl :]
    _, _, place, count = position()
    rows, w = ctx_ref.shape[1:]
    total = w * count
    inv_depth, inv_albedo = inverse_scales(recv_ref, 3, float(rows * total))
    surface = tile_ref[0] - STEP_DEPTH * jnp.tanh(grad_ref[0] * inv_depth)
    albedo = tile_ref[1] - STEP_ALBEDO * jnp.tanh(grad_ref[1] * inv_albedo)
    out_ref[0] = surface
    out_ref[1] = albedo
    srow_ref[...] = jnp.zeros_like(srow_ref)
    srow_ref[2:4, :] = edge_ref[0:2, :]

    @pl.when(place > 0)
    def _():
        frm = exchange_index(jnp.maximum(place - 1, 0))
        srow_ref[0:2, :] = recv_ref[frm, 0:2, :]
        srow_ref[6:7, :] = recv_ref[frm, 2:3, :]

    @pl.when(place < count - 1)
    def _():
        frm = exchange_index(jnp.minimum(place + 1, count - 1))
        srow_ref[4:6, :] = recv_ref[frm, 0:2, :]
        srow_ref[7:8, :] = recv_ref[frm, 2:3, :]

    changes = srow_ref[0:8, :]
    kind = iota(changes.shape, 0) < 6
    changes = jnp.where(
        kind, STEP_DEPTH * jnp.tanh(changes * inv_depth), STEP_ALBEDO * jnp.tanh(changes * inv_albedo)
    )
    srow_ref[0:8, :] = srow0_ref[0:8, :] - changes
    srow_ref[8:16, :] = srow0_ref[8:16, :]
    fill_context(ctx_ref, surface, albedo, srow_ref[1:2, :], srow_ref[4:5, :])
    n = lights_of(obs_refs[0], rows)
    chunks = [
        chunk_of(obs_refs[0], pb_refs[0], flat_refs[0], n),
        chunk_of(obs_refs[1], pb_refs[0], flat_refs[0], n, n, n),
    ]
    chunks += [chunk_of(obs_refs[k], pb_refs[k - 1], flat_refs[k - 1], n) for k in range(2, nl - 1)]
    late = lights_of(obs_refs[nl], rows)
    chunks.append(
        chunk_of(obs_refs[nl - 1], pb_refs[-1], flat_refs[-2], n - late)
        + chunk_of(obs_refs[nl], pb_refs[-1], flat_refs[-1], late, n - late)
    )
    sweep(ctx_ref, chunks, total, lambda at: None, state_store(state_ref, w), True)
    low, high = halo_slopes(pack_ref, srow_ref, rows, w)
    depth, grad_albedo = finish(state_ref, ctx_ref, albedo, tile_ref[2], low, high, None, None, pay_ref)
    out_ref[2] = depth
    out_ref[3] = grad_albedo


def final_body(nl, recv_ref, *rest):
    parts, (depth_ref, albedo_ref) = rest[:nl], rest[nl:]
    li, _, _, count = position()
    rows, w = parts[0].shape[1:]
    inv_depth, inv_albedo = inverse_scales(recv_ref, 0, float(rows * w * count))
    for k in range(nl):
        at = pl.ds(pl.multiple_of((li ^ k) * w, w), w)
        depth_ref[:, at] = parts[k][0] - STEP_DEPTH * jnp.tanh(parts[k][2] * inv_depth)
        albedo_ref[:, at] = parts[k][1] - STEP_ALBEDO * jnp.tanh(parts[k][3] * inv_albedo)


def shape(*dims, dtype=F32):
    return jax.ShapeDtypeStruct(dims, dtype)


def program(depth_start, albedo_start, observations, light_table, valid_mask):
    nl, ns = lax.axis_size("light"), lax.axis_size("strip")
    nd = nl * ns
    lights, rows, cols = observations.shape
    w = cols // nl

    def swap(x, k):
        return lax.ppermute(x, "light", [(i, i ^ k) for i in range(nl)])

    hbm = pl.BlockSpec(memory_space=pltpu.HBM)
    field = (rows, w)
    *blocks, late, end = call(
        functools.partial(cut_body, nl),
        tuple(shape(block_rows(lights, rows, k, nl), w, dtype=jnp.bfloat16) for k in range(nl))
        + (shape(LATE * rows, w, dtype=jnp.bfloat16), shape(2 * lights, rows)),
        [
            pltpu.VMEM((4, lights), jnp.int32),
            pltpu.VMEM((nl + 2, 2 * lights, rows), F32),
            pltpu.SemaphoreType.DMA((nl * lights,)),
            pltpu.SemaphoreType.DMA((1,)),
        ],
        in_specs=[hbm] * 2,
    )(*(pltpu.with_memory_space_constraint(x, pltpu.HBM) for x in (observations, light_table.T)))
    obs2 = swap(blocks[2], 2)
    obs3 = swap(blocks[3], 3)
    obs1 = swap(blocks[1], 1)
    obs0 = blocks[0]
    tile, sr, strip = call(
        functools.partial(join_body, nl), (shape(3, *field), shape(16, rows), shape(2 * lights + 8, rows))
    )(depth_start, albedo_start, valid_mask, obs1, end)
    pairs = []
    for i in range(ns - 1):
        for l in range(nl):
            source, target = (i, i + 1) if l % 2 == 0 else (i + 1, i)
            pairs.append((l * ns + source, l * ns + target))
    direct = lax.ppermute(strip, AXES, pairs)
    relayed = swap(direct, 2)
    late = swap(late, 3)

    def tiles(n):
        return shape(n, 5, 8, w)

    ctx, srow, state, pb0, flat0 = call(
        functools.partial(first_body, nl),
        (shape(4, *field), shape(16, rows), shape(7, *field), tiles(2 * lights), shape(2 * lights, *field)),
    )(tile, sr, direct, obs0, obs1)
    early = lights - LATE
    state, pb2, flat2 = call(more_body, (shape(7, *field), tiles(lights), shape(lights, *field)))(ctx, state, obs2)
    state, pb3, flat3 = call(more_body, (shape(7, *field), tiles(lights), shape(early, *field)))(ctx, state, obs3)
    pack, slope = call(
        functools.partial(sides_body, nl), (shape(3, nl * lights, rows), shape(8, rows))
    )(srow, direct, relayed, obs0, obs1, obs2, obs3)
    state, flat4 = call(late_body, (shape(7, *field), shape(LATE, *field)))(ctx, state, late, pb3)
    grad, edge, pay = call(last_body, (shape(2, *field), shape(8, rows), shape(nd, 4, rows)))(ctx, tile, state, slope)
    recv = lax.all_to_all(pay, AXES, 0, 0, tiled=True)
    own, pay = call(
        functools.partial(second_body, nl),
        (shape(4, *field), shape(nd, 1, rows)),
        [
            pltpu.VMEM((4, *field), F32),
            pltpu.VMEM((7, *field), F32),
            pltpu.VMEM((16, rows), F32),
        ],
    )(recv, grad, edge, tile, srow, pack, obs0, obs1, obs2, obs3, late, pb0, pb2, pb3, flat0, flat2, flat3, flat4)
    part2 = swap(own, 2)
    part1 = swap(own, 1)
    recv = lax.all_to_all(pay, AXES, 0, 0, tiled=True)
    recv, part2 = lax.optimization_barrier((recv, part2))
    part3 = swap(part2, 1)
    return tuple(
        call(functools.partial(final_body, nl), (shape(rows, cols), shape(rows, cols)))(recv, own, part1, part2, part3)
    )


def solution(mesh):
    in_specs = (
        P(None, "strip"),
        P(None, "strip"),
        P("light", None, "strip"),
        P("light", None),
        P(None, "strip"),
    )
    out_specs = (P(None, "strip"), P(None, "strip"))
    return jax.shard_map(program, mesh=mesh, in_specs=in_specs, out_specs=out_specs, check_vma=False)
```

```python
import functools
import math

import jax
import jax.numpy as jnp
from jax import lax
from jax.experimental import pallas as pl
from jax.experimental.pallas import tpu as pltpu
from jax.sharding import PartitionSpec as P


AXES = ("light", "strip")
STEP_DEPTH = 0.1
STEP_ALBEDO = 0.2
EPS = 1e-06
HALF_LOG2E = 0.5 * math.log2(math.e)
F32 = jnp.float32
VM = pl.BlockSpec(memory_space=pltpu.VMEM)
TR = 16


def iota(shape, dim):
    return lax.broadcasted_iota(jnp.int32, shape, dim)


def position():
    nl, ns = lax.axis_size("light"), lax.axis_size("strip")
    li, si = lax.axis_index("light"), lax.axis_index("strip")
    return li, si, si * nl + li, nl * ns


def exchange_index(place):
    nl, ns = lax.axis_size("light"), lax.axis_size("strip")
    return lax.rem(place, nl) * ns + lax.div(place, nl)


def call(body, out, scratch=(), vmem=40 << 20, **more):
    return pl.pallas_call(
        body,
        out_shape=out,
        scratch_shapes=list(scratch),
        compiler_params=pltpu.CompilerParams(vmem_limit_bytes=vmem),
        **more,
    )


UNDER = 16
LATE = 3


def block_rows(lights, rows, k, nl):
    here = lights - LATE if k == nl - 1 else lights
    return here * rows + UNDER + 2 * lights + (2 * lights if k == 1 else 0)


def cut_body(nl, obs_ref, table_ref, *rest):
    blocks, (late_ref, end_ref, table, eh_ref, sems, extra) = rest[:nl], rest[nl:]
    lights, rows, cols = obs_ref.shape
    w = cols // nl
    li = lax.axis_index("light")
    here = [lights_of(block, rows) for block in blocks]

    def slot(k, l):
        if l < here[k]:
            return blocks[k].at[pl.ds(l * rows, rows)]
        return late_ref.at[pl.ds((l - here[k]) * rows, rows)]

    copies = []
    for k in (2, 3, 1, 0):
        for l in range(lights):
            at = pl.ds(pl.multiple_of((li ^ k) * w, w), w)
            copies.append(pltpu.make_async_copy(obs_ref.at[l, :, at], slot(k, l), sems.at[k * lights + l]))
            copies[-1].start()
    fetch = pltpu.make_async_copy(table_ref, table, extra.at[0])
    fetch.start()
    eh_ref[...] = jnp.zeros_like(eh_ref)
    at, col = iota((8, w), 0), iota((8, w), 1)
    pick = (((at == 0) & (col == 0)) | ((at == 1) & (col == w - 1))).astype(jnp.bfloat16)
    fetch.wait()
    entries = table[...]
    high = lax.shift_right_logical(entries, 5)
    both = jnp.concatenate([high, entries - high * 32], axis=0).astype(F32)
    wide = jnp.concatenate([both, jnp.zeros((8, w - lights), F32)], axis=1)
    under = jnp.concatenate([wide, jnp.zeros((UNDER - 8, w), F32)], axis=0).astype(jnp.bfloat16)
    for k in range(nl):
        blocks[k][pl.ds(here[k] * rows, UNDER), :] = under
    for copy in copies:
        copy.wait()
    for k in range(nl):
        q = li ^ k
        for l in range(lights):
            e = lax.dot_general(
                pick,
                slot(k, l)[...],
                (((1,), (1,)), ((), ())),
                preferred_element_type=F32,
            )
            eh_ref[q, lights + l : lights + l + 1, :] = e[0:1]
            eh_ref[q + 2, l : l + 1, :] = e[1:2]
    ends = jnp.concatenate([eh_ref[nl + 1, 0:lights, :], eh_ref[0, lights:, :]], axis=0)
    end_ref[...] = ends
    for k in range(nl):
        halo = pl.ds(here[k] * rows + UNDER, 2 * lights)
        blocks[k][halo, :] = eh_ref[(li ^ k) + 1].astype(jnp.bfloat16)
    blocks[1][pl.ds(lights * rows + UNDER + 2 * lights, 2 * lights), :] = ends.astype(jnp.bfloat16)


def join_body(nl, depth_ref, albedo_ref, valid_ref, block_ref, end_ref, tile_ref, sr_ref, out_ref):
    rows, w = tile_ref.shape[1:]
    n = end_ref.shape[0] // 2
    li = lax.axis_index("light")
    right = lax.rem(li, 2) == 0
    other = block_ref[pl.ds(block_ref.shape[0] - 2 * n, 2 * n), :].astype(F32)
    out_ref[0:n, :] = jnp.where(right, end_ref[0:n, :], end_ref[n:, :])
    out_ref[n : 2 * n, :] = jnp.where(right, other[0:n], other[n:])
    out_ref[2 * n :, :] = jnp.zeros((8, rows), F32)
    sr_ref[...] = jnp.zeros_like(sr_ref)
    lane = iota((rows, w), 1)

    def columns(ref, q):
        return ref[:, pl.ds(pl.multiple_of(q * w, w), w)].astype(F32)

    for f, ref in enumerate((depth_ref, albedo_ref, valid_ref)):
        own = columns(ref, li)
        before = columns(ref, jnp.maximum(li - 1, 0))
        after = columns(ref, jnp.minimum(li + 1, nl - 1))
        tile_ref[f] = own
        inner = jnp.transpose(own)
        outer = jnp.transpose(jnp.where(lane < w // 2, after, before))
        edge = jnp.transpose(columns(ref, jnp.where(right, nl - 1, 0)))
        low = jnp.where(li == 0, 0.0, outer[w - 2 : w])
        high = jnp.where(li == nl - 1, 0.0, outer[0:2])
        if f == 0:
            sr_ref[0:2, :] = low
            sr_ref[2:3, :] = inner[0:1]
            sr_ref[3:4, :] = inner[w - 1 : w]
            sr_ref[4:6, :] = high
            out_ref[2 * n : 2 * n + 2, :] = jnp.where(right, edge[w - 2 : w], edge[0:2])
        else:
            at = 4 + 2 * f
            sr_ref[at : at + 1, :] = low[1:2]
            sr_ref[at + 1 : at + 2, :] = high[0:1]
            at = 2 * n + 1 + f
            out_ref[at : at + 1, :] = jnp.where(right, edge[w - 1 : w], edge[0:1])


def decode(table):
    return (
        table[:, 0:1] / 500.0 - 1.0,
        table[:, 1:2] / 500.0 - 1.0,
        1.0 + table[:, 2:3] / 1000.0,
        0.5 + table[:, 3:4] / 1000.0,
    )


def decode_rows(table):
    return (
        table[0:1] / 500.0 - 1.0,
        table[1:2] / 500.0 - 1.0,
        1.0 + table[2:3] / 1000.0,
        0.5 + table[3:4] / 1000.0,
    )


def columns_from(left, right, shape):
    rows, w = shape
    at = iota((w, rows), 0)
    return jnp.transpose(jnp.where(at == 0, left, jnp.where(at == w - 1, right, 0.0)))


def shifts_rows(x):
    r = iota(x.shape, 0)
    n = x.shape[0]
    above = jnp.where(r == 0, 0.0, pltpu.roll(x, 1, 0))
    below = jnp.where(r == n - 1, 0.0, pltpu.roll(x, n - 1, 0))
    return above, below


def shifts_cols(x, ends):
    c = iota(x.shape, 1)
    n = x.shape[1]
    before = jnp.where(c == 0, ends, pltpu.roll(x, 1, 1))
    after = jnp.where(c == n - 1, ends, pltpu.roll(x, n - 1, 1))
    return before, after


def fill_context(ctx_ref, surface, albedo, left, right):
    ends = columns_from(left, right, surface.shape)
    before, after = shifts_cols(surface, ends)
    above, below = shifts_rows(surface)
    sx = 0.5 * (after - before)
    sy = 0.5 * (below - above)
    ctx_ref[0] = surface
    ctx_ref[1] = sx
    ctx_ref[2] = sy
    ctx_ref[3] = albedo * lax.rsqrt(1.0 + sx * sx + sy * sy)


def lights_of(block_ref, rows):
    return block_ref.shape[0] // rows


def table_rows(block_ref, rows):
    under = block_ref[pl.ds(lights_of(block_ref, rows) * rows, UNDER), :].astype(F32)
    return under[0:4] * 32.0 + under[4:8]


def fill_params(pb_ref, base, block_ref, n, rows, w, place, total):
    lx, ly, lz, le = decode_rows(table_rows(block_ref, rows))
    col = iota((8, w), 1) + place * w
    px = (col.astype(F32) + 0.5) / total - 0.5
    for j in range(n):
        dx = jnp.broadcast_to(lx[:, j : j + 1], (8, w)) - px
        pb_ref[base + j, 0] = dx
        pb_ref[base + j, 1] = dx * dx
        pb_ref[base + j, 2] = jnp.broadcast_to(ly[:, j : j + 1], (8, w))
        pb_ref[base + j, 3] = jnp.broadcast_to(lz[:, j : j + 1], (8, w))
        pb_ref[base + j, 4] = jnp.broadcast_to(le[:, j : j + 1], (8, w))


def accumulate(state, tile, py, lights):
    surface, sx, sy, scaled = tile
    kept = []
    least = None
    for obs, pb, across in lights:
        dx = pb(0)
        dy = pb(2) - py
        dz = pb(3) - surface
        flat = across(None)
        if flat is None:
            flat = pb(1) + dy * dy
            across(flat)
        dist = flat + dz * dz
        facing = dz - (sx * dx + sy * dy)
        r = lax.rsqrt(dist)
        r2 = r * r
        g = (r2 * r) * pb(4)
        residual = scaled * (g * facing) - obs
        square = residual * residual
        least = square if least is None else jnp.minimum(least, square)
        kept.append((square, residual * g, facing, dz * r2, dx, dy))
    if state is not None:
        before = state[0]
        least = jnp.minimum(least, before)
    sums = None
    for square, q, facing, drop, dx, dy in kept:
        w = jnp.exp2((least - square) * HALF_LOG2E)
        p = w * q
        pf = p * facing
        terms = (w, p, p * dx, p * dy, pf, pf * drop)
        sums = terms if sums is None else tuple(a + b for a, b in zip(sums, terms))
    if state is not None:
        fade = jnp.exp2((least - before) * HALF_LOG2E)
        sums = tuple(a * fade + b for a, b in zip(state[1:], sums))
    return (least,) + sums


def sweep(ctx_ref, chunks, total, load, store, known):
    rows, w = ctx_ref.shape[1:]
    split = (TR // 8, 8, w)

    def step(i, carry):
        at = pl.ds(pl.multiple_of(i * TR, TR), TR)
        tile = tuple(ctx_ref[f, at, :].reshape(split) for f in range(4))
        row = iota(split, 0) * 8 + iota(split, 1) + i * TR
        py = (row.astype(F32) + (0.5 - rows / 2.0)) / total

        def light(entry):
            (obs_ref, j), (pb_ref, p), (flat_ref, f) = entry
            obs = obs_ref[pl.ds(pl.multiple_of(j * rows + i * TR, TR), TR), :].astype(F32).reshape(split)

            def across(value):
                if known:
                    return flat_ref[f, at, :].reshape(split)
                if value is not None:
                    flat_ref[f, at, :] = value.reshape(TR, w)
                return None

            return obs, lambda field: pb_ref[p, field], across

        state = load(at)
        for chunk in chunks:
            state = accumulate(state, tile, py, [light(entry) for entry in chunk])
        store(at, state)
        return carry

    lax.fori_loop(0, rows // TR, step, 0)


def chunk_of(obs_ref, pb_ref, flat_ref, count, pb_at=0, flat_at=0):
    return [((obs_ref, j), (pb_ref, pb_at + j), (flat_ref, flat_at + j)) for j in range(count)]


def state_load(state_ref, w):
    return lambda at: tuple(state_ref[f, at, :].reshape(TR // 8, 8, w) for f in range(7))


def state_store(state_ref, w):
    def store(at, state):
        for f in range(7):
            state_ref[f, at, :] = state[f].reshape(TR, w)

    return store


def halo_slope(column, side, pack_ref, srow_ref, rows, total):
    obs = pack_ref[side]
    lx, ly, lz, le = decode(pack_ref[2])
    outer, inner = (0, 2) if side == 0 else (5, 3)
    here = 1 if side == 0 else 4
    surface = srow_ref[here : here + 1, :]
    toward = srow_ref[inner : inner + 1, :] - srow_ref[outer : outer + 1, :]
    sx = 0.5 * toward if side == 0 else -0.5 * toward
    lane = iota((8, rows), 1)
    wide = jnp.broadcast_to(surface, (8, rows))
    above = jnp.where(lane == 0, 0.0, pltpu.roll(wide, 1, 1))
    below = jnp.where(lane == rows - 1, 0.0, pltpu.roll(wide, rows - 1, 1))
    sy = (0.5 * (below - above))[0:1]
    albedo = srow_ref[6 + side : 7 + side, :]
    valid = srow_ref[8 + side : 9 + side, :]
    px = (column.astype(F32) + 0.5) / total - 0.5
    py = (iota((1, rows), 1).astype(F32) + (0.5 - rows / 2.0)) / total
    rn = lax.rsqrt(1.0 + sx * sx + sy * sy)
    dx = jnp.broadcast_to(lx - px, obs.shape)
    dy = ly - py
    dz = lz - surface
    dist = dx * dx + dy * dy + dz * dz
    facing = dz - (sx * dx + sy * dy)
    r = lax.rsqrt(dist)
    g = (r * r) * r * le
    residual = (albedo * rn) * (g * facing) - obs
    square = residual * residual
    least = jnp.min(square, axis=0, keepdims=True)
    w = jnp.exp2((least - square) * HALF_LOG2E)
    p = w * residual * g
    total_w = jnp.sum(w, axis=0, keepdims=True)
    px_sum = jnp.sum(p * dx, axis=0, keepdims=True)
    pf_sum = jnp.sum(p * facing, axis=0, keepdims=True)
    return -(valid * albedo * rn / total_w) * (px_sum + (sx * rn * rn) * pf_sum)


def gradients(state_ref, ctx_ref, albedo, valid, slope_low, slope_high):
    sx, sy = ctx_ref[1], ctx_ref[2]
    rn = lax.rsqrt(1.0 + sx * sx + sy * sy)
    inverse = valid * rn / state_ref[1]
    factor = inverse * albedo
    pf = state_ref[5]
    rn2pf = rn * rn * pf
    grad_albedo = inverse * pf
    direct = factor * (3.0 * state_ref[6] - state_ref[2])
    grad_x = -factor * (state_ref[3] + sx * rn2pf)
    grad_y = -factor * (state_ref[4] + sy * rn2pf)
    before, after = shifts_cols(grad_x, columns_from(slope_low, slope_high, grad_x.shape))
    above, below = shifts_rows(grad_y)
    return direct + 0.5 * (before - after) + 0.5 * (above - below), grad_albedo


def partial_sums(depth, albedo):
    n = depth.shape[1]
    d = jnp.sum(depth * depth, axis=0, keepdims=True)
    a = jnp.sum(albedo * albedo, axis=0, keepdims=True)
    d = jnp.broadcast_to(d, (8, n))
    a = jnp.broadcast_to(a, (8, n))
    d = d + pltpu.roll(d, n // 2, 1)
    a = a + pltpu.roll(a, n // 2, 1)
    return jnp.where(iota((8, n), 1) < n // 2, d, a)[0:1]


def inverse_scales(recv_ref, row, count):
    rows = recv_ref[:, row, :]
    n = rows.shape[1]
    lane = iota(rows.shape, 1)
    d = jnp.sum(jnp.where(lane < n // 2, rows, 0.0), keepdims=True)
    a = jnp.sum(jnp.where(lane < n // 2, 0.0, rows), keepdims=True)
    return lax.rsqrt(d / count + EPS), lax.rsqrt(a / count + EPS)


def first_body(nl, tile_ref, sr_ref, strip_ref, obs0, obs1, ctx_ref, srow_ref, state_ref, pb_ref, flat_ref):
    li, _, place, count = position()
    rows, w = ctx_ref.shape[1:]
    srow_ref[...] = sr_ref[...]
    at = strip_ref.shape[0] - 8

    @pl.when(li == 0)
    def _():
        srow_ref[0:2, :] = strip_ref[at : at + 2, :]
        srow_ref[6:7, :] = strip_ref[at + 2 : at + 3, :]
        srow_ref[8:9, :] = strip_ref[at + 3 : at + 4, :]

    @pl.when(li == nl - 1)
    def _():
        srow_ref[4:6, :] = strip_ref[at : at + 2, :]
        srow_ref[7:8, :] = strip_ref[at + 2 : at + 3, :]
        srow_ref[9:10, :] = strip_ref[at + 3 : at + 4, :]

    fill_context(ctx_ref, tile_ref[0], tile_ref[1], srow_ref[1:2, :], srow_ref[4:5, :])
    total = w * count
    n = lights_of(obs0, rows)
    fill_params(pb_ref, 0, obs0, n, rows, w, place, total)
    fill_params(pb_ref, n, obs1, n, rows, w, place, total)
    chunks = [chunk_of(obs0, pb_ref, flat_ref, n), chunk_of(obs1, pb_ref, flat_ref, n, n, n)]
    sweep(ctx_ref, chunks, total, lambda at: None, state_store(state_ref, w), False)


def more_body(ctx_ref, in_ref, obs, state_ref, pb_ref, flat_ref):
    _, _, place, count = position()
    rows, w = ctx_ref.shape[1:]
    total = w * count
    fill_params(pb_ref, 0, obs, pb_ref.shape[0], rows, w, place, total)
    chunks = [chunk_of(obs, pb_ref, flat_ref, lights_of(obs, rows))]
    sweep(ctx_ref, chunks, total, state_load(in_ref, w), state_store(state_ref, w), False)


def late_body(ctx_ref, in_ref, obs, pb_ref, state_ref, flat_ref):
    _, _, _, count = position()
    rows, w = ctx_ref.shape[1:]
    n = lights_of(obs, rows)
    chunks = [chunk_of(obs, pb_ref, flat_ref, n, pb_ref.shape[0] - n)]
    sweep(ctx_ref, chunks, w * count, state_load(in_ref, w), state_store(state_ref, w), False)


def halo_slopes(pack_ref, srow_ref, rows, w):
    _, _, place, count = position()
    total = w * count
    low = halo_slope(place * w - 1, 0, pack_ref, srow_ref, rows, total)
    high = halo_slope(place * w + w, 1, pack_ref, srow_ref, rows, total)
    return low, high


def finish(state_ref, ctx_ref, albedo, valid, low, high, grad_ref, edge_ref, pay_ref):
    _, _, place, count = position()
    rows, w = ctx_ref.shape[1:]
    depth, grad_albedo = gradients(state_ref, ctx_ref, albedo, valid, low, high)
    sums = partial_sums(depth, grad_albedo)
    if edge_ref is None:
        pay_ref[...] = jnp.broadcast_to(sums[None], pay_ref.shape)
        return depth, grad_albedo
    grad_ref[0] = depth
    grad_ref[1] = grad_albedo
    dt = jnp.transpose(depth)
    at = jnp.transpose(grad_albedo)
    edge_ref[0:1, :] = dt[0:1]
    edge_ref[1:2, :] = dt[w - 1 : w]
    pay_ref[:, 0:2, :] = jnp.broadcast_to(dt[0:2][None], (count, 2, rows))
    pay_ref[:, 2:3, :] = jnp.broadcast_to(at[0:1][None], (count, 1, rows))
    pay_ref[:, 3:4, :] = jnp.broadcast_to(sums[None], (count, 1, w))

    @pl.when(place < count - 1)
    def _():
        to = exchange_index(place + 1)
        pay_ref[to, 0:2, :] = dt[w - 2 : w]
        pay_ref[to, 2:3, :] = at[w - 1 : w]

    return depth, grad_albedo


def sides_body(nl, srow_ref, direct_ref, relayed_ref, *rest):
    block_refs, (pack_ref, slope_ref) = rest[:nl], rest[nl:]
    li = lax.axis_index("light")
    w = block_refs[0].shape[1]
    rows = srow_ref.shape[1]
    n = (direct_ref.shape[0] - 8) // 2
    table = jnp.zeros((4, w), F32)
    for k in range(nl):
        halo = block_refs[k][pl.ds(lights_of(block_refs[k], rows) * rows + UNDER, 2 * n), :].astype(F32)
        beyond = (direct_ref if k < 2 else relayed_ref)[(k % 2) * n : (k % 2 + 1) * n, :]
        pack_ref[0, k * n : (k + 1) * n, :] = jnp.where(li == 0, beyond, halo[0:n])
        pack_ref[1, k * n : (k + 1) * n, :] = jnp.where(li == nl - 1, beyond, halo[n:])
        entries = jnp.concatenate([table_rows(block_refs[k], rows)] * 2, axis=0)
        table = table + (pltpu.roll(entries, k * n, 1) if k else entries)[0:4]
    tall = jnp.concatenate([table, jnp.zeros((w - 4, w), F32)], axis=0)
    pack_ref[2] = jnp.transpose(tall)[0 : nl * n]
    slope_ref[0:1, :], slope_ref[1:2, :] = halo_slopes(pack_ref, srow_ref, rows, w)


def last_body(ctx_ref, tile_ref, state_ref, slope_ref, grad_ref, edge_ref, pay_ref):
    edge_ref[...] = jnp.zeros_like(edge_ref)
    finish(
        state_ref, ctx_ref, tile_ref[1], tile_ref[2], slope_ref[0:1, :], slope_ref[1:2, :], grad_ref, edge_ref, pay_ref
    )


def second_body(nl, recv_ref, grad_ref, edge_ref, tile_ref, srow0_ref, pack_ref, *rest):
    obs_refs, pb_refs, flat_refs = rest[: nl + 1], rest[nl + 1 : 2 * nl], rest[2 * nl : 3 * nl]
    out_ref, pay_ref, ctx_ref, state_ref, srow_ref = rest[3 * nl :]
    _, _, place, count = position()
    rows, w = ctx_ref.shape[1:]
    total = w * count
    inv_depth, inv_albedo = inverse_scales(recv_ref, 3, float(rows * total))
    surface = tile_ref[0] - STEP_DEPTH * jnp.tanh(grad_ref[0] * inv_depth)
    albedo = tile_ref[1] - STEP_ALBEDO * jnp.tanh(grad_ref[1] * inv_albedo)
    out_ref[0] = surface
    out_ref[1] = albedo
    srow_ref[...] = jnp.zeros_like(srow_ref)
    srow_ref[2:4, :] = edge_ref[0:2, :]

    @pl.when(place > 0)
    def _():
        frm = exchange_index(jnp.maximum(place - 1, 0))
        srow_ref[0:2, :] = recv_ref[frm, 0:2, :]
        srow_ref[6:7, :] = recv_ref[frm, 2:3, :]

    @pl.when(place < count - 1)
    def _():
        frm = exchange_index(jnp.minimum(place + 1, count - 1))
        srow_ref[4:6, :] = recv_ref[frm, 0:2, :]
        srow_ref[7:8, :] = recv_ref[frm, 2:3, :]

    changes = srow_ref[0:8, :]
    kind = iota(changes.shape, 0) < 6
    changes = jnp.where(
        kind, STEP_DEPTH * jnp.tanh(changes * inv_depth), STEP_ALBEDO * jnp.tanh(changes * inv_albedo)
    )
    srow_ref[0:8, :] = srow0_ref[0:8, :] - changes
    srow_ref[8:16, :] = srow0_ref[8:16, :]
    fill_context(ctx_ref, surface, albedo, srow_ref[1:2, :], srow_ref[4:5, :])
    n = lights_of(obs_refs[0], rows)
    chunks = [
        chunk_of(obs_refs[0], pb_refs[0], flat_refs[0], n),
        chunk_of(obs_refs[1], pb_refs[0], flat_refs[0], n, n, n),
    ]
    chunks += [chunk_of(obs_refs[k], pb_refs[k - 1], flat_refs[k - 1], n) for k in range(2, nl - 1)]
    late = lights_of(obs_refs[nl], rows)
    chunks.append(
        chunk_of(obs_refs[nl - 1], pb_refs[-1], flat_refs[-2], n - late)
        + chunk_of(obs_refs[nl], pb_refs[-1], flat_refs[-1], late, n - late)
    )
    sweep(ctx_ref, chunks, total, lambda at: None, state_store(state_ref, w), True)
    low, high = halo_slopes(pack_ref, srow_ref, rows, w)
    depth, grad_albedo = finish(state_ref, ctx_ref, albedo, tile_ref[2], low, high, None, None, pay_ref)
    out_ref[2] = depth
    out_ref[3] = grad_albedo


def hop_body(in_ref, out_ref):
    out_ref[...] = in_ref[...]


def final_body(nl, recv_ref, *rest):
    parts, (depth_ref, albedo_ref) = rest[:nl], rest[nl:]
    li, _, _, count = position()
    rows, w = parts[0].shape[1:]
    inv_depth, inv_albedo = inverse_scales(recv_ref, 0, float(rows * w * count))
    for k in range(nl):
        at = pl.ds(pl.multiple_of((li ^ k) * w, w), w)
        depth_ref[:, at] = parts[k][0] - STEP_DEPTH * jnp.tanh(parts[k][2] * inv_depth)
        albedo_ref[:, at] = parts[k][1] - STEP_ALBEDO * jnp.tanh(parts[k][3] * inv_albedo)


def shape(*dims, dtype=F32):
    return jax.ShapeDtypeStruct(dims, dtype)


def program(depth_start, albedo_start, observations, light_table, valid_mask):
    nl, ns = lax.axis_size("light"), lax.axis_size("strip")
    nd = nl * ns
    lights, rows, cols = observations.shape
    w = cols // nl

    def swap(x, k):
        return lax.ppermute(x, "light", [(i, i ^ k) for i in range(nl)])

    hbm = pl.BlockSpec(memory_space=pltpu.HBM)
    field = (rows, w)
    *blocks, late, end = call(
        functools.partial(cut_body, nl),
        tuple(shape(block_rows(lights, rows, k, nl), w, dtype=jnp.bfloat16) for k in range(nl))
        + (shape(LATE * rows, w, dtype=jnp.bfloat16), shape(2 * lights, rows)),
        [
            pltpu.VMEM((4, lights), jnp.int32),
            pltpu.VMEM((nl + 2, 2 * lights, rows), F32),
            pltpu.SemaphoreType.DMA((nl * lights,)),
            pltpu.SemaphoreType.DMA((1,)),
        ],
        in_specs=[hbm] * 2,
    )(*(pltpu.with_memory_space_constraint(x, pltpu.HBM) for x in (observations, light_table.T)))
    obs2 = swap(blocks[2], 2)
    obs3 = swap(blocks[3], 3)
    obs1 = swap(blocks[1], 1)
    obs0 = blocks[0]
    tile, sr, strip = call(
        functools.partial(join_body, nl), (shape(3, *field), shape(16, rows), shape(2 * lights + 8, rows))
    )(depth_start, albedo_start, valid_mask, obs1, end)
    pairs = []
    for i in range(ns - 1):
        for l in range(nl):
            source, target = (i, i + 1) if l % 2 == 0 else (i + 1, i)
            pairs.append((l * ns + source, l * ns + target))
    direct = lax.ppermute(strip, AXES, pairs)
    relayed = swap(direct, 2)
    late = swap(late, 3)

    def tiles(n):
        return shape(n, 5, 8, w)

    ctx, srow, state, pb0, flat0 = call(
        functools.partial(first_body, nl),
        (shape(4, *field), shape(16, rows), shape(7, *field), tiles(2 * lights), shape(2 * lights, *field)),
    )(tile, sr, direct, obs0, obs1)
    early = lights - LATE
    state, pb2, flat2 = call(more_body, (shape(7, *field), tiles(lights), shape(lights, *field)))(ctx, state, obs2)
    state, pb3, flat3 = call(more_body, (shape(7, *field), tiles(lights), shape(early, *field)))(ctx, state, obs3)
    pack, slope = call(
        functools.partial(sides_body, nl), (shape(3, nl * lights, rows), shape(8, rows))
    )(srow, direct, relayed, obs0, obs1, obs2, obs3)
    state, flat4 = call(late_body, (shape(7, *field), shape(LATE, *field)))(ctx, state, late, pb3)
    grad, edge, pay = call(last_body, (shape(2, *field), shape(8, rows), shape(nd, 4, rows)))(ctx, tile, state, slope)
    recv = lax.all_to_all(pay, AXES, 0, 0, tiled=True)
    own, pay = call(
        functools.partial(second_body, nl),
        (shape(4, *field), shape(nd, 1, rows)),
        [
            pltpu.VMEM((4, *field), F32),
            pltpu.VMEM((7, *field), F32),
            pltpu.VMEM((16, rows), F32),
        ],
    )(recv, grad, edge, tile, srow, pack, obs0, obs1, obs2, obs3, late, pb0, pb2, pb3, flat0, flat2, flat3, flat4)
    part2 = swap(own, 2)
    part1 = swap(own, 1)
    recv = lax.all_to_all(pay, AXES, 0, 0, tiled=True)
    part3 = swap(call(hop_body, shape(4, *field))(part2), 1)
    return tuple(
        call(functools.partial(final_body, nl), (shape(rows, cols), shape(rows, cols)))(recv, own, part1, part2, part3)
    )


def solution(mesh):
    in_specs = (
        P(None, "strip"),
        P(None, "strip"),
        P("light", None, "strip"),
        P("light", None),
        P(None, "strip"),
    )
    out_specs = (P(None, "strip"), P(None, "strip"))
    return jax.shard_map(program, mesh=mesh, in_specs=in_specs, out_specs=out_specs, check_vma=False)
```

```python
import functools
import math

import jax
import jax.numpy as jnp
from jax import lax
from jax.experimental import pallas as pl
from jax.experimental.pallas import tpu as pltpu
from jax.sharding import PartitionSpec as P


AXES = ("light", "strip")
STEP_DEPTH = 0.1
STEP_ALBEDO = 0.2
EPS = 1e-06
HALF_LOG2E = 0.5 * math.log2(math.e)
F32 = jnp.float32
VM = pl.BlockSpec(memory_space=pltpu.VMEM)
TR = 16


def iota(shape, dim):
    return lax.broadcasted_iota(jnp.int32, shape, dim)


def position():
    nl, ns = lax.axis_size("light"), lax.axis_size("strip")
    li, si = lax.axis_index("light"), lax.axis_index("strip")
    return li, si, si * nl + li, nl * ns


def exchange_index(place):
    nl, ns = lax.axis_size("light"), lax.axis_size("strip")
    return lax.rem(place, nl) * ns + lax.div(place, nl)


def call(body, out, scratch=(), vmem=40 << 20, **more):
    return pl.pallas_call(
        body,
        out_shape=out,
        scratch_shapes=list(scratch),
        compiler_params=pltpu.CompilerParams(vmem_limit_bytes=vmem),
        **more,
    )


UNDER = 16
LATE = 3


def block_rows(lights, rows, k, nl):
    here = lights - LATE if k == nl - 1 else lights
    return here * rows + UNDER + 2 * lights + (2 * lights if k == 1 else 0)


def cut_body(nl, obs_ref, table_ref, *rest):
    blocks, (late_ref, end_ref, table, eh_ref, sems, extra) = rest[:nl], rest[nl:]
    lights, rows, cols = obs_ref.shape
    w = cols // nl
    li = lax.axis_index("light")
    here = [lights_of(block, rows) for block in blocks]

    copies = []
    for k in (2, 3, 1, 0):
        at = pl.ds(pl.multiple_of((li ^ k) * w, w), w)
        groups = [(0, here[k], blocks[k])]
        if here[k] < lights:
            groups.append((here[k], lights - here[k], late_ref))
        for start, size, ref in groups:
            target = ref.at[pl.ds(0, size * rows)].reshape(size, rows, w)
            copies.append(
                pltpu.make_async_copy(obs_ref.at[pl.ds(start, size), :, at], target, sems.at[len(copies)])
            )
            copies[-1].start()
    fetch = pltpu.make_async_copy(table_ref, table, extra.at[0])
    fetch.start()
    eh_ref[...] = jnp.zeros_like(eh_ref)
    at, col = iota((2 * lights, lights * w), 0), iota((2 * lights, lights * w), 1)
    pick = (col == jnp.where(at < lights, at * w + w - 1, (at - lights) * w)).astype(jnp.bfloat16)
    fetch.wait()
    entries = table[...]
    high = lax.shift_right_logical(entries, 5)
    both = jnp.concatenate([high, entries - high * 32], axis=0).astype(F32)
    wide = jnp.concatenate([both, jnp.zeros((8, w - lights), F32)], axis=1)
    under = jnp.concatenate([wide, jnp.zeros((UNDER - 8, w), F32)], axis=0).astype(jnp.bfloat16)
    for k in range(nl):
        blocks[k][pl.ds(here[k] * rows, UNDER), :] = under
    for copy in copies:
        copy.wait()
    for k in range(nl):
        q = li ^ k
        side_by_side = [blocks[k][pl.ds(l * rows, rows), :] for l in range(here[k])]
        side_by_side += [late_ref[pl.ds(l * rows, rows), :] for l in range(lights - here[k])]
        e = lax.dot_general(
            pick,
            jnp.concatenate(side_by_side, axis=1),
            (((1,), (1,)), ((), ())),
            preferred_element_type=F32,
        )
        eh_ref[q, lights:, :] = e[lights:]
        eh_ref[q + 2, 0:lights, :] = e[0:lights]
    ends = jnp.concatenate([eh_ref[nl + 1, 0:lights, :], eh_ref[0, lights:, :]], axis=0)
    end_ref[...] = ends
    for k in range(nl):
        halo = pl.ds(here[k] * rows + UNDER, 2 * lights)
        blocks[k][halo, :] = eh_ref[(li ^ k) + 1].astype(jnp.bfloat16)
    blocks[1][pl.ds(lights * rows + UNDER + 2 * lights, 2 * lights), :] = ends.astype(jnp.bfloat16)


def join_body(nl, depth_ref, albedo_ref, valid_ref, block_ref, end_ref, tile_ref, sr_ref, out_ref):
    rows, w = tile_ref.shape[1:]
    n = end_ref.shape[0] // 2
    li = lax.axis_index("light")
    right = lax.rem(li, 2) == 0
    other = block_ref[pl.ds(block_ref.shape[0] - 2 * n, 2 * n), :].astype(F32)
    out_ref[0:n, :] = jnp.where(right, end_ref[0:n, :], end_ref[n:, :])
    out_ref[n : 2 * n, :] = jnp.where(right, other[0:n], other[n:])
    out_ref[2 * n :, :] = jnp.zeros((8, rows), F32)
    sr_ref[...] = jnp.zeros_like(sr_ref)
    lane = iota((rows, w), 1)

    def columns(ref, q):
        return ref[:, pl.ds(pl.multiple_of(q * w, w), w)].astype(F32)

    for f, ref in enumerate((depth_ref, albedo_ref, valid_ref)):
        own = columns(ref, li)
        before = columns(ref, jnp.maximum(li - 1, 0))
        after = columns(ref, jnp.minimum(li + 1, nl - 1))
        tile_ref[f] = own
        inner = jnp.transpose(own)
        outer = jnp.transpose(jnp.where(lane < w // 2, after, before))
        edge = jnp.transpose(columns(ref, jnp.where(right, nl - 1, 0)))
        low = jnp.where(li == 0, 0.0, outer[w - 2 : w])
        high = jnp.where(li == nl - 1, 0.0, outer[0:2])
        if f == 0:
            sr_ref[0:2, :] = low
            sr_ref[2:3, :] = inner[0:1]
            sr_ref[3:4, :] = inner[w - 1 : w]
            sr_ref[4:6, :] = high
            out_ref[2 * n : 2 * n + 2, :] = jnp.where(right, edge[w - 2 : w], edge[0:2])
        else:
            at = 4 + 2 * f
            sr_ref[at : at + 1, :] = low[1:2]
            sr_ref[at + 1 : at + 2, :] = high[0:1]
            at = 2 * n + 1 + f
            out_ref[at : at + 1, :] = jnp.where(right, edge[w - 1 : w], edge[0:1])


def decode(table):
    return (
        table[:, 0:1] / 500.0 - 1.0,
        table[:, 1:2] / 500.0 - 1.0,
        1.0 + table[:, 2:3] / 1000.0,
        0.5 + table[:, 3:4] / 1000.0,
    )


def decode_rows(table):
    return (
        table[0:1] / 500.0 - 1.0,
        table[1:2] / 500.0 - 1.0,
        1.0 + table[2:3] / 1000.0,
        0.5 + table[3:4] / 1000.0,
    )


def columns_from(left, right, shape):
    rows, w = shape
    at = iota((w, rows), 0)
    return jnp.transpose(jnp.where(at == 0, left, jnp.where(at == w - 1, right, 0.0)))


def shifts_rows(x):
    r = iota(x.shape, 0)
    n = x.shape[0]
    above = jnp.where(r == 0, 0.0, pltpu.roll(x, 1, 0))
    below = jnp.where(r == n - 1, 0.0, pltpu.roll(x, n - 1, 0))
    return above, below


def shifts_cols(x, ends):
    c = iota(x.shape, 1)
    n = x.shape[1]
    before = jnp.where(c == 0, ends, pltpu.roll(x, 1, 1))
    after = jnp.where(c == n - 1, ends, pltpu.roll(x, n - 1, 1))
    return before, after


def fill_context(ctx_ref, surface, albedo, left, right):
    ends = columns_from(left, right, surface.shape)
    before, after = shifts_cols(surface, ends)
    above, below = shifts_rows(surface)
    sx = 0.5 * (after - before)
    sy = 0.5 * (below - above)
    ctx_ref[0] = surface
    ctx_ref[1] = sx
    ctx_ref[2] = sy
    ctx_ref[3] = albedo * lax.rsqrt(1.0 + sx * sx + sy * sy)


def lights_of(block_ref, rows):
    return block_ref.shape[0] // rows


def table_rows(block_ref, rows):
    under = block_ref[pl.ds(lights_of(block_ref, rows) * rows, UNDER), :].astype(F32)
    return under[0:4] * 32.0 + under[4:8]


def fill_params(pb_ref, base, block_ref, n, rows, w, place, total):
    lx, ly, lz, le = decode_rows(table_rows(block_ref, rows))
    col = iota((8, w), 1) + place * w
    px = (col.astype(F32) + 0.5) / total - 0.5
    for j in range(n):
        dx = jnp.broadcast_to(lx[:, j : j + 1], (8, w)) - px
        pb_ref[base + j, 0] = dx
        pb_ref[base + j, 1] = dx * dx
        pb_ref[base + j, 2] = jnp.broadcast_to(ly[:, j : j + 1], (8, w))
        pb_ref[base + j, 3] = jnp.broadcast_to(lz[:, j : j + 1], (8, w))
        pb_ref[base + j, 4] = jnp.broadcast_to(le[:, j : j + 1], (8, w))


def accumulate(state, tile, py, lights):
    surface, sx, sy, scaled = tile
    kept = []
    least = None
    for obs, pb, across in lights:
        dx = pb(0)
        dy = pb(2) - py
        dz = pb(3) - surface
        flat = across(None)
        if flat is None:
            flat = pb(1) + dy * dy
            across(flat)
        dist = flat + dz * dz
        facing = dz - (sx * dx + sy * dy)
        r = lax.rsqrt(dist)
        r2 = r * r
        g = (r2 * r) * pb(4)
        residual = scaled * (g * facing) - obs
        square = residual * residual
        least = square if least is None else jnp.minimum(least, square)
        kept.append((square, residual * g, facing, dz * r2, dx, dy))
    if state is not None:
        before = state[0]
        least = jnp.minimum(least, before)
    sums = None
    for square, q, facing, drop, dx, dy in kept:
        w = jnp.exp2((least - square) * HALF_LOG2E)
        p = w * q
        pf = p * facing
        terms = (w, p, p * dx, p * dy, pf, pf * drop)
        sums = terms if sums is None else tuple(a + b for a, b in zip(sums, terms))
    if state is not None:
        fade = jnp.exp2((least - before) * HALF_LOG2E)
        sums = tuple(a * fade + b for a, b in zip(state[1:], sums))
    return (least,) + sums


def sweep(ctx_ref, chunks, total, load, store, known):
    rows, w = ctx_ref.shape[1:]
    split = (TR // 8, 8, w)

    def step(i, carry):
        at = pl.ds(pl.multiple_of(i * TR, TR), TR)
        tile = tuple(ctx_ref[f, at, :].reshape(split) for f in range(4))
        row = iota(split, 0) * 8 + iota(split, 1) + i * TR
        py = (row.astype(F32) + (0.5 - rows / 2.0)) / total

        def light(entry):
            (obs_ref, j), (pb_ref, p), (flat_ref, f) = entry
            obs = obs_ref[pl.ds(pl.multiple_of(j * rows + i * TR, TR), TR), :].astype(F32).reshape(split)

            def across(value):
                if known:
                    return flat_ref[f, at, :].reshape(split)
                if value is not None:
                    flat_ref[f, at, :] = value.reshape(TR, w)
                return None

            return obs, lambda field: pb_ref[p, field], across

        state = load(at)
        for chunk in chunks:
            state = accumulate(state, tile, py, [light(entry) for entry in chunk])
        store(at, state)
        return carry

    lax.fori_loop(0, rows // TR, step, 0)


def chunk_of(obs_ref, pb_ref, flat_ref, count, pb_at=0, flat_at=0):
    return [((obs_ref, j), (pb_ref, pb_at + j), (flat_ref, flat_at + j)) for j in range(count)]


def state_load(state_ref, w):
    return lambda at: tuple(state_ref[f, at, :].reshape(TR // 8, 8, w) for f in range(7))


def state_store(state_ref, w):
    def store(at, state):
        for f in range(7):
            state_ref[f, at, :] = state[f].reshape(TR, w)

    return store


def halo_slope(column, side, pack_ref, srow_ref, rows, total):
    obs = pack_ref[side]
    lx, ly, lz, le = decode(pack_ref[2])
    outer, inner = (0, 2) if side == 0 else (5, 3)
    here = 1 if side == 0 else 4
    surface = srow_ref[here : here + 1, :]
    toward = srow_ref[inner : inner + 1, :] - srow_ref[outer : outer + 1, :]
    sx = 0.5 * toward if side == 0 else -0.5 * toward
    lane = iota((8, rows), 1)
    wide = jnp.broadcast_to(surface, (8, rows))
    above = jnp.where(lane == 0, 0.0, pltpu.roll(wide, 1, 1))
    below = jnp.where(lane == rows - 1, 0.0, pltpu.roll(wide, rows - 1, 1))
    sy = (0.5 * (below - above))[0:1]
    albedo = srow_ref[6 + side : 7 + side, :]
    valid = srow_ref[8 + side : 9 + side, :]
    px = (column.astype(F32) + 0.5) / total - 0.5
    py = (iota((1, rows), 1).astype(F32) + (0.5 - rows / 2.0)) / total
    rn = lax.rsqrt(1.0 + sx * sx + sy * sy)
    dx = jnp.broadcast_to(lx - px, obs.shape)
    dy = ly - py
    dz = lz - surface
    dist = dx * dx + dy * dy + dz * dz
    facing = dz - (sx * dx + sy * dy)
    r = lax.rsqrt(dist)
    g = (r * r) * r * le
    residual = (albedo * rn) * (g * facing) - obs
    square = residual * residual
    least = jnp.min(square, axis=0, keepdims=True)
    w = jnp.exp2((least - square) * HALF_LOG2E)
    p = w * residual * g
    total_w = jnp.sum(w, axis=0, keepdims=True)
    px_sum = jnp.sum(p * dx, axis=0, keepdims=True)
    pf_sum = jnp.sum(p * facing, axis=0, keepdims=True)
    return -(valid * albedo * rn / total_w) * (px_sum + (sx * rn * rn) * pf_sum)


def gradients(state_ref, ctx_ref, albedo, valid, slope_low, slope_high):
    sx, sy = ctx_ref[1], ctx_ref[2]
    rn = lax.rsqrt(1.0 + sx * sx + sy * sy)
    inverse = valid * rn / state_ref[1]
    factor = inverse * albedo
    pf = state_ref[5]
    rn2pf = rn * rn * pf
    grad_albedo = inverse * pf
    direct = factor * (3.0 * state_ref[6] - state_ref[2])
    grad_x = -factor * (state_ref[3] + sx * rn2pf)
    grad_y = -factor * (state_ref[4] + sy * rn2pf)
    before, after = shifts_cols(grad_x, columns_from(slope_low, slope_high, grad_x.shape))
    above, below = shifts_rows(grad_y)
    return direct + 0.5 * (before - after) + 0.5 * (above - below), grad_albedo


def partial_sums(depth, albedo):
    n = depth.shape[1]
    d = jnp.sum(depth * depth, axis=0, keepdims=True)
    a = jnp.sum(albedo * albedo, axis=0, keepdims=True)
    d = jnp.broadcast_to(d, (8, n))
    a = jnp.broadcast_to(a, (8, n))
    d = d + pltpu.roll(d, n // 2, 1)
    a = a + pltpu.roll(a, n // 2, 1)
    return jnp.where(iota((8, n), 1) < n // 2, d, a)[0:1]


def inverse_scales(recv_ref, row, count):
    rows = recv_ref[:, row, :]
    n = rows.shape[1]
    lane = iota(rows.shape, 1)
    d = jnp.sum(jnp.where(lane < n // 2, rows, 0.0), keepdims=True)
    a = jnp.sum(jnp.where(lane < n // 2, 0.0, rows), keepdims=True)
    return lax.rsqrt(d / count + EPS), lax.rsqrt(a / count + EPS)


def first_body(nl, tile_ref, sr_ref, strip_ref, obs0, obs1, ctx_ref, srow_ref, state_ref, pb_ref, flat_ref):
    li, _, place, count = position()
    rows, w = ctx_ref.shape[1:]
    srow_ref[...] = sr_ref[...]
    at = strip_ref.shape[0] - 8

    @pl.when(li == 0)
    def _():
        srow_ref[0:2, :] = strip_ref[at : at + 2, :]
        srow_ref[6:7, :] = strip_ref[at + 2 : at + 3, :]
        srow_ref[8:9, :] = strip_ref[at + 3 : at + 4, :]

    @pl.when(li == nl - 1)
    def _():
        srow_ref[4:6, :] = strip_ref[at : at + 2, :]
        srow_ref[7:8, :] = strip_ref[at + 2 : at + 3, :]
        srow_ref[9:10, :] = strip_ref[at + 3 : at + 4, :]

    fill_context(ctx_ref, tile_ref[0], tile_ref[1], srow_ref[1:2, :], srow_ref[4:5, :])
    total = w * count
    n = lights_of(obs0, rows)
    fill_params(pb_ref, 0, obs0, n, rows, w, place, total)
    fill_params(pb_ref, n, obs1, n, rows, w, place, total)
    chunks = [chunk_of(obs0, pb_ref, flat_ref, n), chunk_of(obs1, pb_ref, flat_ref, n, n, n)]
    sweep(ctx_ref, chunks, total, lambda at: None, state_store(state_ref, w), False)


def more_body(ctx_ref, in_ref, obs, state_ref, pb_ref, flat_ref):
    _, _, place, count = position()
    rows, w = ctx_ref.shape[1:]
    total = w * count
    fill_params(pb_ref, 0, obs, pb_ref.shape[0], rows, w, place, total)
    chunks = [chunk_of(obs, pb_ref, flat_ref, lights_of(obs, rows))]
    sweep(ctx_ref, chunks, total, state_load(in_ref, w), state_store(state_ref, w), False)


def late_body(ctx_ref, in_ref, obs, pb_ref, state_ref, flat_ref):
    _, _, _, count = position()
    rows, w = ctx_ref.shape[1:]
    n = lights_of(obs, rows)
    chunks = [chunk_of(obs, pb_ref, flat_ref, n, pb_ref.shape[0] - n)]
    sweep(ctx_ref, chunks, w * count, state_load(in_ref, w), state_store(state_ref, w), False)


def halo_slopes(pack_ref, srow_ref, rows, w):
    _, _, place, count = position()
    total = w * count
    low = halo_slope(place * w - 1, 0, pack_ref, srow_ref, rows, total)
    high = halo_slope(place * w + w, 1, pack_ref, srow_ref, rows, total)
    return low, high


def finish(state_ref, ctx_ref, albedo, valid, low, high, grad_ref, edge_ref, pay_ref):
    _, _, place, count = position()
    rows, w = ctx_ref.shape[1:]
    depth, grad_albedo = gradients(state_ref, ctx_ref, albedo, valid, low, high)
    sums = partial_sums(depth, grad_albedo)
    if edge_ref is None:
        pay_ref[...] = jnp.broadcast_to(sums[None], pay_ref.shape)
        return depth, grad_albedo
    grad_ref[0] = depth
    grad_ref[1] = grad_albedo
    dt = jnp.transpose(depth)
    at = jnp.transpose(grad_albedo)
    edge_ref[0:1, :] = dt[0:1]
    edge_ref[1:2, :] = dt[w - 1 : w]
    pay_ref[:, 0:2, :] = jnp.broadcast_to(dt[0:2][None], (count, 2, rows))
    pay_ref[:, 2:3, :] = jnp.broadcast_to(at[0:1][None], (count, 1, rows))
    pay_ref[:, 3:4, :] = jnp.broadcast_to(sums[None], (count, 1, w))

    @pl.when(place < count - 1)
    def _():
        to = exchange_index(place + 1)
        pay_ref[to, 0:2, :] = dt[w - 2 : w]
        pay_ref[to, 2:3, :] = at[w - 1 : w]

    return depth, grad_albedo


def sides_body(nl, srow_ref, direct_ref, relayed_ref, *rest):
    block_refs, (pack_ref, slope_ref) = rest[:nl], rest[nl:]
    li = lax.axis_index("light")
    w = block_refs[0].shape[1]
    rows = srow_ref.shape[1]
    n = (direct_ref.shape[0] - 8) // 2
    table = jnp.zeros((4, w), F32)
    for k in range(nl):
        halo = block_refs[k][pl.ds(lights_of(block_refs[k], rows) * rows + UNDER, 2 * n), :].astype(F32)
        beyond = (direct_ref if k < 2 else relayed_ref)[(k % 2) * n : (k % 2 + 1) * n, :]
        pack_ref[0, k * n : (k + 1) * n, :] = jnp.where(li == 0, beyond, halo[0:n])
        pack_ref[1, k * n : (k + 1) * n, :] = jnp.where(li == nl - 1, beyond, halo[n:])
        entries = jnp.concatenate([table_rows(block_refs[k], rows)] * 2, axis=0)
        table = table + (pltpu.roll(entries, k * n, 1) if k else entries)[0:4]
    tall = jnp.concatenate([table, jnp.zeros((w - 4, w), F32)], axis=0)
    pack_ref[2] = jnp.transpose(tall)[0 : nl * n]
    slope_ref[0:1, :], slope_ref[1:2, :] = halo_slopes(pack_ref, srow_ref, rows, w)


def last_body(ctx_ref, tile_ref, state_ref, slope_ref, grad_ref, edge_ref, pay_ref):
    edge_ref[...] = jnp.zeros_like(edge_ref)
    finish(
        state_ref, ctx_ref, tile_ref[1], tile_ref[2], slope_ref[0:1, :], slope_ref[1:2, :], grad_ref, edge_ref, pay_ref
    )


def second_body(nl, recv_ref, grad_ref, edge_ref, tile_ref, srow0_ref, pack_ref, *rest):
    obs_refs, pb_refs, flat_refs = rest[: nl + 1], rest[nl + 1 : 2 * nl], rest[2 * nl : 3 * nl]
    out_ref, pay_ref, ctx_ref, state_ref, srow_ref = rest[3 * nl :]
    _, _, place, count = position()
    rows, w = ctx_ref.shape[1:]
    total = w * count
    inv_depth, inv_albedo = inverse_scales(recv_ref, 3, float(rows * total))
    surface = tile_ref[0] - STEP_DEPTH * jnp.tanh(grad_ref[0] * inv_depth)
    albedo = tile_ref[1] - STEP_ALBEDO * jnp.tanh(grad_ref[1] * inv_albedo)
    out_ref[0] = surface
    out_ref[1] = albedo
    srow_ref[...] = jnp.zeros_like(srow_ref)
    srow_ref[2:4, :] = edge_ref[0:2, :]

    @pl.when(place > 0)
    def _():
        frm = exchange_index(jnp.maximum(place - 1, 0))
        srow_ref[0:2, :] = recv_ref[frm, 0:2, :]
        srow_ref[6:7, :] = recv_ref[frm, 2:3, :]

    @pl.when(place < count - 1)
    def _():
        frm = exchange_index(jnp.minimum(place + 1, count - 1))
        srow_ref[4:6, :] = recv_ref[frm, 0:2, :]
        srow_ref[7:8, :] = recv_ref[frm, 2:3, :]

    changes = srow_ref[0:8, :]
    kind = iota(changes.shape, 0) < 6
    changes = jnp.where(
        kind, STEP_DEPTH * jnp.tanh(changes * inv_depth), STEP_ALBEDO * jnp.tanh(changes * inv_albedo)
    )
    srow_ref[0:8, :] = srow0_ref[0:8, :] - changes
    srow_ref[8:16, :] = srow0_ref[8:16, :]
    fill_context(ctx_ref, surface, albedo, srow_ref[1:2, :], srow_ref[4:5, :])
    n = lights_of(obs_refs[0], rows)
    chunks = [
        chunk_of(obs_refs[0], pb_refs[0], flat_refs[0], n),
        chunk_of(obs_refs[1], pb_refs[0], flat_refs[0], n, n, n),
    ]
    chunks += [chunk_of(obs_refs[k], pb_refs[k - 1], flat_refs[k - 1], n) for k in range(2, nl - 1)]
    late = lights_of(obs_refs[nl], rows)
    chunks.append(
        chunk_of(obs_refs[nl - 1], pb_refs[-1], flat_refs[-2], n - late)
        + chunk_of(obs_refs[nl], pb_refs[-1], flat_refs[-1], late, n - late)
    )
    sweep(ctx_ref, chunks, total, lambda at: None, state_store(state_ref, w), True)
    low, high = halo_slopes(pack_ref, srow_ref, rows, w)
    depth, grad_albedo = finish(state_ref, ctx_ref, albedo, tile_ref[2], low, high, None, None, pay_ref)
    out_ref[2] = depth
    out_ref[3] = grad_albedo


def hop_body(in_ref, out_ref):
    out_ref[...] = in_ref[...]


def final_body(nl, recv_ref, *rest):
    parts, (depth_ref, albedo_ref) = rest[:nl], rest[nl:]
    li, _, _, count = position()
    rows, w = parts[0].shape[1:]
    inv_depth, inv_albedo = inverse_scales(recv_ref, 0, float(rows * w * count))
    for k in range(nl):
        at = pl.ds(pl.multiple_of((li ^ k) * w, w), w)
        depth_ref[:, at] = parts[k][0] - STEP_DEPTH * jnp.tanh(parts[k][2] * inv_depth)
        albedo_ref[:, at] = parts[k][1] - STEP_ALBEDO * jnp.tanh(parts[k][3] * inv_albedo)


def shape(*dims, dtype=F32):
    return jax.ShapeDtypeStruct(dims, dtype)


def program(depth_start, albedo_start, observations, light_table, valid_mask):
    nl, ns = lax.axis_size("light"), lax.axis_size("strip")
    nd = nl * ns
    lights, rows, cols = observations.shape
    w = cols // nl

    def swap(x, k):
        return lax.ppermute(x, "light", [(i, i ^ k) for i in range(nl)])

    hbm = pl.BlockSpec(memory_space=pltpu.HBM)
    field = (rows, w)
    *blocks, late, end = call(
        functools.partial(cut_body, nl),
        tuple(shape(block_rows(lights, rows, k, nl), w, dtype=jnp.bfloat16) for k in range(nl))
        + (shape(LATE * rows, w, dtype=jnp.bfloat16), shape(2 * lights, rows)),
        [
            pltpu.VMEM((4, lights), jnp.int32),
            pltpu.VMEM((nl + 2, 2 * lights, rows), F32),
            pltpu.SemaphoreType.DMA((nl + 1,)),
            pltpu.SemaphoreType.DMA((1,)),
        ],
        in_specs=[hbm] * 2,
    )(*(pltpu.with_memory_space_constraint(x, pltpu.HBM) for x in (observations, light_table.T)))
    obs2 = swap(blocks[2], 2)
    obs3 = swap(blocks[3], 3)
    obs1 = swap(blocks[1], 1)
    obs0 = blocks[0]
    tile, sr, strip = call(
        functools.partial(join_body, nl), (shape(3, *field), shape(16, rows), shape(2 * lights + 8, rows))
    )(depth_start, albedo_start, valid_mask, obs1, end)
    pairs = []
    for i in range(ns - 1):
        for l in range(nl):
            source, target = (i, i + 1) if l % 2 == 0 else (i + 1, i)
            pairs.append((l * ns + source, l * ns + target))
    direct = lax.ppermute(strip, AXES, pairs)
    relayed = swap(direct, 2)
    late = swap(late, 3)

    def tiles(n):
        return shape(n, 5, 8, w)

    ctx, srow, state, pb0, flat0 = call(
        functools.partial(first_body, nl),
        (shape(4, *field), shape(16, rows), shape(7, *field), tiles(2 * lights), shape(2 * lights, *field)),
    )(tile, sr, direct, obs0, obs1)
    early = lights - LATE
    state, pb2, flat2 = call(more_body, (shape(7, *field), tiles(lights), shape(lights, *field)))(ctx, state, obs2)
    state, pb3, flat3 = call(more_body, (shape(7, *field), tiles(lights), shape(early, *field)))(ctx, state, obs3)
    pack, slope = call(
        functools.partial(sides_body, nl), (shape(3, nl * lights, rows), shape(8, rows))
    )(srow, direct, relayed, obs0, obs1, obs2, obs3)
    state, flat4 = call(late_body, (shape(7, *field), shape(LATE, *field)))(ctx, state, late, pb3)
    grad, edge, pay = call(last_body, (shape(2, *field), shape(8, rows), shape(nd, 4, rows)))(ctx, tile, state, slope)
    recv = lax.all_to_all(pay, AXES, 0, 0, tiled=True)
    own, pay = call(
        functools.partial(second_body, nl),
        (shape(4, *field), shape(nd, 1, rows)),
        [
            pltpu.VMEM((4, *field), F32),
            pltpu.VMEM((7, *field), F32),
            pltpu.VMEM((16, rows), F32),
        ],
    )(recv, grad, edge, tile, srow, pack, obs0, obs1, obs2, obs3, late, pb0, pb2, pb3, flat0, flat2, flat3, flat4)
    part2 = swap(own, 2)
    part1 = swap(own, 1)
    recv = lax.all_to_all(pay, AXES, 0, 0, tiled=True)
    part3 = swap(call(hop_body, shape(4, *field))(part2), 1)
    return tuple(
        call(functools.partial(final_body, nl), (shape(rows, cols), shape(rows, cols)))(recv, own, part1, part2, part3)
    )


def solution(mesh):
    in_specs = (
        P(None, "strip"),
        P(None, "strip"),
        P("light", None, "strip"),
        P("light", None),
        P(None, "strip"),
    )
    out_specs = (P(None, "strip"), P(None, "strip"))
    return jax.shard_map(program, mesh=mesh, in_specs=in_specs, out_specs=out_specs, check_vma=False)
```

```python
import functools
import math

import jax
import jax.numpy as jnp
from jax import lax
from jax.experimental import pallas as pl
from jax.experimental.pallas import tpu as pltpu
from jax.sharding import PartitionSpec as P


AXES = ("light", "strip")
STEP_DEPTH = 0.1
STEP_ALBEDO = 0.2
EPS = 1e-06
HALF_LOG2E = 0.5 * math.log2(math.e)
F32 = jnp.float32
VM = pl.BlockSpec(memory_space=pltpu.VMEM)
TR = 16


def iota(shape, dim):
    return lax.broadcasted_iota(jnp.int32, shape, dim)


def position():
    nl, ns = lax.axis_size("light"), lax.axis_size("strip")
    li, si = lax.axis_index("light"), lax.axis_index("strip")
    return li, si, si * nl + li, nl * ns


def exchange_index(place):
    nl, ns = lax.axis_size("light"), lax.axis_size("strip")
    return lax.rem(place, nl) * ns + lax.div(place, nl)


def call(body, out, scratch=(), vmem=40 << 20, **more):
    return pl.pallas_call(
        body,
        out_shape=out,
        scratch_shapes=list(scratch),
        compiler_params=pltpu.CompilerParams(vmem_limit_bytes=vmem),
        **more,
    )


UNDER = 16
LATE = 3


def block_rows(lights, rows, k, nl):
    here = lights - LATE if k == nl - 1 else lights
    return here * rows + UNDER + 2 * lights + (2 * lights if k == 1 else 0)


def cut_body(nl, obs_ref, table_ref, *rest):
    blocks, (late_ref, end_ref, table, eh_ref, sems, extra) = rest[:nl], rest[nl:]
    lights, rows, cols = obs_ref.shape
    w = cols // nl
    li = lax.axis_index("light")
    here = [lights_of(block, rows) for block in blocks]

    copies = []
    for k in (2, 3, 1, 0):
        at = pl.ds(pl.multiple_of((li ^ k) * w, w), w)
        groups = [(0, here[k], blocks[k])]
        if here[k] < lights:
            groups.append((here[k], lights - here[k], late_ref))
        for start, size, ref in groups:
            target = ref.at[pl.ds(0, size * rows)].reshape(size, rows, w)
            copies.append(
                pltpu.make_async_copy(obs_ref.at[pl.ds(start, size), :, at], target, sems.at[len(copies)])
            )
            copies[-1].start()
    fetch = pltpu.make_async_copy(table_ref, table, extra.at[0])
    fetch.start()
    eh_ref[...] = jnp.zeros_like(eh_ref)
    at, col = iota((2 * lights, lights * w), 0), iota((2 * lights, lights * w), 1)
    pick = (col == jnp.where(at < lights, at * w + w - 1, (at - lights) * w)).astype(jnp.bfloat16)
    fetch.wait()
    entries = table[...]
    high = lax.shift_right_logical(entries, 5)
    both = jnp.concatenate([high, entries - high * 32], axis=0).astype(F32)
    wide = jnp.concatenate([both, jnp.zeros((8, w - lights), F32)], axis=1)
    under = jnp.concatenate([wide, jnp.zeros((UNDER - 8, w), F32)], axis=0).astype(jnp.bfloat16)
    for k in range(nl):
        blocks[k][pl.ds(here[k] * rows, UNDER), :] = under
    for copy in copies:
        copy.wait()
    for k in range(nl):
        q = li ^ k
        side_by_side = [blocks[k][pl.ds(l * rows, rows), :] for l in range(here[k])]
        side_by_side += [late_ref[pl.ds(l * rows, rows), :] for l in range(lights - here[k])]
        e = lax.dot_general(
            pick,
            jnp.concatenate(side_by_side, axis=1),
            (((1,), (1,)), ((), ())),
            preferred_element_type=F32,
        )
        eh_ref[q, lights:, :] = e[lights:]
        eh_ref[q + 2, 0:lights, :] = e[0:lights]
    ends = jnp.concatenate([eh_ref[nl + 1, 0:lights, :], eh_ref[0, lights:, :]], axis=0)
    end_ref[...] = ends
    for k in range(nl):
        halo = pl.ds(here[k] * rows + UNDER, 2 * lights)
        blocks[k][halo, :] = eh_ref[(li ^ k) + 1].astype(jnp.bfloat16)
    blocks[1][pl.ds(lights * rows + UNDER + 2 * lights, 2 * lights), :] = ends.astype(jnp.bfloat16)


def join_body(nl, depth_ref, albedo_ref, valid_ref, block_ref, end_ref, tile_ref, sr_ref, out_ref):
    rows, w = tile_ref.shape[1:]
    n = end_ref.shape[0] // 2
    li = lax.axis_index("light")
    right = lax.rem(li, 2) == 0
    other = block_ref[pl.ds(block_ref.shape[0] - 2 * n, 2 * n), :].astype(F32)
    out_ref[0:n, :] = jnp.where(right, end_ref[0:n, :], end_ref[n:, :])
    out_ref[n : 2 * n, :] = jnp.where(right, other[0:n], other[n:])
    out_ref[2 * n :, :] = jnp.zeros((8, rows), F32)
    sr_ref[...] = jnp.zeros_like(sr_ref)
    lane = iota((rows, w), 1)

    def columns(ref, q):
        return ref[:, pl.ds(pl.multiple_of(q * w, w), w)].astype(F32)

    for f, ref in enumerate((depth_ref, albedo_ref, valid_ref)):
        own = columns(ref, li)
        before = columns(ref, jnp.maximum(li - 1, 0))
        after = columns(ref, jnp.minimum(li + 1, nl - 1))
        tile_ref[f] = own
        inner = jnp.transpose(own)
        outer = jnp.transpose(jnp.where(lane < w // 2, after, before))
        edge = jnp.transpose(columns(ref, jnp.where(right, nl - 1, 0)))
        low = jnp.where(li == 0, 0.0, outer[w - 2 : w])
        high = jnp.where(li == nl - 1, 0.0, outer[0:2])
        if f == 0:
            sr_ref[0:2, :] = low
            sr_ref[2:3, :] = inner[0:1]
            sr_ref[3:4, :] = inner[w - 1 : w]
            sr_ref[4:6, :] = high
            out_ref[2 * n : 2 * n + 2, :] = jnp.where(right, edge[w - 2 : w], edge[0:2])
        else:
            at = 4 + 2 * f
            sr_ref[at : at + 1, :] = low[1:2]
            sr_ref[at + 1 : at + 2, :] = high[0:1]
            at = 2 * n + 1 + f
            out_ref[at : at + 1, :] = jnp.where(right, edge[w - 1 : w], edge[0:1])


def decode(table):
    return (
        table[:, 0:1] / 500.0 - 1.0,
        table[:, 1:2] / 500.0 - 1.0,
        1.0 + table[:, 2:3] / 1000.0,
        0.5 + table[:, 3:4] / 1000.0,
    )


def decode_rows(table):
    return (
        table[0:1] / 500.0 - 1.0,
        table[1:2] / 500.0 - 1.0,
        1.0 + table[2:3] / 1000.0,
        0.5 + table[3:4] / 1000.0,
    )


def columns_from(left, right, shape):
    rows, w = shape
    at = iota((w, rows), 0)
    return jnp.transpose(jnp.where(at == 0, left, jnp.where(at == w - 1, right, 0.0)))


def shifts_rows(x):
    r = iota(x.shape, 0)
    n = x.shape[0]
    above = jnp.where(r == 0, 0.0, pltpu.roll(x, 1, 0))
    below = jnp.where(r == n - 1, 0.0, pltpu.roll(x, n - 1, 0))
    return above, below


def shifts_cols(x, ends):
    c = iota(x.shape, 1)
    n = x.shape[1]
    before = jnp.where(c == 0, ends, pltpu.roll(x, 1, 1))
    after = jnp.where(c == n - 1, ends, pltpu.roll(x, n - 1, 1))
    return before, after


def fill_context(ctx_ref, surface, albedo, left, right):
    ends = columns_from(left, right, surface.shape)
    before, after = shifts_cols(surface, ends)
    above, below = shifts_rows(surface)
    sx = 0.5 * (after - before)
    sy = 0.5 * (below - above)
    ctx_ref[0] = surface
    ctx_ref[1] = sx
    ctx_ref[2] = sy
    ctx_ref[3] = albedo * lax.rsqrt(1.0 + sx * sx + sy * sy)


def lights_of(block_ref, rows):
    return block_ref.shape[0] // rows


def table_rows(block_ref, rows):
    under = block_ref[pl.ds(lights_of(block_ref, rows) * rows, UNDER), :].astype(F32)
    return under[0:4] * 32.0 + under[4:8]


def fill_params(pb_ref, base, block_ref, n, rows, w, place, total):
    lx, ly, lz, le = decode_rows(table_rows(block_ref, rows))
    col = iota((8, w), 1) + place * w
    px = (col.astype(F32) + 0.5) / total - 0.5
    for j in range(n):
        dx = jnp.broadcast_to(lx[:, j : j + 1], (8, w)) - px
        pb_ref[base + j, 0] = dx
        pb_ref[base + j, 1] = dx * dx
        pb_ref[base + j, 2] = jnp.broadcast_to(ly[:, j : j + 1], (8, w))
        pb_ref[base + j, 3] = jnp.broadcast_to(lz[:, j : j + 1], (8, w))
        pb_ref[base + j, 4] = jnp.broadcast_to(le[:, j : j + 1], (8, w))


def accumulate(state, tile, py, lights):
    surface, sx, sy, scaled = tile
    kept = []
    least = None
    for obs, pb, across in lights:
        dx = pb(0)
        dy = pb(2) - py
        dz = pb(3) - surface
        flat = across(None)
        if flat is None:
            flat = pb(1) + dy * dy
            across(flat)
        dist = flat + dz * dz
        facing = dz - (sx * dx + sy * dy)
        r = lax.rsqrt(dist)
        r2 = r * r
        g = (r2 * r) * pb(4)
        residual = scaled * (g * facing) - obs
        square = residual * residual
        least = square if least is None else jnp.minimum(least, square)
        kept.append((square, residual * g, facing, dz * r2, dx, dy))
    if state is not None:
        before = state[0]
        least = jnp.minimum(least, before)
    sums = None
    for square, q, facing, drop, dx, dy in kept:
        w = jnp.exp2((least - square) * HALF_LOG2E)
        p = w * q
        pf = p * facing
        terms = (w, p, p * dx, p * dy, pf, pf * drop)
        sums = terms if sums is None else tuple(a + b for a, b in zip(sums, terms))
    if state is not None:
        fade = jnp.exp2((least - before) * HALF_LOG2E)
        sums = tuple(a * fade + b for a, b in zip(state[1:], sums))
    return (least,) + sums


def sweep(ctx_ref, chunks, total, load, store, known):
    rows, w = ctx_ref.shape[1:]
    split = (TR // 8, 8, w)

    def step(i, carry):
        at = pl.ds(pl.multiple_of(i * TR, TR), TR)
        tile = tuple(ctx_ref[f, at, :].reshape(split) for f in range(4))
        row = iota(split, 0) * 8 + iota(split, 1) + i * TR
        py = (row.astype(F32) + (0.5 - rows / 2.0)) / total

        def light(entry):
            (obs_ref, j), (pb_ref, p), (flat_ref, f) = entry
            obs = obs_ref[pl.ds(pl.multiple_of(j * rows + i * TR, TR), TR), :].astype(F32).reshape(split)

            def across(value):
                if known:
                    return flat_ref[f, at, :].reshape(split)
                if value is not None:
                    flat_ref[f, at, :] = value.reshape(TR, w)
                return None

            return obs, lambda field: pb_ref[p, field], across

        state = load(at)
        for chunk in chunks:
            state = accumulate(state, tile, py, [light(entry) for entry in chunk])
        store(at, state)
        return carry

    lax.fori_loop(0, rows // TR, step, 0)


def chunk_of(obs_ref, pb_ref, flat_ref, count, pb_at=0, flat_at=0):
    return [((obs_ref, j), (pb_ref, pb_at + j), (flat_ref, flat_at + j)) for j in range(count)]


def state_load(state_ref, w):
    return lambda at: tuple(state_ref[f, at, :].reshape(TR // 8, 8, w) for f in range(7))


def state_store(state_ref, w):
    def store(at, state):
        for f in range(7):
            state_ref[f, at, :] = state[f].reshape(TR, w)

    return store


def halo_slope(column, side, pack_ref, srow_ref, rows, total):
    obs = pack_ref[side]
    lx, ly, lz, le = decode(pack_ref[2])
    outer, inner = (0, 2) if side == 0 else (5, 3)
    here = 1 if side == 0 else 4
    surface = srow_ref[here : here + 1, :]
    toward = srow_ref[inner : inner + 1, :] - srow_ref[outer : outer + 1, :]
    sx = 0.5 * toward if side == 0 else -0.5 * toward
    lane = iota((8, rows), 1)
    wide = jnp.broadcast_to(surface, (8, rows))
    above = jnp.where(lane == 0, 0.0, pltpu.roll(wide, 1, 1))
    below = jnp.where(lane == rows - 1, 0.0, pltpu.roll(wide, rows - 1, 1))
    sy = (0.5 * (below - above))[0:1]
    albedo = srow_ref[6 + side : 7 + side, :]
    valid = srow_ref[8 + side : 9 + side, :]
    px = (column.astype(F32) + 0.5) / total - 0.5
    py = (iota((1, rows), 1).astype(F32) + (0.5 - rows / 2.0)) / total
    rn = lax.rsqrt(1.0 + sx * sx + sy * sy)
    dx = jnp.broadcast_to(lx - px, obs.shape)
    dy = ly - py
    dz = lz - surface
    dist = dx * dx + dy * dy + dz * dz
    facing = dz - (sx * dx + sy * dy)
    r = lax.rsqrt(dist)
    g = (r * r) * r * le
    residual = (albedo * rn) * (g * facing) - obs
    square = residual * residual
    least = jnp.min(square, axis=0, keepdims=True)
    w = jnp.exp2((least - square) * HALF_LOG2E)
    p = w * residual * g
    total_w = jnp.sum(w, axis=0, keepdims=True)
    px_sum = jnp.sum(p * dx, axis=0, keepdims=True)
    pf_sum = jnp.sum(p * facing, axis=0, keepdims=True)
    return -(valid * albedo * rn / total_w) * (px_sum + (sx * rn * rn) * pf_sum)


def gradients(state_ref, ctx_ref, albedo, valid, ends):
    sx, sy = ctx_ref[1], ctx_ref[2]
    rn = lax.rsqrt(1.0 + sx * sx + sy * sy)
    inverse = valid * rn / state_ref[1]
    factor = inverse * albedo
    pf = state_ref[5]
    rn2pf = rn * rn * pf
    grad_albedo = inverse * pf
    direct = factor * (3.0 * state_ref[6] - state_ref[2])
    grad_x = -factor * (state_ref[3] + sx * rn2pf)
    grad_y = -factor * (state_ref[4] + sy * rn2pf)
    before, after = shifts_cols(grad_x, ends)
    above, below = shifts_rows(grad_y)
    return direct + 0.5 * (before - after) + 0.5 * (above - below), grad_albedo


def partial_sums(depth, albedo):
    n = depth.shape[1]
    d = jnp.sum(depth * depth, axis=0, keepdims=True)
    a = jnp.sum(albedo * albedo, axis=0, keepdims=True)
    d = jnp.broadcast_to(d, (8, n))
    a = jnp.broadcast_to(a, (8, n))
    d = d + pltpu.roll(d, n // 2, 1)
    a = a + pltpu.roll(a, n // 2, 1)
    return jnp.where(iota((8, n), 1) < n // 2, d, a)[0:1]


def inverse_scales(recv_ref, row, count):
    rows = recv_ref[:, row, :]
    n = rows.shape[1]
    lane = iota(rows.shape, 1)
    d = jnp.sum(jnp.where(lane < n // 2, rows, 0.0), keepdims=True)
    a = jnp.sum(jnp.where(lane < n // 2, 0.0, rows), keepdims=True)
    return lax.rsqrt(d / count + EPS), lax.rsqrt(a / count + EPS)


def first_body(nl, tile_ref, sr_ref, strip_ref, obs0, obs1, ctx_ref, srow_ref, state_ref, pb_ref, flat_ref):
    li, _, place, count = position()
    rows, w = ctx_ref.shape[1:]
    srow_ref[...] = sr_ref[...]
    at = strip_ref.shape[0] - 8

    @pl.when(li == 0)
    def _():
        srow_ref[0:2, :] = strip_ref[at : at + 2, :]
        srow_ref[6:7, :] = strip_ref[at + 2 : at + 3, :]
        srow_ref[8:9, :] = strip_ref[at + 3 : at + 4, :]

    @pl.when(li == nl - 1)
    def _():
        srow_ref[4:6, :] = strip_ref[at : at + 2, :]
        srow_ref[7:8, :] = strip_ref[at + 2 : at + 3, :]
        srow_ref[9:10, :] = strip_ref[at + 3 : at + 4, :]

    fill_context(ctx_ref, tile_ref[0], tile_ref[1], srow_ref[1:2, :], srow_ref[4:5, :])
    total = w * count
    n = lights_of(obs0, rows)
    fill_params(pb_ref, 0, obs0, n, rows, w, place, total)
    fill_params(pb_ref, n, obs1, n, rows, w, place, total)
    chunks = [chunk_of(obs0, pb_ref, flat_ref, n), chunk_of(obs1, pb_ref, flat_ref, n, n, n)]
    sweep(ctx_ref, chunks, total, lambda at: None, state_store(state_ref, w), False)


def more_body(ctx_ref, in_ref, obs, state_ref, pb_ref, flat_ref):
    _, _, place, count = position()
    rows, w = ctx_ref.shape[1:]
    total = w * count
    fill_params(pb_ref, 0, obs, pb_ref.shape[0], rows, w, place, total)
    chunks = [chunk_of(obs, pb_ref, flat_ref, lights_of(obs, rows))]
    sweep(ctx_ref, chunks, total, state_load(in_ref, w), state_store(state_ref, w), False)


def halo_slopes(pack_ref, srow_ref, rows, w):
    _, _, place, count = position()
    total = w * count
    low = halo_slope(place * w - 1, 0, pack_ref, srow_ref, rows, total)
    high = halo_slope(place * w + w, 1, pack_ref, srow_ref, rows, total)
    return columns_from(low, high, (rows, w))


def finish(state_ref, ctx_ref, albedo, valid, ends, grad_ref, edge_ref, pay_ref):
    _, _, place, count = position()
    rows, w = ctx_ref.shape[1:]
    depth, grad_albedo = gradients(state_ref, ctx_ref, albedo, valid, ends)
    sums = partial_sums(depth, grad_albedo)
    if edge_ref is None:
        pay_ref[...] = jnp.broadcast_to(sums[None], pay_ref.shape)
        return depth, grad_albedo
    grad_ref[0] = depth
    grad_ref[1] = grad_albedo
    dt = jnp.transpose(depth)
    at = jnp.transpose(grad_albedo)
    edge_ref[0:1, :] = dt[0:1]
    edge_ref[1:2, :] = dt[w - 1 : w]
    pay_ref[:, 0:2, :] = jnp.broadcast_to(dt[0:2][None], (count, 2, rows))
    pay_ref[:, 2:3, :] = jnp.broadcast_to(at[0:1][None], (count, 1, rows))
    pay_ref[:, 3:4, :] = jnp.broadcast_to(sums[None], (count, 1, w))

    @pl.when(place < count - 1)
    def _():
        to = exchange_index(place + 1)
        pay_ref[to, 0:2, :] = dt[w - 2 : w]
        pay_ref[to, 2:3, :] = at[w - 1 : w]

    return depth, grad_albedo


def sides_body(nl, srow_ref, direct_ref, relayed_ref, *rest):
    block_refs, (pack_ref, ends_ref) = rest[:nl], rest[nl:]
    li = lax.axis_index("light")
    w = block_refs[0].shape[1]
    rows = srow_ref.shape[1]
    n = (direct_ref.shape[0] - 8) // 2
    table = jnp.zeros((4, w), F32)
    for k in range(nl):
        halo = block_refs[k][pl.ds(lights_of(block_refs[k], rows) * rows + UNDER, 2 * n), :].astype(F32)
        beyond = (direct_ref if k < 2 else relayed_ref)[(k % 2) * n : (k % 2 + 1) * n, :]
        pack_ref[0, k * n : (k + 1) * n, :] = jnp.where(li == 0, beyond, halo[0:n])
        pack_ref[1, k * n : (k + 1) * n, :] = jnp.where(li == nl - 1, beyond, halo[n:])
        entries = jnp.concatenate([table_rows(block_refs[k], rows)] * 2, axis=0)
        table = table + (pltpu.roll(entries, k * n, 1) if k else entries)[0:4]
    tall = jnp.concatenate([table, jnp.zeros((w - 4, w), F32)], axis=0)
    pack_ref[2] = jnp.transpose(tall)[0 : nl * n]
    ends_ref[...] = halo_slopes(pack_ref, srow_ref, rows, w)


def last_body(ctx_ref, in_ref, obs, pb_ref, tile_ref, ends_ref, grad_ref, edge_ref, pay_ref, flat_ref, state_ref):
    _, _, _, count = position()
    rows, w = ctx_ref.shape[1:]
    n = lights_of(obs, rows)
    edge_ref[...] = jnp.zeros_like(edge_ref)
    chunks = [chunk_of(obs, pb_ref, flat_ref, n, pb_ref.shape[0] - n)]
    sweep(ctx_ref, chunks, w * count, state_load(in_ref, w), state_store(state_ref, w), False)
    finish(state_ref, ctx_ref, tile_ref[1], tile_ref[2], ends_ref[...], grad_ref, edge_ref, pay_ref)


def second_body(nl, recv_ref, grad_ref, edge_ref, tile_ref, srow0_ref, pack_ref, *rest):
    obs_refs, pb_refs, flat_refs = rest[: nl + 1], rest[nl + 1 : 2 * nl], rest[2 * nl : 3 * nl]
    out_ref, pay_ref, ctx_ref, state_ref, srow_ref, ends_ref = rest[3 * nl :]
    _, _, place, count = position()
    rows, w = ctx_ref.shape[1:]
    total = w * count
    inv_depth, inv_albedo = inverse_scales(recv_ref, 3, float(rows * total))
    surface = tile_ref[0] - STEP_DEPTH * jnp.tanh(grad_ref[0] * inv_depth)
    albedo = tile_ref[1] - STEP_ALBEDO * jnp.tanh(grad_ref[1] * inv_albedo)
    out_ref[0] = surface
    out_ref[1] = albedo
    srow_ref[...] = jnp.zeros_like(srow_ref)
    srow_ref[2:4, :] = edge_ref[0:2, :]

    @pl.when(place > 0)
    def _():
        frm = exchange_index(jnp.maximum(place - 1, 0))
        srow_ref[0:2, :] = recv_ref[frm, 0:2, :]
        srow_ref[6:7, :] = recv_ref[frm, 2:3, :]

    @pl.when(place < count - 1)
    def _():
        frm = exchange_index(jnp.minimum(place + 1, count - 1))
        srow_ref[4:6, :] = recv_ref[frm, 0:2, :]
        srow_ref[7:8, :] = recv_ref[frm, 2:3, :]

    changes = srow_ref[0:8, :]
    kind = iota(changes.shape, 0) < 6
    changes = jnp.where(
        kind, STEP_DEPTH * jnp.tanh(changes * inv_depth), STEP_ALBEDO * jnp.tanh(changes * inv_albedo)
    )
    srow_ref[0:8, :] = srow0_ref[0:8, :] - changes
    srow_ref[8:16, :] = srow0_ref[8:16, :]
    fill_context(ctx_ref, surface, albedo, srow_ref[1:2, :], srow_ref[4:5, :])
    n = lights_of(obs_refs[0], rows)
    chunks = [
        chunk_of(obs_refs[0], pb_refs[0], flat_refs[0], n),
        chunk_of(obs_refs[1], pb_refs[0], flat_refs[0], n, n, n),
    ]
    chunks += [chunk_of(obs_refs[k], pb_refs[k - 1], flat_refs[k - 1], n) for k in range(2, nl - 1)]
    late = lights_of(obs_refs[nl], rows)
    chunks.append(
        chunk_of(obs_refs[nl - 1], pb_refs[-1], flat_refs[-2], n - late)
        + chunk_of(obs_refs[nl], pb_refs[-1], flat_refs[-1], late, n - late)
    )
    ends_ref[...] = halo_slopes(pack_ref, srow_ref, rows, w)
    sweep(ctx_ref, chunks, total, lambda at: None, state_store(state_ref, w), True)
    depth, grad_albedo = finish(
        state_ref, ctx_ref, out_ref[1], tile_ref[2], ends_ref[...], None, None, pay_ref
    )
    out_ref[2] = depth
    out_ref[3] = grad_albedo


def hop_body(in_ref, out_ref):
    out_ref[...] = in_ref[...]


def final_body(nl, recv_ref, *rest):
    parts, (depth_ref, albedo_ref) = rest[:nl], rest[nl:]
    li, _, _, count = position()
    rows, w = parts[0].shape[1:]
    inv_depth, inv_albedo = inverse_scales(recv_ref, 0, float(rows * w * count))
    for k in range(nl):
        at = pl.ds(pl.multiple_of((li ^ k) * w, w), w)
        depth_ref[:, at] = parts[k][0] - STEP_DEPTH * jnp.tanh(parts[k][2] * inv_depth)
        albedo_ref[:, at] = parts[k][1] - STEP_ALBEDO * jnp.tanh(parts[k][3] * inv_albedo)


def shape(*dims, dtype=F32):
    return jax.ShapeDtypeStruct(dims, dtype)


def program(depth_start, albedo_start, observations, light_table, valid_mask):
    nl, ns = lax.axis_size("light"), lax.axis_size("strip")
    nd = nl * ns
    lights, rows, cols = observations.shape
    w = cols // nl

    def swap(x, k):
        return lax.ppermute(x, "light", [(i, i ^ k) for i in range(nl)])

    hbm = pl.BlockSpec(memory_space=pltpu.HBM)
    field = (rows, w)
    *blocks, late, end = call(
        functools.partial(cut_body, nl),
        tuple(shape(block_rows(lights, rows, k, nl), w, dtype=jnp.bfloat16) for k in range(nl))
        + (shape(LATE * rows, w, dtype=jnp.bfloat16), shape(2 * lights, rows)),
        [
            pltpu.VMEM((4, lights), jnp.int32),
            pltpu.VMEM((nl + 2, 2 * lights, rows), F32),
            pltpu.SemaphoreType.DMA((nl + 1,)),
            pltpu.SemaphoreType.DMA((1,)),
        ],
        in_specs=[hbm] * 2,
    )(*(pltpu.with_memory_space_constraint(x, pltpu.HBM) for x in (observations, light_table.T)))
    obs2 = swap(blocks[2], 2)
    obs3 = swap(blocks[3], 3)
    obs1 = swap(blocks[1], 1)
    obs0 = blocks[0]
    tile, sr, strip = call(
        functools.partial(join_body, nl), (shape(3, *field), shape(16, rows), shape(2 * lights + 8, rows))
    )(depth_start, albedo_start, valid_mask, obs1, end)
    pairs = []
    for i in range(ns - 1):
        for l in range(nl):
            source, target = (i, i + 1) if l % 2 == 0 else (i + 1, i)
            pairs.append((l * ns + source, l * ns + target))
    direct = lax.ppermute(strip, AXES, pairs)
    relayed = swap(direct, 2)
    late = swap(late, 3)

    def tiles(n):
        return shape(n, 5, 8, w)

    ctx, srow, state, pb0, flat0 = call(
        functools.partial(first_body, nl),
        (shape(4, *field), shape(16, rows), shape(7, *field), tiles(2 * lights), shape(2 * lights, *field)),
    )(tile, sr, direct, obs0, obs1)
    early = lights - LATE
    state, pb2, flat2 = call(more_body, (shape(7, *field), tiles(lights), shape(lights, *field)))(ctx, state, obs2)
    state, pb3, flat3 = call(more_body, (shape(7, *field), tiles(lights), shape(early, *field)))(ctx, state, obs3)
    pack, ends = call(
        functools.partial(sides_body, nl), (shape(3, nl * lights, rows), shape(*field))
    )(srow, direct, relayed, obs0, obs1, obs2, obs3)
    grad, edge, pay, flat4 = call(
        last_body,
        (shape(2, *field), shape(8, rows), shape(nd, 4, rows), shape(LATE, *field)),
        [pltpu.VMEM((7, *field), F32)],
    )(ctx, state, late, pb3, tile, ends)
    recv = lax.all_to_all(pay, AXES, 0, 0, tiled=True)
    own, pay = call(
        functools.partial(second_body, nl),
        (shape(4, *field), shape(nd, 1, rows)),
        [
            pltpu.VMEM((4, *field), F32),
            pltpu.VMEM((7, *field), F32),
            pltpu.VMEM((16, rows), F32),
            pltpu.VMEM(field, F32),
        ],
    )(recv, grad, edge, tile, srow, pack, obs0, obs1, obs2, obs3, late, pb0, pb2, pb3, flat0, flat2, flat3, flat4)
    part2 = swap(own, 2)
    part1 = swap(own, 1)
    recv = lax.all_to_all(pay, AXES, 0, 0, tiled=True)
    part3 = swap(call(hop_body, shape(4, *field))(part2), 1)
    return tuple(
        call(functools.partial(final_body, nl), (shape(rows, cols), shape(rows, cols)))(recv, own, part1, part2, part3)
    )


def solution(mesh):
    in_specs = (
        P(None, "strip"),
        P(None, "strip"),
        P("light", None, "strip"),
        P("light", None),
        P(None, "strip"),
    )
    out_specs = (P(None, "strip"), P(None, "strip"))
    return jax.shard_map(program, mesh=mesh, in_specs=in_specs, out_specs=out_specs, check_vma=False)
```

```python
import functools
import math

import jax
import jax.numpy as jnp
from jax import lax
from jax.experimental import pallas as pl
from jax.experimental.pallas import tpu as pltpu
from jax.sharding import PartitionSpec as P


AXES = ("light", "strip")
STEP_DEPTH = 0.1
STEP_ALBEDO = 0.2
EPS = 1e-06
HALF_LOG2E = 0.5 * math.log2(math.e)
F32 = jnp.float32
VM = pl.BlockSpec(memory_space=pltpu.VMEM)
TR = 16


def iota(shape, dim):
    return lax.broadcasted_iota(jnp.int32, shape, dim)


def position():
    nl, ns = lax.axis_size("light"), lax.axis_size("strip")
    li, si = lax.axis_index("light"), lax.axis_index("strip")
    return li, si, si * nl + li, nl * ns


def exchange_index(place):
    nl, ns = lax.axis_size("light"), lax.axis_size("strip")
    return lax.rem(place, nl) * ns + lax.div(place, nl)


def call(body, out, scratch=(), vmem=40 << 20, **more):
    return pl.pallas_call(
        body,
        out_shape=out,
        scratch_shapes=list(scratch),
        compiler_params=pltpu.CompilerParams(vmem_limit_bytes=vmem),
        **more,
    )


UNDER = 16
LATE = 2


def block_rows(lights, rows, k, nl):
    here = lights - LATE if k == nl - 1 else lights
    return here * rows + UNDER + 2 * lights + (2 * lights if k == 1 else 0)


def cut_body(nl, obs_ref, table_ref, *rest):
    blocks, (late_ref, end_ref, table, eh_ref, sems, extra) = rest[:nl], rest[nl:]
    lights, rows, cols = obs_ref.shape
    w = cols // nl
    li = lax.axis_index("light")
    here = [lights_of(block, rows) for block in blocks]

    copies = []
    for k in (2, 3, 1, 0):
        at = pl.ds(pl.multiple_of((li ^ k) * w, w), w)
        groups = [(0, here[k], blocks[k])]
        if here[k] < lights:
            groups.append((here[k], lights - here[k], late_ref))
        for start, size, ref in groups:
            target = ref.at[pl.ds(0, size * rows)].reshape(size, rows, w)
            copies.append(
                pltpu.make_async_copy(obs_ref.at[pl.ds(start, size), :, at], target, sems.at[len(copies)])
            )
            copies[-1].start()
    fetch = pltpu.make_async_copy(table_ref, table, extra.at[0])
    fetch.start()
    eh_ref[...] = jnp.zeros_like(eh_ref)
    at, col = iota((2 * lights, lights * w), 0), iota((2 * lights, lights * w), 1)
    pick = (col == jnp.where(at < lights, at * w + w - 1, (at - lights) * w)).astype(jnp.bfloat16)
    fetch.wait()
    entries = table[...]
    high = lax.shift_right_logical(entries, 5)
    both = jnp.concatenate([high, entries - high * 32], axis=0).astype(F32)
    wide = jnp.concatenate([both, jnp.zeros((8, w - lights), F32)], axis=1)
    under = jnp.concatenate([wide, jnp.zeros((UNDER - 8, w), F32)], axis=0).astype(jnp.bfloat16)
    for k in range(nl):
        blocks[k][pl.ds(here[k] * rows, UNDER), :] = under
    for copy in copies:
        copy.wait()
    for k in range(nl):
        q = li ^ k
        side_by_side = [blocks[k][pl.ds(l * rows, rows), :] for l in range(here[k])]
        side_by_side += [late_ref[pl.ds(l * rows, rows), :] for l in range(lights - here[k])]
        e = lax.dot_general(
            pick,
            jnp.concatenate(side_by_side, axis=1),
            (((1,), (1,)), ((), ())),
            preferred_element_type=F32,
        )
        eh_ref[q, lights:, :] = e[lights:]
        eh_ref[q + 2, 0:lights, :] = e[0:lights]
    ends = jnp.concatenate([eh_ref[nl + 1, 0:lights, :], eh_ref[0, lights:, :]], axis=0)
    end_ref[...] = ends
    for k in range(nl):
        halo = pl.ds(here[k] * rows + UNDER, 2 * lights)
        blocks[k][halo, :] = eh_ref[(li ^ k) + 1].astype(jnp.bfloat16)
    blocks[1][pl.ds(lights * rows + UNDER + 2 * lights, 2 * lights), :] = ends.astype(jnp.bfloat16)


def join_body(
    nl, depth_from, albedo_from, valid_from, block_ref, end_ref, tile_ref, sr_ref, out_ref, fields, valid_ref, sems
):
    depth_ref, albedo_ref = fields.at[0], fields.at[1]
    copies = []
    for source, target in ((depth_from, depth_ref), (albedo_from, albedo_ref), (valid_from, valid_ref)):
        copies.append(pltpu.make_async_copy(source, target, sems.at[len(copies)]))
        copies[-1].start()
    rows, w = tile_ref.shape[1:]
    n = end_ref.shape[0] // 2
    li = lax.axis_index("light")
    right = lax.rem(li, 2) == 0
    other = block_ref[pl.ds(block_ref.shape[0] - 2 * n, 2 * n), :].astype(F32)
    out_ref[0:n, :] = jnp.where(right, end_ref[0:n, :], end_ref[n:, :])
    out_ref[n : 2 * n, :] = jnp.where(right, other[0:n], other[n:])
    out_ref[2 * n :, :] = jnp.zeros((8, rows), F32)
    sr_ref[...] = jnp.zeros_like(sr_ref)
    lane = iota((rows, w), 1)
    for copy in copies:
        copy.wait()

    def columns(ref, q):
        return ref[:, pl.ds(pl.multiple_of(q * w, w), w)].astype(F32)

    for f, ref in enumerate((depth_ref, albedo_ref, valid_ref)):
        own = columns(ref, li)
        before = columns(ref, jnp.maximum(li - 1, 0))
        after = columns(ref, jnp.minimum(li + 1, nl - 1))
        tile_ref[f] = own
        inner = jnp.transpose(own)
        outer = jnp.transpose(jnp.where(lane < w // 2, after, before))
        edge = jnp.transpose(columns(ref, jnp.where(right, nl - 1, 0)))
        low = jnp.where(li == 0, 0.0, outer[w - 2 : w])
        high = jnp.where(li == nl - 1, 0.0, outer[0:2])
        if f == 0:
            sr_ref[0:2, :] = low
            sr_ref[2:3, :] = inner[0:1]
            sr_ref[3:4, :] = inner[w - 1 : w]
            sr_ref[4:6, :] = high
            out_ref[2 * n : 2 * n + 2, :] = jnp.where(right, edge[w - 2 : w], edge[0:2])
        else:
            at = 4 + 2 * f
            sr_ref[at : at + 1, :] = low[1:2]
            sr_ref[at + 1 : at + 2, :] = high[0:1]
            at = 2 * n + 1 + f
            out_ref[at : at + 1, :] = jnp.where(right, edge[w - 1 : w], edge[0:1])


def decode(table):
    return (
        table[:, 0:1] / 500.0 - 1.0,
        table[:, 1:2] / 500.0 - 1.0,
        1.0 + table[:, 2:3] / 1000.0,
        0.5 + table[:, 3:4] / 1000.0,
    )


def decode_rows(table):
    return (
        table[0:1] / 500.0 - 1.0,
        table[1:2] / 500.0 - 1.0,
        1.0 + table[2:3] / 1000.0,
        0.5 + table[3:4] / 1000.0,
    )


def columns_from(left, right, shape):
    rows, w = shape
    at = iota((w, rows), 0)
    return jnp.transpose(jnp.where(at == 0, left, jnp.where(at == w - 1, right, 0.0)))


def shifts_rows(x):
    r = iota(x.shape, 0)
    n = x.shape[0]
    above = jnp.where(r == 0, 0.0, pltpu.roll(x, 1, 0))
    below = jnp.where(r == n - 1, 0.0, pltpu.roll(x, n - 1, 0))
    return above, below


def shifts_cols(x, ends):
    c = iota(x.shape, 1)
    n = x.shape[1]
    before = jnp.where(c == 0, ends, pltpu.roll(x, 1, 1))
    after = jnp.where(c == n - 1, ends, pltpu.roll(x, n - 1, 1))
    return before, after


def fill_context(ctx_ref, surface, albedo, left, right):
    ends = columns_from(left, right, surface.shape)
    before, after = shifts_cols(surface, ends)
    above, below = shifts_rows(surface)
    sx = 0.5 * (after - before)
    sy = 0.5 * (below - above)
    ctx_ref[0] = surface
    ctx_ref[1] = sx
    ctx_ref[2] = sy
    ctx_ref[3] = albedo * lax.rsqrt(1.0 + sx * sx + sy * sy)


def lights_of(block_ref, rows):
    return block_ref.shape[0] // rows


def table_rows(block_ref, rows):
    under = block_ref[pl.ds(lights_of(block_ref, rows) * rows, UNDER), :].astype(F32)
    return under[0:4] * 32.0 + under[4:8]


def fill_params(pb_ref, base, block_ref, n, rows, w, place, total):
    lx, ly, lz, le = decode_rows(table_rows(block_ref, rows))
    col = iota((8, w), 1) + place * w
    px = (col.astype(F32) + 0.5) / total - 0.5
    for j in range(n):
        dx = jnp.broadcast_to(lx[:, j : j + 1], (8, w)) - px
        pb_ref[base + j, 0] = dx
        pb_ref[base + j, 1] = dx * dx
        pb_ref[base + j, 2] = jnp.broadcast_to(ly[:, j : j + 1], (8, w))
        pb_ref[base + j, 3] = jnp.broadcast_to(lz[:, j : j + 1], (8, w))
        pb_ref[base + j, 4] = jnp.broadcast_to(le[:, j : j + 1], (8, w))


def accumulate(state, tile, py, lights):
    surface, sx, sy, scaled = tile
    kept = []
    least = None
    for obs, pb, across in lights:
        dx = pb(0)
        dy = pb(2) - py
        dz = pb(3) - surface
        flat = across(None)
        if flat is None:
            flat = pb(1) + dy * dy
            across(flat)
        dist = flat + dz * dz
        facing = dz - (sx * dx + sy * dy)
        r = lax.rsqrt(dist)
        r2 = r * r
        g = (r2 * r) * pb(4)
        residual = scaled * (g * facing) - obs
        square = residual * residual
        least = square if least is None else jnp.minimum(least, square)
        kept.append((square, residual * g, facing, dz * r2, dx, dy))
    if state is not None:
        before = state[0]
        least = jnp.minimum(least, before)
    sums = None
    for square, q, facing, drop, dx, dy in kept:
        w = jnp.exp2((least - square) * HALF_LOG2E)
        p = w * q
        pf = p * facing
        terms = (w, p, p * dx, p * dy, pf, pf * drop)
        sums = terms if sums is None else tuple(a + b for a, b in zip(sums, terms))
    if state is not None:
        fade = jnp.exp2((least - before) * HALF_LOG2E)
        sums = tuple(a * fade + b for a, b in zip(state[1:], sums))
    return (least,) + sums


def sweep(ctx_ref, chunks, total, load, store, known):
    rows, w = ctx_ref.shape[1:]
    split = (TR // 8, 8, w)

    def step(i, carry):
        at = pl.ds(pl.multiple_of(i * TR, TR), TR)
        tile = tuple(ctx_ref[f, at, :].reshape(split) for f in range(4))
        row = iota(split, 0) * 8 + iota(split, 1) + i * TR
        py = (row.astype(F32) + (0.5 - rows / 2.0)) / total

        def light(entry):
            (obs_ref, j), (pb_ref, p), (flat_ref, f) = entry
            obs = obs_ref[pl.ds(pl.multiple_of(j * rows + i * TR, TR), TR), :].astype(F32).reshape(split)

            def across(value):
                if known:
                    return flat_ref[f, at, :].reshape(split)
                if value is not None:
                    flat_ref[f, at, :] = value.reshape(TR, w)
                return None

            return obs, lambda field: pb_ref[p, field], across

        state = load(at)
        for chunk in chunks:
            state = accumulate(state, tile, py, [light(entry) for entry in chunk])
        store(at, state)
        return carry

    lax.fori_loop(0, rows // TR, step, 0)


def chunk_of(obs_ref, pb_ref, flat_ref, count, pb_at=0, flat_at=0):
    return [((obs_ref, j), (pb_ref, pb_at + j), (flat_ref, flat_at + j)) for j in range(count)]


def state_load(state_ref, w):
    return lambda at: tuple(state_ref[f, at, :].reshape(TR // 8, 8, w) for f in range(7))


def state_store(state_ref, w):
    def store(at, state):
        for f in range(7):
            state_ref[f, at, :] = state[f].reshape(TR, w)

    return store


def halo_slope(column, side, pack_ref, srow_ref, rows, total):
    obs = pack_ref[side]
    lx, ly, lz, le = decode(pack_ref[2])
    outer, inner = (0, 2) if side == 0 else (5, 3)
    here = 1 if side == 0 else 4
    surface = srow_ref[here : here + 1, :]
    toward = srow_ref[inner : inner + 1, :] - srow_ref[outer : outer + 1, :]
    sx = 0.5 * toward if side == 0 else -0.5 * toward
    lane = iota((8, rows), 1)
    wide = jnp.broadcast_to(surface, (8, rows))
    above = jnp.where(lane == 0, 0.0, pltpu.roll(wide, 1, 1))
    below = jnp.where(lane == rows - 1, 0.0, pltpu.roll(wide, rows - 1, 1))
    sy = (0.5 * (below - above))[0:1]
    albedo = srow_ref[6 + side : 7 + side, :]
    valid = srow_ref[8 + side : 9 + side, :]
    px = (column.astype(F32) + 0.5) / total - 0.5
    py = (iota((1, rows), 1).astype(F32) + (0.5 - rows / 2.0)) / total
    rn = lax.rsqrt(1.0 + sx * sx + sy * sy)
    dx = jnp.broadcast_to(lx - px, obs.shape)
    dy = ly - py
    dz = lz - surface
    dist = dx * dx + dy * dy + dz * dz
    facing = dz - (sx * dx + sy * dy)
    r = lax.rsqrt(dist)
    g = (r * r) * r * le
    residual = (albedo * rn) * (g * facing) - obs
    square = residual * residual
    least = jnp.min(square, axis=0, keepdims=True)
    w = jnp.exp2((least - square) * HALF_LOG2E)
    p = w * residual * g
    total_w = jnp.sum(w, axis=0, keepdims=True)
    px_sum = jnp.sum(p * dx, axis=0, keepdims=True)
    pf_sum = jnp.sum(p * facing, axis=0, keepdims=True)
    return -(valid * albedo * rn / total_w) * (px_sum + (sx * rn * rn) * pf_sum)


def gradients(state_ref, ctx_ref, albedo, valid, ends):
    sx, sy = ctx_ref[1], ctx_ref[2]
    rn = lax.rsqrt(1.0 + sx * sx + sy * sy)
    inverse = valid * rn / state_ref[1]
    factor = inverse * albedo
    pf = state_ref[5]
    rn2pf = rn * rn * pf
    grad_albedo = inverse * pf
    direct = factor * (3.0 * state_ref[6] - state_ref[2])
    grad_x = -factor * (state_ref[3] + sx * rn2pf)
    grad_y = -factor * (state_ref[4] + sy * rn2pf)
    before, after = shifts_cols(grad_x, ends)
    above, below = shifts_rows(grad_y)
    return direct + 0.5 * (before - after) + 0.5 * (above - below), grad_albedo


def partial_sums(depth, albedo):
    n = depth.shape[1]
    d = jnp.sum(depth * depth, axis=0, keepdims=True)
    a = jnp.sum(albedo * albedo, axis=0, keepdims=True)
    d = jnp.broadcast_to(d, (8, n))
    a = jnp.broadcast_to(a, (8, n))
    d = d + pltpu.roll(d, n // 2, 1)
    a = a + pltpu.roll(a, n // 2, 1)
    return jnp.where(iota((8, n), 1) < n // 2, d, a)[0:1]


def inverse_scales(recv_ref, row, count):
    rows = recv_ref[:, row, :]
    n = rows.shape[1]
    lane = iota(rows.shape, 1)
    d = jnp.sum(jnp.where(lane < n // 2, rows, 0.0), keepdims=True)
    a = jnp.sum(jnp.where(lane < n // 2, 0.0, rows), keepdims=True)
    return lax.rsqrt(d / count + EPS), lax.rsqrt(a / count + EPS)


def first_body(nl, tile_ref, sr_ref, strip_ref, obs0, obs1, ctx_ref, srow_ref, state_ref, pb_ref, flat_ref):
    li, _, place, count = position()
    rows, w = ctx_ref.shape[1:]
    srow_ref[...] = sr_ref[...]
    at = strip_ref.shape[0] - 8

    @pl.when(li == 0)
    def _():
        srow_ref[0:2, :] = strip_ref[at : at + 2, :]
        srow_ref[6:7, :] = strip_ref[at + 2 : at + 3, :]
        srow_ref[8:9, :] = strip_ref[at + 3 : at + 4, :]

    @pl.when(li == nl - 1)
    def _():
        srow_ref[4:6, :] = strip_ref[at : at + 2, :]
        srow_ref[7:8, :] = strip_ref[at + 2 : at + 3, :]
        srow_ref[9:10, :] = strip_ref[at + 3 : at + 4, :]

    fill_context(ctx_ref, tile_ref[0], tile_ref[1], srow_ref[1:2, :], srow_ref[4:5, :])
    total = w * count
    n = lights_of(obs0, rows)
    fill_params(pb_ref, 0, obs0, n, rows, w, place, total)
    fill_params(pb_ref, n, obs1, n, rows, w, place, total)
    chunks = [chunk_of(obs0, pb_ref, flat_ref, n), chunk_of(obs1, pb_ref, flat_ref, n, n, n)]
    sweep(ctx_ref, chunks, total, lambda at: None, state_store(state_ref, w), False)


def more_body(ctx_ref, in_ref, obs, state_ref, pb_ref, flat_ref):
    _, _, place, count = position()
    rows, w = ctx_ref.shape[1:]
    total = w * count
    fill_params(pb_ref, 0, obs, pb_ref.shape[0], rows, w, place, total)
    chunks = [chunk_of(obs, pb_ref, flat_ref, lights_of(obs, rows))]
    sweep(ctx_ref, chunks, total, state_load(in_ref, w), state_store(state_ref, w), False)


def halo_slopes(pack_ref, srow_ref, rows, w):
    _, _, place, count = position()
    total = w * count
    low = halo_slope(place * w - 1, 0, pack_ref, srow_ref, rows, total)
    high = halo_slope(place * w + w, 1, pack_ref, srow_ref, rows, total)
    return columns_from(low, high, (rows, w))


def finish(state_ref, ctx_ref, albedo, valid, ends, grad_ref, edge_ref, pay_ref):
    _, _, place, count = position()
    rows, w = ctx_ref.shape[1:]
    depth, grad_albedo = gradients(state_ref, ctx_ref, albedo, valid, ends)
    sums = partial_sums(depth, grad_albedo)
    if edge_ref is None:
        pay_ref[...] = jnp.broadcast_to(sums[None], pay_ref.shape)
        return depth, grad_albedo
    grad_ref[0] = depth
    grad_ref[1] = grad_albedo
    dt = jnp.transpose(depth)
    at = jnp.transpose(grad_albedo)
    edge_ref[0:1, :] = dt[0:1]
    edge_ref[1:2, :] = dt[w - 1 : w]
    pay_ref[:, 0:2, :] = jnp.broadcast_to(dt[0:2][None], (count, 2, rows))
    pay_ref[:, 2:3, :] = jnp.broadcast_to(at[0:1][None], (count, 1, rows))
    pay_ref[:, 3:4, :] = jnp.broadcast_to(sums[None], (count, 1, w))

    @pl.when(place < count - 1)
    def _():
        to = exchange_index(place + 1)
        pay_ref[to, 0:2, :] = dt[w - 2 : w]
        pay_ref[to, 2:3, :] = at[w - 1 : w]

    return depth, grad_albedo


def sides_body(nl, srow_ref, direct_ref, relayed_ref, *rest):
    block_refs, (pack_ref, ends_ref) = rest[:nl], rest[nl:]
    li = lax.axis_index("light")
    w = block_refs[0].shape[1]
    rows = srow_ref.shape[1]
    n = (direct_ref.shape[0] - 8) // 2
    table = jnp.zeros((4, w), F32)
    for k in range(nl):
        halo = block_refs[k][pl.ds(lights_of(block_refs[k], rows) * rows + UNDER, 2 * n), :].astype(F32)
        beyond = (direct_ref if k < 2 else relayed_ref)[(k % 2) * n : (k % 2 + 1) * n, :]
        pack_ref[0, k * n : (k + 1) * n, :] = jnp.where(li == 0, beyond, halo[0:n])
        pack_ref[1, k * n : (k + 1) * n, :] = jnp.where(li == nl - 1, beyond, halo[n:])
        entries = jnp.concatenate([table_rows(block_refs[k], rows)] * 2, axis=0)
        table = table + (pltpu.roll(entries, k * n, 1) if k else entries)[0:4]
    tall = jnp.concatenate([table, jnp.zeros((w - 4, w), F32)], axis=0)
    pack_ref[2] = jnp.transpose(tall)[0 : nl * n]
    ends_ref[...] = halo_slopes(pack_ref, srow_ref, rows, w)


def last_body(ctx_ref, in_ref, obs, pb_ref, tile_ref, ends_ref, grad_ref, edge_ref, pay_ref, flat_ref, state_ref):
    _, _, _, count = position()
    rows, w = ctx_ref.shape[1:]
    n = lights_of(obs, rows)
    edge_ref[...] = jnp.zeros_like(edge_ref)
    chunks = [chunk_of(obs, pb_ref, flat_ref, n, pb_ref.shape[0] - n)]
    sweep(ctx_ref, chunks, w * count, state_load(in_ref, w), state_store(state_ref, w), False)
    finish(state_ref, ctx_ref, tile_ref[1], tile_ref[2], ends_ref[...], grad_ref, edge_ref, pay_ref)


def second_body(nl, recv_ref, grad_ref, edge_ref, tile_ref, srow0_ref, pack_ref, *rest):
    obs_refs, pb_refs, flat_refs = rest[: nl + 1], rest[nl + 1 : 2 * nl], rest[2 * nl : 3 * nl]
    out_ref, pay_ref, ctx_ref, state_ref, srow_ref, ends_ref = rest[3 * nl :]
    _, _, place, count = position()
    rows, w = ctx_ref.shape[1:]
    total = w * count
    inv_depth, inv_albedo = inverse_scales(recv_ref, 3, float(rows * total))
    surface = tile_ref[0] - STEP_DEPTH * jnp.tanh(grad_ref[0] * inv_depth)
    albedo = tile_ref[1] - STEP_ALBEDO * jnp.tanh(grad_ref[1] * inv_albedo)
    out_ref[0] = surface
    out_ref[1] = albedo
    srow_ref[...] = jnp.zeros_like(srow_ref)
    srow_ref[2:4, :] = edge_ref[0:2, :]

    @pl.when(place > 0)
    def _():
        frm = exchange_index(jnp.maximum(place - 1, 0))
        srow_ref[0:2, :] = recv_ref[frm, 0:2, :]
        srow_ref[6:7, :] = recv_ref[frm, 2:3, :]

    @pl.when(place < count - 1)
    def _():
        frm = exchange_index(jnp.minimum(place + 1, count - 1))
        srow_ref[4:6, :] = recv_ref[frm, 0:2, :]
        srow_ref[7:8, :] = recv_ref[frm, 2:3, :]

    changes = srow_ref[0:8, :]
    kind = iota(changes.shape, 0) < 6
    changes = jnp.where(
        kind, STEP_DEPTH * jnp.tanh(changes * inv_depth), STEP_ALBEDO * jnp.tanh(changes * inv_albedo)
    )
    srow_ref[0:8, :] = srow0_ref[0:8, :] - changes
    srow_ref[8:16, :] = srow0_ref[8:16, :]
    fill_context(ctx_ref, surface, albedo, srow_ref[1:2, :], srow_ref[4:5, :])
    n = lights_of(obs_refs[0], rows)
    chunks = [
        chunk_of(obs_refs[0], pb_refs[0], flat_refs[0], n),
        chunk_of(obs_refs[1], pb_refs[0], flat_refs[0], n, n, n),
    ]
    chunks += [chunk_of(obs_refs[k], pb_refs[k - 1], flat_refs[k - 1], n) for k in range(2, nl - 1)]
    late = lights_of(obs_refs[nl], rows)
    chunks.append(
        chunk_of(obs_refs[nl - 1], pb_refs[-1], flat_refs[-2], n - late)
        + chunk_of(obs_refs[nl], pb_refs[-1], flat_refs[-1], late, n - late)
    )
    ends_ref[...] = halo_slopes(pack_ref, srow_ref, rows, w)
    sweep(ctx_ref, chunks, total, lambda at: None, state_store(state_ref, w), True)
    depth, grad_albedo = finish(
        state_ref, ctx_ref, out_ref[1], tile_ref[2], ends_ref[...], None, None, pay_ref
    )
    out_ref[2] = depth
    out_ref[3] = grad_albedo


def hop_body(in_ref, out_ref):
    out_ref[...] = in_ref[...]


def final_body(nl, recv_ref, *rest):
    parts, (depth_ref, albedo_ref) = rest[:nl], rest[nl:]
    li, _, _, count = position()
    rows, w = parts[0].shape[1:]
    inv_depth, inv_albedo = inverse_scales(recv_ref, 0, float(rows * w * count))
    for k in range(nl):
        at = pl.ds(pl.multiple_of((li ^ k) * w, w), w)
        depth_ref[:, at] = parts[k][0] - STEP_DEPTH * jnp.tanh(parts[k][2] * inv_depth)
        albedo_ref[:, at] = parts[k][1] - STEP_ALBEDO * jnp.tanh(parts[k][3] * inv_albedo)


def in_hbm(x):
    return pltpu.with_memory_space_constraint(x, pltpu.HBM)


def shape(*dims, dtype=F32):
    return jax.ShapeDtypeStruct(dims, dtype)


def program(depth_start, albedo_start, observations, light_table, valid_mask):
    nl, ns = lax.axis_size("light"), lax.axis_size("strip")
    nd = nl * ns
    lights, rows, cols = observations.shape
    w = cols // nl

    def swap(x, k):
        return lax.ppermute(x, "light", [(i, i ^ k) for i in range(nl)])

    hbm = pl.BlockSpec(memory_space=pltpu.HBM)
    field = (rows, w)
    *blocks, late, end = call(
        functools.partial(cut_body, nl),
        tuple(shape(block_rows(lights, rows, k, nl), w, dtype=jnp.bfloat16) for k in range(nl))
        + (shape(LATE * rows, w, dtype=jnp.bfloat16), shape(2 * lights, rows)),
        [
            pltpu.VMEM((4, lights), jnp.int32),
            pltpu.VMEM((nl + 2, 2 * lights, rows), F32),
            pltpu.SemaphoreType.DMA((nl + 1,)),
            pltpu.SemaphoreType.DMA((1,)),
        ],
        in_specs=[hbm] * 2,
    )(in_hbm(observations), in_hbm(light_table.T))
    obs2 = swap(blocks[2], 2)
    obs3 = swap(blocks[3], 3)
    obs1 = swap(blocks[1], 1)
    obs0 = blocks[0]
    tile, sr, strip = call(
        functools.partial(join_body, nl),
        (shape(3, *field), shape(16, rows), shape(2 * lights + 8, rows)),
        [
            pltpu.VMEM((2, rows, cols), F32),
            pltpu.VMEM((rows, cols), jnp.int32),
            pltpu.SemaphoreType.DMA((3,)),
        ],
        in_specs=[hbm] * 3 + [pl.BlockSpec(memory_space=pltpu.VMEM)] * 2,
    )(*(in_hbm(x) for x in (depth_start, albedo_start, valid_mask)), obs1, end)
    pairs = []
    for i in range(ns - 1):
        for l in range(nl):
            source, target = (i, i + 1) if l % 2 == 0 else (i + 1, i)
            pairs.append((l * ns + source, l * ns + target))
    direct = lax.ppermute(strip, AXES, pairs)
    relayed = swap(direct, 2)
    late = swap(late, 3)

    def tiles(n):
        return shape(n, 5, 8, w)

    ctx, srow, state, pb0, flat0 = call(
        functools.partial(first_body, nl),
        (shape(4, *field), shape(16, rows), shape(7, *field), tiles(2 * lights), shape(2 * lights, *field)),
    )(tile, sr, direct, obs0, obs1)
    early = lights - LATE
    state, pb2, flat2 = call(more_body, (shape(7, *field), tiles(lights), shape(lights, *field)))(ctx, state, obs2)
    state, pb3, flat3 = call(more_body, (shape(7, *field), tiles(lights), shape(early, *field)))(ctx, state, obs3)
    pack, ends = call(
        functools.partial(sides_body, nl), (shape(3, nl * lights, rows), shape(*field))
    )(srow, direct, relayed, obs0, obs1, obs2, obs3)
    grad, edge, pay, flat4 = call(
        last_body,
        (shape(2, *field), shape(8, rows), shape(nd, 4, rows), shape(LATE, *field)),
        [pltpu.VMEM((7, *field), F32)],
    )(ctx, state, late, pb3, tile, ends)
    recv = lax.all_to_all(pay, AXES, 0, 0, tiled=True)
    own, pay = call(
        functools.partial(second_body, nl),
        (shape(4, *field), shape(nd, 1, rows)),
        [
            pltpu.VMEM((4, *field), F32),
            pltpu.VMEM((7, *field), F32),
            pltpu.VMEM((16, rows), F32),
            pltpu.VMEM(field, F32),
        ],
    )(recv, grad, edge, tile, srow, pack, obs0, obs1, obs2, obs3, late, pb0, pb2, pb3, flat0, flat2, flat3, flat4)
    part2 = swap(own, 2)
    part1 = swap(own, 1)
    recv = lax.all_to_all(pay, AXES, 0, 0, tiled=True)
    part3 = swap(call(hop_body, shape(4, *field))(part2), 1)
    return tuple(
        call(functools.partial(final_body, nl), (shape(rows, cols), shape(rows, cols)))(recv, own, part1, part2, part3)
    )


def solution(mesh):
    in_specs = (
        P(None, "strip"),
        P(None, "strip"),
        P("light", None, "strip"),
        P("light", None),
        P(None, "strip"),
    )
    out_specs = (P(None, "strip"), P(None, "strip"))
    return jax.shard_map(program, mesh=mesh, in_specs=in_specs, out_specs=out_specs, check_vma=False)
```
